128 devices in a mesh: dp: 2 (over core), expert: 64 (over y, x, z).
Axes of the slice: x: 4, y: 4, z: 4, core: 2. Of those that a mesh axis runs over, the one named last changes fastest.
Arguments:
- tokens: bfloat16 [8192, 2048], P(('dp', 'expert')), may hold values from -6 to 6
- tangent: bfloat16 [8192, 2048], P(('dp', 'expert'))
- adjoint: bfloat16 [8192, 2048], P(('dp', 'expert')), may hold values from -6 to 6
- gates: float32 [8192, 8], P(('dp', 'expert')), may hold values from 0.05 to 0.5
- expert_ids: int32 [8192, 8], P(('dp', 'expert')), may hold values from 0 to 127, all different within a row; in each aligned block of 64 rows (0 to 63, 64 to 127, ...) at most 8 rows name the same one
- w_gate: bfloat16 [128, 2048, 768], P('expert'), may hold values from -0.125 to 0.125
- w_up: bfloat16 [128, 2048, 768], P('expert'), may hold values from -0.125 to 0.125
- w_down: bfloat16 [128, 768, 2048], P('expert'), may hold values from -0.21875 to 0.21875
Outputs:
- hvp: float32 [8192, 2048], P(('dp', 'expert'))
- quotient: float32 [], replicated
The draws below stay inside these ranges and needn't reach their ends.
Inputs may be any that keep to these rules, and one draw needn't show every extreme that they name: `expert_ids`: each token names 8 different experts. Among the tokens of one device no expert is named more than 8 times, a bound that some block reaches; every expert is named somewhere.
All inputs are finite; a program needn't handle non-finite values.
Results may differ from the reference program's by a relative error of at most 0.0041.
Values may be sent and summed in bfloat16 or wider, within the bound.
A program may use at most 128 MiB of HBM per device.

```python
import math
import jax
import jax.numpy as jnp
import numpy as np
from jax import lax

D = 2048
FF = 768
TOP = 8
TOK_DEV = 64
EXPERTS = 128
CAP = 8
TOKENS = 8192
N_DP = 2
N_EXPERT = 64


def draw_tangent(key, part):
    first_key = jax.random.fold_in(key, 0)
    rows = jnp.arange(TOKENS, dtype=jnp.float32)
    ramp = 1.0 + 2.0 * rows / (TOKENS - 1.0)
    base = jnp.clip(jax.random.normal(first_key, (TOKENS, D), jnp.float32), -6.0, 6.0)
    return (base * ramp[:, None]).astype(jnp.bfloat16)


def levels(own_key, dims, shards, low, largest):
    loudness, own = 1.0, jax.random.fold_in(own_key, 6)
    for dim, parts in shards:
        steps = jnp.exp(jax.random.uniform(jax.random.fold_in(own, dim), (parts,), jnp.float32, low / len(shards), largest / len(shards)))
        loudness = loudness * jnp.repeat(steps, dims[dim] // parts).reshape([-1 if axis == dim else 1 for axis in range(len(dims))])
    return loudness


def shared_out(rng, own, number, rows, count, top, bound, lean):
    order = jax.random.permutation(rng, count)
    crowded, common = portions_of(count, rows * top, bound, lean, True), portions_of(count, rows * top, bound, lean, False)
    places = jnp.arange(count)

    def named(tallies, turn):
        used = int((tallies > 0).sum())
        fixed = max(1, used // 4)
        moved = fixed + (places - fixed + turn * (used - fixed)) % max(1, count - fixed)
        return jnp.zeros((count,), jnp.int32).at[order[jnp.where(places < fixed, places, moved)]].set(jnp.asarray(tallies, jnp.int32))

    tallies = jnp.where(number % 4 == 0, named(crowded, number // 4), named(common, number - number // 4 - 1))
    mixed = jax.random.permutation(jax.random.fold_in(own, 3), count)
    donor, taker = mixed[0:count // 2 * 2:2], mixed[1:count // 2 * 2:2]
    slack = jnp.minimum(tallies[donor] - 1, bound - tallies[taker]) // 2
    slack = jnp.where((donor == order[0]) | (taker == order[0]) | (tallies[taker] == 0), 0, jnp.maximum(slack, 0))
    moved = jax.random.randint(jax.random.fold_in(own, 4), (count // 2,), 0, 1 << 20) % (slack + 1)
    tallies = tallies.at[donor].add(-moved).at[taker].add(moved)
    members = jnp.searchsorted(jnp.cumsum(tallies), jnp.arange(rows * top), side="right").astype(jnp.int32)
    listing = members.reshape(top, rows).T
    listing = listing[jax.random.permutation(jax.random.fold_in(own, 1), rows)]
    turn = jax.random.randint(jax.random.fold_in(own, 2), (rows, 1), 0, top)
    return jnp.take_along_axis(listing, (jnp.arange(top)[None, :] + turn) % top, axis=1)


def portions_of(count, total, reach, skew, full):
    weights = [(1 << 20) // math.isqrt(grade ** skew) + 1 for grade in range(1, count + 1)]
    largest = reach if full else min(reach, max(-(-total // count), total * weights[0] // sum(weights)))
    least = 1 if total - largest >= count - 1 else 0
    given, spare = [largest] + [least] * (count - 1), total - largest - least * (count - 1)
    while spare > 0:
        candidates = [i for i in range(1, count) if given[i] < largest] or [i for i in range(1, count) if given[i] < reach]
        pool, left = sum([weights[i] for i in candidates]), spare
        for i in candidates:
            addition = min(reach - given[i], max(1, left * weights[i] // pool), spare)
            given[i] = given[i] + addition
            spare = spare - addition
    return np.array(given)


def normal_values(key, extent, spread, bound, pieces=(), kind=jnp.bfloat16):
    array = spread * jax.random.normal(key, extent, jnp.float32)
    if pieces:
        array = array * levels(key, extent, pieces, -0.22, 0.18)
    return jnp.clip(array, -bound, bound).astype(kind)


def setup_inputs(seed: int = 0) -> dict:
    streams_of = jax.random.split(jax.random.key(seed), 9)
    tokens = normal_values(streams_of[0], (TOKENS, D), 1.0, 6.0, ((0, 128),))
    tangent = draw_tangent(jax.random.fold_in(streams_of[8], 71), 0)
    adjoint = normal_values(streams_of[2], (TOKENS, D), 1.0, 6.0, ((0, 128),))
    gates = jnp.clip(jnp.exp(math.log(0.5) - 2.3025851 * jax.random.uniform(streams_of[3], (TOKENS, TOP), jnp.float32) ** levels(streams_of[3], (TOKENS, TOP), ((0, 128),), -0.2, 0.2)), 0.05, 0.5)
    expert_ids_keys = jax.random.split(jax.random.fold_in(streams_of[4], 1), TOKENS // TOK_DEV)
    expert_ids_turns = jax.random.permutation(jax.random.fold_in(streams_of[4], 3), TOKENS // TOK_DEV)
    expert_ids = jax.vmap(lambda own, number: shared_out(jax.random.fold_in(streams_of[4], 2), own, number, TOK_DEV, EXPERTS, TOP, CAP, 2))(expert_ids_keys, expert_ids_turns).reshape((TOKENS, TOP))
    w_gate = normal_values(streams_of[5], (EXPERTS, D, FF), D ** -0.5, 0.125, ((0, 64),))
    w_up = normal_values(streams_of[6], (EXPERTS, D, FF), D ** -0.5, 0.125, ((0, 64),))
    w_down = normal_values(streams_of[7], (EXPERTS, FF, D), FF ** -0.5, 0.21875, ((0, 64),))
    return dict(tokens=tokens, tangent=tangent, adjoint=adjoint, gates=gates, expert_ids=expert_ids, w_gate=w_gate, w_up=w_up, w_down=w_down)


def expert_terms(primal_rows, tangent_rows, adjoint_rows, gate_mat, up_mat, down_mat):
    pre_gate = jnp.einsum("erd,edf->erf", primal_rows, gate_mat, preferred_element_type=jnp.float32)
    pre_up = jnp.einsum("erd,edf->erf", primal_rows, up_mat, preferred_element_type=jnp.float32)
    dir_gate = jnp.einsum("erd,edf->erf", tangent_rows, gate_mat, preferred_element_type=jnp.float32)
    dir_up = jnp.einsum("erd,edf->erf", tangent_rows, up_mat, preferred_element_type=jnp.float32)
    back_units = jnp.einsum("erd,efd->erf", adjoint_rows, down_mat, preferred_element_type=jnp.float32)
    sigmoid_g = jax.nn.sigmoid(pre_gate)
    first_der = sigmoid_g * (1.0 + pre_gate * (1.0 - sigmoid_g))
    second_der = sigmoid_g * (1.0 - sigmoid_g) * (2.0 + pre_gate * (1.0 - 2.0 * sigmoid_g))
    part_gate = (back_units * (dir_up * first_der + pre_up * second_der * dir_gate)).astype(jnp.bfloat16)
    part_up = (back_units * first_der * dir_gate).astype(jnp.bfloat16)
    result = jnp.einsum("erf,edf->erd", part_gate, gate_mat, preferred_element_type=jnp.float32)
    return result + jnp.einsum("erf,edf->erd", part_up, up_mat, preferred_element_type=jnp.float32)


def reference(tokens, tangent, adjoint, gates, expert_ids, w_gate, w_up, w_down):
    devices_all = N_DP * N_EXPERT
    tok_total, top_count = expert_ids.shape
    tok_rows = tok_total // devices_all
    width = tokens.shape[1]
    flat_ids = expert_ids.reshape(devices_all, tok_rows * top_count)
    onehot = (flat_ids[:, :, None] == jnp.arange(EXPERTS, dtype=jnp.int32)[None, None, :]).astype(jnp.int32)
    before = jnp.cumsum(onehot, axis=1) - onehot
    slot_index = jnp.sum(before * onehot, axis=2).astype(jnp.int32)
    device_index = jnp.arange(devices_all, dtype=jnp.int32)[:, None]
    per_expert = devices_all * CAP
    position = (flat_ids * per_expert + device_index * CAP + slot_index).reshape(-1).astype(jnp.int32)
    token_of = (jnp.arange(tok_total * top_count, dtype=jnp.int32) // top_count).astype(jnp.int32)
    owner = jnp.full((EXPERTS * per_expert,), tok_total, jnp.int32).at[position].set(token_of)
    zero_row = jnp.zeros((1, width), jnp.bfloat16)
    primal_pad = jnp.concatenate([tokens, zero_row], axis=0)
    tangent_pad = jnp.concatenate([tangent, zero_row], axis=0)
    adjoint_pad = jnp.concatenate([adjoint, zero_row], axis=0)

    def one_expert(packed):
        expert_index, gate_mat, up_mat, down_mat = packed
        picked = lax.dynamic_slice_in_dim(owner, (expert_index * per_expert).astype(jnp.int32), per_expert)
        terms = expert_terms(primal_pad[picked][None], tangent_pad[picked][None], adjoint_pad[picked][None],
                             gate_mat[None], up_mat[None], down_mat[None])[0]
        return terms.astype(jnp.bfloat16)

    replies = lax.map(one_expert, (jnp.arange(EXPERTS, dtype=jnp.int32), w_gate, w_up, w_down))
    replies = replies.reshape(EXPERTS * per_expert, width)
    picked_rows = replies[position].reshape(tok_total, top_count, width).astype(jnp.float32)
    hvp = jnp.sum(gates[:, :, None] * picked_rows, axis=1)
    tangent_wide = tangent.astype(jnp.float32)
    quotient = jnp.sum(hvp * hvp) / jnp.sum(tangent_wide * tangent_wide)
    return hvp, quotient
```

```python
import functools

import jax
import jax.numpy as jnp
from jax import lax
from jax.experimental import pallas as pl
from jax.experimental.pallas import tpu as pltpu
from jax.sharding import PartitionSpec as P

MESH = pl.DeviceIdType.MESH
STRIDE = (16, 4, 1)
ORDERS = ((0, 1, 2), (1, 2, 0), (2, 0, 1))
PARTS = ((0, 768), (768, 640), (1408, 640))
TOK, D, FF, R = 64, 2048, 768, 4
BF, F32 = jnp.bfloat16, jnp.float32


class Place:
    def __init__(self):
        self.me = lax.axis_index("expert")
        self.dp = lax.axis_index("dp")
        self.at = (self.me // 16, (self.me // 4) % 4, self.me % 4)

    def shifted(self, dim, by):
        c = self.at[dim]
        return self.me + (lax.rem(c + by, 4) - c) * STRIDE[dim]


def barrier(place, core):
    sem = pltpu.get_barrier_semaphore()
    for dim in range(3):
        for by in (1, 2, 3):
            pl.semaphore_signal(
                sem, inc=1, device_id=(place.dp, place.shifted(dim, by)), device_id_type=MESH
            )
    if core:
        pl.semaphore_signal(sem, inc=1, device_id=(1 - place.dp, place.me), device_id_type=MESH)
    pl.semaphore_wait(sem, 10 if core else 9)


class Wire:
    def __init__(self, place, send, recv):
        self.place, self.send, self.recv, self.used, self.open = place, send, recv, 0, []

    def take(self):
        self.used += 1
        return self.used - 1

    def _copy(self, src, dst, k, target):
        return pltpu.make_async_remote_copy(
            src_ref=src, dst_ref=dst, send_sem=self.send.at[k], recv_sem=self.recv.at[k],
            device_id=target, device_id_type=MESH,
        )

    def go(self, k, src, dst, dim, by):
        c = self._copy(src, dst, k, (self.place.dp, self.place.shifted(dim, by)))
        c.start()
        self.open.append(c)

    def cross(self, k, src, dst):
        c = self._copy(src, dst, k, (1 - self.place.dp, self.place.me))
        c.start()
        self.open.append(c)

    def got(self, k, view):
        self._copy(view, view, k, (self.place.dp, self.place.shifted(0, 1))).wait_recv()

    def drain(self):
        for c in self.open:
            c.wait_send()
        self.open = []


def mod4(v):
    return lax.rem(v, 4)


def column_terms(meta, a, s2, place):
    dim = ORDERS[a][2]
    blocks = [meta[a, s2, s] for s in range(4)]
    low = lax.broadcasted_iota(jnp.int32, (8, 128), 1) < 64
    turn = [pltpu.roll(b, 64, 1) for b in blocks]
    ids = jnp.concatenate([jnp.where(low, blocks[0], turn[1]), jnp.where(low, blocks[2], turn[3])], axis=1)
    gates = jnp.concatenate([jnp.where(low, turn[0], blocks[1]), jnp.where(low, turn[2], blocks[3])], axis=1)
    row = lax.broadcasted_iota(jnp.int32, (8, 256), 0)
    named = jnp.zeros((8, 256), F32)
    weight = jnp.zeros((8, 256), F32)
    for r in range(8):
        e = 2 * (place.me + (r // 2 - place.at[dim]) * STRIDE[dim]) + r % 2
        hit = ids == e.astype(F32)
        n = jnp.sum(jnp.where(hit, 1.0, 0.0), axis=0, keepdims=True)
        g = jnp.sum(jnp.where(hit, gates, 0.0), axis=0, keepdims=True)
        named = jnp.where(row == r, n, named)
        weight = jnp.where(row == r, g, weight)
    i = lax.broadcasted_iota(jnp.int32, (256, 256), 0)
    l = lax.broadcasted_iota(jnp.int32, (256, 256), 1)
    upper = jnp.where((i // 64 == l // 64) & (i < l), 1.0, 0.0).astype(BF)
    before = jnp.dot(named.astype(BF), upper, preferred_element_type=F32)
    base = (lax.broadcasted_iota(jnp.int32, (8, 256), 1) // 64 * 8).astype(F32)
    return jnp.where(named > 0.5, base + before, -1.0), weight


def dispatch_kernel(tok, tan, adj, meta_in, r0, r1, r2, meta_out,
                    held, packed, relay, meta, pick, send, recv, local):
    place = Place()
    wire = Wire(place, send, recv)
    outs = (r0, r1, r2)
    barrier(place, False)

    own = []
    for a, src in enumerate((tok, tan, adj)):
        d1, d2, d3 = ORDERS[a]
        c = pltpu.make_async_copy(src, held.at[a, place.at[d2], place.at[d1]], local.at[a])
        c.start()
        own.append(c)
        c = pltpu.make_async_copy(meta_in, meta.at[a, place.at[d2], place.at[d1]], local.at[3 + a])
        c.start()
        own.append(c)
    for c in own:
        c.wait()

    def half(a, s2, s1, h):
        return held.at[a, s2, s1, pl.ds(32 * h, 32)]

    def spread(a, dim, at2, at1, keys):
        for h in (0, 1):
            wire.go(keys[0][h], half(a, at2, at1, h), half(a, at2, at1, h), dim, 1)
            wire.go(keys[1][1 - h], half(a, at2, at1, 1 - h), half(a, at2, at1, 1 - h), dim, 3)

    def keys_of():
        return ((wire.take(), wire.take()), (wire.take(), wire.take()), (wire.take(), wire.take()))

    first = [keys_of() for _ in range(3)]
    second = [[keys_of() for _ in range(4)] for _ in range(3)]
    rel1 = (0, 3, 1, 2)
    at = [(place.at[ORDERS[a][1]], place.at[ORDERS[a][0]]) for a in range(3)]

    mk1 = [[wire.take() for _ in range(3)] for _ in range(3)]
    mk2 = [[wire.take() for _ in range(3)] for _ in range(3)]
    for a in range(3):
        n2, n1 = at[a]
        for i, by in enumerate((1, 2, 3)):
            wire.go(mk1[a][i], meta.at[a, n2, n1], meta.at[a, n2, n1], ORDERS[a][0], by)
    for a in range(3):
        n2, n1 = at[a]
        spread(a, ORDERS[a][0], n2, n1, first[a])
    for a in range(3):
        n2, n1 = at[a]
        spread(a, ORDERS[a][1], n2, n1, second[a][0])
    for a in range(3):
        n2, n1 = at[a]
        for i, by in enumerate((1, 2, 3)):
            wire.got(mk1[a][i], meta.at[a, n2, mod4(n1 + 4 - by)])
        for i, by in enumerate((1, 2, 3)):
            wire.go(mk2[a][i], meta.at[a, n2], meta.at[a, n2], ORDERS[a][1], by)

    def pass_on(a, dim, keys, minus, plus):
        wire.got(keys[0][0], minus(0))
        wire.go(keys[2][0], minus(0), minus(0), dim, 1)
        wire.got(keys[1][1], plus(1))
        wire.go(keys[2][1], plus(1), plus(1), dim, 3)

    def rest(keys, minus, plus):
        wire.got(keys[0][1], minus(1))
        wire.got(keys[1][0], plus(0))

    def views1(a):
        n2, n1 = at[a]
        return (lambda h: half(a, n2, mod4(n1 + 3), h)), (lambda h: half(a, n2, mod4(n1 + 1), h))

    def views2(a, b):
        n2, n1 = at[a]
        s1 = mod4(n1 + rel1[b])
        return (lambda h: half(a, mod4(n2 + 3), s1, h)), (lambda h: half(a, mod4(n2 + 1), s1, h))

    for a in range(3):
        pass_on(a, ORDERS[a][0], first[a], *views1(a))
    for a in range(3):
        rest(first[a], *views1(a))
        n2, n1 = at[a]
        for b in (1, 2):
            spread(a, ORDERS[a][1], n2, mod4(n1 + rel1[b]), second[a][b])
    for a in range(3):
        pass_on(a, ORDERS[a][1], second[a][0], *views2(a, 0))
    for a in range(3):
        n2, n1 = at[a]
        wire.got(first[a][2][0], half(a, n2, mod4(n1 + 2), 0))
        wire.got(first[a][2][1], half(a, n2, mod4(n1 + 2), 1))
        spread(a, ORDERS[a][1], n2, mod4(n1 + 2), second[a][3])

    moved = []
    third = [[[wire.take() for _ in range(6)] for _ in range(4)] for _ in range(3)]

    def pack(a, r):
        n2, n1 = at[a]
        dim = ORDERS[a][2]
        n3 = place.at[dim]
        s2 = mod4(n2 + r)
        index, _ = column_terms(meta, a, s2, place)
        slots = lax.broadcasted_iota(jnp.int32, (32, 256), 0).astype(F32)
        for e in range(8):
            pick[pl.ds(32 * e, 32), :] = jnp.where(index[e : e + 1, :] == slots, 1.0, 0.0).astype(BF)
        chosen = pick[...]

        @pl.loop(0, 4)
        def _(n):
            cols = pl.ds(pl.multiple_of(n * 512, 512), 512)
            rows = held[a, s2, :, :, cols].reshape(256, 512)
            got = jnp.dot(chosen, rows, preferred_element_type=F32).astype(BF)
            packed[a, r, :, :, :, cols] = got.reshape(4, 2, 32, 512)

        k = third[a][r]
        far, right, left = mod4(n3 + 2), mod4(n3 + 1), mod4(n3 + 3)
        wire.go(k[0], packed.at[a, r, far, 0], relay.at[a, r, 0], dim, 1)
        wire.go(k[1], packed.at[a, r, far, 1], relay.at[a, r, 1], dim, 3)
        wire.go(k[2], packed.at[a, r, right], outs[a].at[:, n3, s2], dim, 1)
        wire.go(k[3], packed.at[a, r, left], outs[a].at[:, n3, s2], dim, 3)
        c = pltpu.make_async_copy(packed.at[a, r, n3], outs[a].at[:, n3, s2], local.at[6 + a * 4 + r])
        c.start()
        moved.append(c)

    def relays(a, r):
        n2, n1 = at[a]
        dim = ORDERS[a][2]
        n3 = place.at[dim]
        s2 = mod4(n2 + r)
        k = third[a][r]
        wire.got(k[0], relay.at[a, r, 0])
        wire.go(k[4], relay.at[a, r, 0], outs[a].at[0, mod4(n3 + 3), s2], dim, 1)
        wire.got(k[1], relay.at[a, r, 1])
        wire.go(k[5], relay.at[a, r, 1], outs[a].at[1, mod4(n3 + 1), s2], dim, 3)

    for a in range(3):
        n2, n1 = at[a]
        for i, by in enumerate((1, 2, 3)):
            wire.got(mk2[a][i], meta.at[a, mod4(n2 + 4 - by)])
    for b in (1, 2):
        for a in range(3):
            pass_on(a, ORDERS[a][1], second[a][b], *views2(a, b))
    for a in range(3):
        pack(a, 0)
    for a in range(3):
        pass_on(a, ORDERS[a][1], second[a][3], *views2(a, 3))
    for a in range(3):
        for b in range(4):
            rest(second[a][b], *views2(a, b))
    for r in (1, 3):
        for a in range(3):
            pack(a, r)
        for a in range(3):
            relays(a, 0 if r == 1 else 1)
    for a in range(3):
        n2, n1 = at[a]
        for b in range(4):
            s1 = mod4(n1 + rel1[b])
            wire.got(second[a][b][2][0], half(a, mod4(n2 + 2), s1, 0))
            wire.got(second[a][b][2][1], half(a, mod4(n2 + 2), s1, 1))
        pack(a, 2)
    for r in (3, 2):
        for a in range(3):
            relays(a, r)
    c = pltpu.make_async_copy(meta, meta_out, local.at[18])
    c.start()
    moved.append(c)
    for r in (0, 1, 3, 2):
        for a in range(3):
            n2, n1 = at[a]
            n3 = place.at[ORDERS[a][2]]
            s2 = mod4(n2 + r)
            k = third[a][r]
            wire.got(k[2], outs[a].at[:, mod4(n3 + 3), s2])
            wire.got(k[3], outs[a].at[:, mod4(n3 + 1), s2])
            wire.got(k[4], outs[a].at[0, mod4(n3 + 2), s2])
            wire.got(k[5], outs[a].at[1, mod4(n3 + 2), s2])
    for c in moved:
        c.wait()
    wire.drain()


N_DISPATCH = 3 * 6 + 12 * 6 + 18 + 72


def dispatch(tok, tan, adj, meta):
    vmem = pl.BlockSpec(memory_space=pltpu.VMEM)
    hbm = pl.BlockSpec(memory_space=pl.ANY)
    rows = jax.ShapeDtypeStruct((2, 4, 4, 32, D), BF)
    return pl.pallas_call(
        dispatch_kernel,
        out_shape=(rows, rows, rows, jax.ShapeDtypeStruct((3, 4, 4, 8, 128), F32)),
        in_specs=[vmem] * 4,
        out_specs=(hbm, hbm, hbm, hbm),
        scratch_shapes=[
            pltpu.VMEM((3, 4, 4, TOK, D), BF),
            pltpu.VMEM((3, 4, 4, 2, 32, D), BF),
            pltpu.VMEM((3, 4, 2, 32, D), BF),
            pltpu.VMEM((3, 4, 4, 8, 128), F32),
            pltpu.VMEM((256, 256), BF),
            pltpu.SemaphoreType.DMA((N_DISPATCH,)),
            pltpu.SemaphoreType.DMA((N_DISPATCH,)),
            pltpu.SemaphoreType.DMA((19,)),
        ],
        compiler_params=pltpu.CompilerParams(
            collective_id=1, has_side_effects=True, vmem_limit_bytes=56 * 2**20
        ),
        name="dispatch",
    )(tok, tan, adj, meta)


NT = (((1,), (1,)), ((), ()))


def expert_kernel(r0, r1, r2, wg, wu, wd, s0, s1, s2,
                  pre, lin, dirg, diru, back, pg, pu):
    x, v, c = (r[0].reshape(512, D) for r in (r0, r1, r2))

    @pl.loop(0, 3)
    def _(n):
        cols = pl.ds(pl.multiple_of(n * 256, 256), 256)

        def put(ref, value):
            ref[:, :, :, :, cols] = value.reshape(4, 4, 4, 8, 256)

        g, u = wg[0, :, cols], wu[0, :, cols]
        put(pre, jnp.dot(x, g, preferred_element_type=F32))
        put(dirg, jnp.dot(v, g, preferred_element_type=F32))
        put(lin, jnp.dot(x, u, preferred_element_type=F32))
        put(diru, jnp.dot(v, u, preferred_element_type=F32))
        put(back, lax.dot_general(c, wd[0, cols, :], NT, preferred_element_type=F32))

    @pl.loop(0, 16)
    def _(i):
        z, xx = i // 4, i % 4
        for y in range(4):
            p, l = pre[z, xx, y], lin[z, xx, y]
            pd, ld = dirg[y, z, xx], diru[y, z, xx]
            b = back[xx, y, z]
            s = jax.nn.sigmoid(p)
            one = s * (1.0 + p * (1.0 - s))
            two = s * (1.0 - s) * (2.0 + p * (1.0 - 2.0 * s))
            pre[z, xx, y] = b * (ld * one + l * two * pd)
            lin[z, xx, y] = b * one * pd

    for a, out in enumerate((s0, s1, s2)):
        f0, f = PARTS[a]

        @pl.loop(0, 16)
        def _(i):
            p, q = i // 4, i % 4
            at = pl.ds(pl.multiple_of(i * 32, 32), 32)
            for src, dst in ((pre, pg), (lin, pu)):
                if a == 0:
                    rows = src[p, q]
                elif a == 1:
                    rows = src[q, :, p]
                else:
                    rows = src[:, p, q]
                dst[at, :] = rows.reshape(32, FF).astype(BF)

        left, up = pg[...], pu[...]
        done = 0
        while done < f:
            n = min(256, f - done)
            got = lax.dot_general(left, wg[0, f0 + done : f0 + done + n, :], NT, preferred_element_type=F32)
            got += lax.dot_general(up, wu[0, f0 + done : f0 + done + n, :], NT, preferred_element_type=F32)
            out[:, :, 0, :, done : done + n] = got.astype(BF).reshape(4, 4, 32, n)
            done += n


def experts(r0, r1, r2, wg, wu, wd):
    rows = pl.BlockSpec((1, 4, 4, 32, D), lambda j: (j, 0, 0, 0, 0))
    wide = pl.BlockSpec((1, D, FF), lambda j: (j, 0, 0))
    tall = pl.BlockSpec((1, FF, D), lambda j: (j, 0, 0))
    return pl.pallas_call(
        expert_kernel,
        grid=(2,),
        out_shape=tuple(jax.ShapeDtypeStruct((4, 4, 2, 32, f), BF) for _, f in PARTS),
        in_specs=[rows, rows, rows, wide, wide, tall],
        out_specs=tuple(pl.BlockSpec((4, 4, 1, 32, f), lambda j: (0, 0, j, 0, 0)) for _, f in PARTS),
        scratch_shapes=[pltpu.VMEM((4, 4, 4, 8, FF), F32)] * 5 + [pltpu.VMEM((512, FF), BF)] * 2,
        compiler_params=pltpu.CompilerParams(vmem_limit_bytes=60 * 2**20),
        name="experts",
    )(r0, r1, r2, wg, wu, wd)


def collect_kernel(s0, s1, s2, meta, tan, hvp, ratio, *scratch):
    place = Place()
    n_part = 9
    parts = [scratch[i * n_part : (i + 1) * n_part] for i in range(3)]
    grown, spin, sums, send, recv, local = scratch[3 * n_part :]
    wire = Wire(place, send, recv)
    srcs = (s0, s1, s2)
    barrier(place, True)
    keys = [[wire.take() for _ in range(18)] for _ in range(3)]
    tot = [[wire.take() for _ in range(3)] for _ in range(3)]
    cross = wire.take()
    at = [tuple(place.at[d] for d in ORDERS[a]) for a in range(3)]

    moved = []
    for a in range(3):
        back, relay = parts[a][0], parts[a][1]
        n3, dim = at[a][2], ORDERS[a][2]
        k = keys[a]
        far = mod4(n3 + 2)
        wire.go(k[0], srcs[a].at[far, pl.ds(0, 2)], relay.at[0], dim, 1)
        wire.go(k[1], srcs[a].at[far, pl.ds(2, 2)], relay.at[1], dim, 3)
        wire.go(k[2], srcs[a].at[mod4(n3 + 1)], back.at[:, n3], dim, 1)
        wire.go(k[3], srcs[a].at[mod4(n3 + 3)], back.at[:, n3], dim, 3)
        c = pltpu.make_async_copy(srcs[a].at[n3], back.at[:, n3], local.at[a])
        c.start()
        moved.append(c)

    t = tan[...].astype(F32)
    sums[3, 1] = jnp.sum((t * t).reshape(8, 8, 16, 128), axis=(0, 2))

    for a in range(3):
        back, relay = parts[a][0], parts[a][1]
        n3, dim = at[a][2], ORDERS[a][2]
        k = keys[a]
        wire.got(k[0], relay.at[0])
        wire.go(k[4], relay.at[0], back.at[pl.ds(0, 2), mod4(n3 + 3)], dim, 1)
        wire.got(k[1], relay.at[1])
        wire.go(k[5], relay.at[1], back.at[pl.ds(2, 2), mod4(n3 + 1)], dim, 3)

    slots = lax.broadcasted_iota(jnp.int32, (32, 256), 0).astype(F32)
    for a in range(3):
        for r in range(4):
            s2 = mod4(at[a][1] + r)
            index, weight = column_terms(meta, a, s2, place)
            for e in range(8):
                spin[pl.ds(32 * e, 32), :] = jnp.where(index[e : e + 1, :] == slots, weight[e : e + 1, :], 0.0)
            w = spin[...].T
            high = w.astype(BF)
            grown[a, r, 0] = high
            grown[a, r, 1] = (w - high.astype(F32)).astype(BF)

    for c in moved:
        c.wait()

    def total(a, r):
        back = parts[a][0]
        s2 = mod4(at[a][1] + r)
        rows = back[s2].reshape(256, PARTS[a][1])
        got = jnp.dot(grown[a, r, 0], rows, preferred_element_type=F32)
        return got + jnp.dot(grown[a, r, 1], rows, preferred_element_type=F32)

    for a in range(3):
        back, relay, own, out2, mid2, to2, in2, *_ = parts[a]
        n1, n2, n3 = at[a]
        k, f = keys[a], PARTS[a][1]
        wire.got(k[2], back.at[:, mod4(n3 + 3)])
        wire.got(k[3], back.at[:, mod4(n3 + 1)])
        wire.got(k[4], back.at[pl.ds(0, 2), mod4(n3 + 2)])
        wire.got(k[5], back.at[pl.ds(2, 2), mod4(n3 + 2)])
        out2[...] = total(a, 2).astype(BF).reshape(4, 64, f)
        dim = ORDERS[a][1]
        wire.go(k[6], out2.at[pl.ds(0, 2)], mid2.at[0], dim, 1)
        wire.go(k[7], out2.at[pl.ds(2, 2)], mid2.at[1], dim, 3)
    for a in range(3):
        back, relay, own, out2, mid2, to2, in2, *_ = parts[a]
        own[...] = total(a, 0).reshape(4, 64, PARTS[a][1])
    for a in range(3):
        back, relay, own, out2, mid2, to2, in2, *_ = parts[a]
        k, f, dim = keys[a], PARTS[a][1], ORDERS[a][1]
        for side, r in ((0, 1), (1, 3)):
            got = total(a, r).reshape(4, 64, f)
            wire.got(k[6 + side], mid2.at[side])
            came = mid2[side].astype(F32)
            lo, hi = got[0:2], got[2:4]
            if side == 0:
                lo = lo + came
            else:
                hi = hi + came
            to2[side, 0:2] = lo.astype(BF)
            to2[side, 2:4] = hi.astype(BF)
            wire.go(k[8 + side], to2.at[side], in2.at[side], dim, r)

    for a in range(3):
        back, relay, own, out2, mid2, to2, in2, out1, mid1 = parts[a]
        n1, n2, n3 = at[a]
        k, f, dim = keys[a], PARTS[a][1], ORDERS[a][0]
        wire.got(k[8], in2.at[0])
        wire.got(k[9], in2.at[1])
        for s in range(4):
            own[s] = own[s] + (in2[0, s].astype(F32) + in2[1, s].astype(F32))
        out1[0] = own[mod4(n1 + 2)].astype(BF)
        wire.go(k[10], out1.at[0, pl.ds(0, 32)], mid1.at[0, pl.ds(0, 32)], dim, 1)
        wire.go(k[11], out1.at[0, pl.ds(32, 32)], mid1.at[0, pl.ds(32, 32)], dim, 3)
    for a in range(3):
        back, relay, own, out2, mid2, to2, in2, out1, mid1 = parts[a]
        n1, n2, n3 = at[a]
        k, f, dim = keys[a], PARTS[a][1], ORDERS[a][0]
        for side, r in ((0, 1), (1, 3)):
            rows = pl.ds(32 * side, 32)
            rest = pl.ds(32 - 32 * side, 32)
            wire.got(k[10 + side], mid1.at[0, rows])
            s = mod4(n1 + r)
            out1[1 + side, rows] = (own[s, rows] + mid1[0, rows].astype(F32)).astype(BF)
            out1[1 + side, rest] = own[s, rest].astype(BF)
            wire.go(k[12 + side], out1.at[1 + side], mid1.at[1 + side], dim, r)
    square = jnp.zeros((8, 128), F32)
    for a in range(3):
        back, relay, own, out2, mid2, to2, in2, out1, mid1 = parts[a]
        n1, n2, n3 = at[a]
        k = keys[a]
        f0, f = PARTS[a]
        wire.got(k[12], mid1.at[1])
        wire.got(k[13], mid1.at[2])
        got = own[n1] + (mid1[1].astype(F32) + mid1[2].astype(F32))
        hvp[:, f0 : f0 + f] = got
        square = square + jnp.sum((got * got).reshape(8, 8, f // 128, 128), axis=(0, 2))

    value = (square, sums[3, 1])
    for dim in range(3):
        c = place.at[dim]
        spots = 4 * dim
        grid = sums.at[pl.ds(4 + spots, 4)]
        grid[c, 0] = value[0]
        grid[c, 1] = value[1]
        for i, by in enumerate((1, 2, 3)):
            wire.go(tot[dim][i], grid.at[c], grid.at[c], dim, by)
        for i, by in enumerate((1, 2, 3)):
            wire.got(tot[dim][i], grid.at[mod4(c + 4 - by)])
        value = tuple((grid[0, q] + grid[1, q]) + (grid[2, q] + grid[3, q]) for q in range(2))
    sums[place.dp, 0] = value[0]
    sums[place.dp, 1] = value[1]
    wire.cross(cross, sums.at[place.dp], sums.at[place.dp])
    wire.got(cross, sums.at[1 - place.dp])
    top = jnp.sum(sums[0, 0] + sums[1, 0])
    low = jnp.sum(sums[0, 1] + sums[1, 1])
    ratio[...] = jnp.full((8, 128), top, F32) / jnp.full((8, 128), low, F32)
    wire.drain()


N_COLLECT = 3 * 18 + 9 + 1


def collect(s0, s1, s2, meta, tan):
    vmem = pl.BlockSpec(memory_space=pltpu.VMEM)
    scratch = []
    for _, f in PARTS:
        scratch += [
            pltpu.VMEM((4, 4, 64, f), BF),
            pltpu.VMEM((2, 2, 64, f), BF),
            pltpu.VMEM((4, 64, f), F32),
            pltpu.VMEM((4, 64, f), BF),
            pltpu.VMEM((2, 2, 64, f), BF),
            pltpu.VMEM((2, 4, 64, f), BF),
            pltpu.VMEM((2, 4, 64, f), BF),
            pltpu.VMEM((3, 64, f), BF),
            pltpu.VMEM((3, 64, f), BF),
        ]
    scratch += [
        pltpu.VMEM((3, 4, 2, 256, 256), BF),
        pltpu.VMEM((256, 256), F32),
        pltpu.VMEM((16, 2, 8, 128), F32),
        pltpu.SemaphoreType.DMA((N_COLLECT,)),
        pltpu.SemaphoreType.DMA((N_COLLECT,)),
        pltpu.SemaphoreType.DMA((3,)),
    ]
    return pl.pallas_call(
        collect_kernel,
        out_shape=(jax.ShapeDtypeStruct((TOK, D), F32), jax.ShapeDtypeStruct((8, 128), F32)),
        in_specs=[vmem] * 5,
        out_specs=(vmem, vmem),
        scratch_shapes=scratch,
        compiler_params=pltpu.CompilerParams(
            collective_id=2, has_side_effects=True, vmem_limit_bytes=48 * 2**20
        ),
        name="collect",
    )(s0, s1, s2, meta, tan)


def local(tokens, tangent, adjoint, gates, expert_ids, w_gate, w_up, w_down):
    meta = jnp.concatenate([expert_ids.astype(F32), gates], axis=0).T
    r0, r1, r2, columns = dispatch(tokens, tangent, adjoint, meta)
    s = experts(r0, r1, r2, w_gate, w_up, w_down)
    s = [p.reshape(4, 4, 64, p.shape[-1]) for p in s]
    hvp, ratio = collect(*s, columns, tangent)
    return hvp, ratio[0, 0]


def solution(mesh):
    rows = P(("dp", "expert"), None)
    weights = P("expert", None, None)
    return jax.shard_map(
        local,
        mesh=mesh,
        in_specs=(rows,) * 5 + (weights,) * 3,
        out_specs=(rows, P()),
        check_vma=False,
    )
```

```python
import functools

import jax
import jax.numpy as jnp
from jax import lax
from jax.experimental import pallas as pl
from jax.experimental.pallas import tpu as pltpu
from jax.sharding import PartitionSpec as P

MESH = pl.DeviceIdType.MESH
STRIDE = (16, 4, 1)
ORDERS = ((0, 1, 2), (1, 2, 0), (2, 0, 1))
PARTS = (
    ((0, 0, 256), (1, 768, 256), (2, 1408, 256)),
    ((0, 256, 256), (1, 1024, 256), (2, 1664, 256)),
    ((0, 512, 256), (1, 1280, 128), (2, 1920, 128)),
)
TOK, D, FF, R = 64, 2048, 768, 4
BF, F32 = jnp.bfloat16, jnp.float32


class Place:
    def __init__(self):
        self.me = lax.axis_index("expert")
        self.dp = lax.axis_index("dp")
        self.at = (self.me // 16, (self.me // 4) % 4, self.me % 4)

    def shifted(self, dim, by):
        c = self.at[dim]
        return self.me + (lax.rem(c + by, 4) - c) * STRIDE[dim]


def barrier(place, core):
    sem = pltpu.get_barrier_semaphore()
    for dim in range(3):
        for by in (1, 2, 3):
            pl.semaphore_signal(
                sem, inc=1, device_id=(place.dp, place.shifted(dim, by)), device_id_type=MESH
            )
    if core:
        pl.semaphore_signal(sem, inc=1, device_id=(1 - place.dp, place.me), device_id_type=MESH)
    pl.semaphore_wait(sem, 10 if core else 9)


class Wire:
    def __init__(self, place, send, recv):
        self.place, self.send, self.recv, self.used, self.open = place, send, recv, 0, []

    def take(self):
        self.used += 1
        return self.used - 1

    def _copy(self, src, dst, k, target):
        return pltpu.make_async_remote_copy(
            src_ref=src, dst_ref=dst, send_sem=self.send.at[k], recv_sem=self.recv.at[k],
            device_id=target, device_id_type=MESH,
        )

    def go(self, k, src, dst, dim, by):
        c = self._copy(src, dst, k, (self.place.dp, self.place.shifted(dim, by)))
        c.start()
        self.open.append(c)
        return c

    def cross(self, k, src, dst):
        c = self._copy(src, dst, k, (1 - self.place.dp, self.place.me))
        c.start()
        self.open.append(c)

    def got(self, k, view):
        self._copy(view, view, k, (self.place.dp, self.place.shifted(0, 1))).wait_recv()

    def sent(self, copies):
        for c in copies:
            c.wait_send()
        self.open = [c for c in self.open if all(c is not d for d in copies)]

    def drain(self):
        self.sent(list(self.open))


def mod4(v):
    return lax.rem(v, 4)


def column_terms(meta, a, s2, place):
    dim = ORDERS[a][2]
    blocks = [meta[a, s2, s] for s in range(4)]
    low = lax.broadcasted_iota(jnp.int32, (8, 128), 1) < 64
    turn = [pltpu.roll(b, 64, 1) for b in blocks]
    ids = jnp.concatenate([jnp.where(low, blocks[0], turn[1]), jnp.where(low, blocks[2], turn[3])], axis=1)
    gates = jnp.concatenate([jnp.where(low, turn[0], blocks[1]), jnp.where(low, turn[2], blocks[3])], axis=1)
    row = lax.broadcasted_iota(jnp.int32, (8, 256), 0)
    named = jnp.zeros((8, 256), F32)
    weight = jnp.zeros((8, 256), F32)
    for r in range(8):
        e = 2 * (place.me + (r // 2 - place.at[dim]) * STRIDE[dim]) + r % 2
        hit = ids == e.astype(F32)
        n = jnp.sum(jnp.where(hit, 1.0, 0.0), axis=0, keepdims=True)
        g = jnp.sum(jnp.where(hit, gates, 0.0), axis=0, keepdims=True)
        named = jnp.where(row == r, n, named)
        weight = jnp.where(row == r, g, weight)
    i = lax.broadcasted_iota(jnp.int32, (256, 256), 0)
    l = lax.broadcasted_iota(jnp.int32, (256, 256), 1)
    upper = jnp.where((i // 64 == l // 64) & (i < l), 1.0, 0.0).astype(BF)
    before = jnp.dot(named.astype(BF), upper, preferred_element_type=F32)
    base = (lax.broadcasted_iota(jnp.int32, (8, 256), 1) // 64 * 8).astype(F32)
    return jnp.where(named > 0.5, base + before, -1.0), weight


NT = (((1,), (1,)), ((), ()))


def dispatch_kernel(tok, tan, adj, ids, gates, wg_in, wu_in, wd_in,
                    r0, r1, r2, p0, p1, grown,
                    held, packed, relay, meta, chunk, wg, wu, wd, pre, lin, dirg, diru, back,
                    table, pick, spin, grow, send, recv, local):
    place = Place()
    wire = Wire(place, send, recv)
    outs = (r0, r1, r2)
    at = [(place.at[ORDERS[a][1]], place.at[ORDERS[a][0]]) for a in range(3)]
    spots = iter(range(64))

    def copy(src, dst):
        c = pltpu.make_async_copy(src, dst, local.at[next(spots)])
        c.start()
        return c

    own = [copy(src, held.at[a, at[a][0], at[a][1]]) for a, src in enumerate((tok, tan, adj))]
    heavy = [copy(wg_in, wg), copy(wu_in, wu), copy(wd_in, wd)]
    table[...] = jnp.zeros((128, 128), F32)
    table[0:64, 0:8] = ids[...].astype(F32)
    table[64:128, 0:8] = gates[...]
    turned = table[...].T
    for a in range(3):
        meta[a, at[a][0], at[a][1]] = turned[0:8]
    barrier(place, False)
    for c in own:
        c.wait()

    def half(a, s2, s1, h):
        return held.at[a, s2, s1, pl.ds(32 * h, 32)]

    def spread(a, dim, at2, at1, keys):
        for h in (0, 1):
            wire.go(keys[0][h], half(a, at2, at1, h), half(a, at2, at1, h), dim, 1)
            wire.go(keys[1][1 - h], half(a, at2, at1, 1 - h), half(a, at2, at1, 1 - h), dim, 3)

    def keys_of():
        return ((wire.take(), wire.take()), (wire.take(), wire.take()), (wire.take(), wire.take()))

    first = [keys_of() for _ in range(3)]
    second = [[keys_of() for _ in range(4)] for _ in range(3)]
    rel1 = (0, 3, 1, 2)

    mk1 = [[wire.take() for _ in range(3)] for _ in range(3)]
    mk2 = [[wire.take() for _ in range(3)] for _ in range(3)]
    for a in range(3):
        n2, n1 = at[a]
        for i, by in enumerate((1, 2, 3)):
            wire.go(mk1[a][i], meta.at[a, n2, n1], meta.at[a, n2, n1], ORDERS[a][0], by)
    for a in range(3):
        n2, n1 = at[a]
        spread(a, ORDERS[a][0], n2, n1, first[a])
    for a in range(3):
        n2, n1 = at[a]
        spread(a, ORDERS[a][1], n2, n1, second[a][0])
    for a in range(3):
        n2, n1 = at[a]
        for i, by in enumerate((1, 2, 3)):
            wire.got(mk1[a][i], meta.at[a, n2, mod4(n1 + 4 - by)])
        for i, by in enumerate((1, 2, 3)):
            wire.go(mk2[a][i], meta.at[a, n2], meta.at[a, n2], ORDERS[a][1], by)

    def pass_on(a, dim, keys, minus, plus):
        wire.got(keys[0][0], minus(0))
        wire.go(keys[2][0], minus(0), minus(0), dim, 1)
        wire.got(keys[1][1], plus(1))
        wire.go(keys[2][1], plus(1), plus(1), dim, 3)

    def rest(keys, minus, plus):
        wire.got(keys[0][1], minus(1))
        wire.got(keys[1][0], plus(0))

    def views1(a):
        n2, n1 = at[a]
        return (lambda h: half(a, n2, mod4(n1 + 3), h)), (lambda h: half(a, n2, mod4(n1 + 1), h))

    def views2(a, b):
        n2, n1 = at[a]
        s1 = mod4(n1 + rel1[b])
        return (lambda h: half(a, mod4(n2 + 3), s1, h)), (lambda h: half(a, mod4(n2 + 1), s1, h))

    for a in range(3):
        pass_on(a, ORDERS[a][0], first[a], *views1(a))
    for a in range(3):
        rest(first[a], *views1(a))
        n2, n1 = at[a]
        for b in (1, 2):
            spread(a, ORDERS[a][1], n2, mod4(n1 + rel1[b]), second[a][b])
    for a in range(3):
        pass_on(a, ORDERS[a][1], second[a][0], *views2(a, 0))
    for a in range(3):
        n2, n1 = at[a]
        wire.got(first[a][2][0], half(a, n2, mod4(n1 + 2), 0))
        wire.got(first[a][2][1], half(a, n2, mod4(n1 + 2), 1))
        spread(a, ORDERS[a][1], n2, mod4(n1 + 2), second[a][3])

    slots = lax.broadcasted_iota(jnp.int32, (32, 256), 0).astype(F32)
    stored = []

    def weigh(a, r):
        index, weight = column_terms(meta, a, mod4(at[a][0] + r), place)
        for e in range(8):
            spin[pl.ds(32 * e, 32), :] = jnp.where(index[e : e + 1, :] == slots, weight[e : e + 1, :], 0.0)
        w = spin[...].T
        high = w.astype(BF)
        n = len(stored)
        if n >= 2:
            stored[n - 2].wait()
        grow[n % 2, 0] = high
        grow[n % 2, 1] = (w - high.astype(F32)).astype(BF)
        stored.append(copy(grow.at[n % 2], grown.at[a, r]))

    third = [[[wire.take() for _ in range(6)] for _ in range(4)] for _ in range(3)]
    going, kept = {}, {}
    turn = {0: 0, 1: 1, 3: 0, 2: 1}

    def pack(a, r):
        n2, n1 = at[a]
        dim = ORDERS[a][2]
        n3 = place.at[dim]
        s2 = mod4(n2 + r)
        buf = turn[r]
        index, _ = column_terms(meta, a, s2, place)
        for e in range(8):
            pick[pl.ds(32 * e, 32), :] = jnp.where(index[e : e + 1, :] == slots, 1.0, 0.0).astype(BF)
        chosen = pick[...]
        if r in (3, 2):
            before = 0 if r == 3 else 1
            wire.sent(going.pop((a, before)))
            kept[a, before].wait()

        @pl.loop(0, 4)
        def _(n):
            cols = pl.ds(pl.multiple_of(n * 512, 512), 512)
            rows = held[a, s2, :, :, cols].reshape(256, 512)
            got = jnp.dot(chosen, rows, preferred_element_type=F32).astype(BF)
            packed[a, buf, :, :, :, cols] = got.reshape(4, 2, 32, 512)

        k = third[a][r]
        far, right, left = mod4(n3 + 2), mod4(n3 + 1), mod4(n3 + 3)
        going[a, r] = [
            wire.go(k[0], packed.at[a, buf, far, 0], relay.at[a, r, 0], dim, 1),
            wire.go(k[1], packed.at[a, buf, far, 1], relay.at[a, r, 1], dim, 3),
            wire.go(k[2], packed.at[a, buf, right], outs[a].at[:, n3, s2], dim, 1),
            wire.go(k[3], packed.at[a, buf, left], outs[a].at[:, n3, s2], dim, 3),
        ]
        kept[a, r] = copy(packed.at[a, buf, n3], outs[a].at[:, n3, s2])

    def relays(a, r):
        n2, n1 = at[a]
        dim = ORDERS[a][2]
        n3 = place.at[dim]
        s2 = mod4(n2 + r)
        k = third[a][r]
        wire.got(k[0], relay.at[a, r, 0])
        wire.go(k[4], relay.at[a, r, 0], outs[a].at[0, mod4(n3 + 3), s2], dim, 1)
        wire.got(k[1], relay.at[a, r, 1])
        wire.go(k[5], relay.at[a, r, 1], outs[a].at[1, mod4(n3 + 1), s2], dim, 3)

    def fetch(a, r):
        n3 = place.at[ORDERS[a][2]]
        s2 = mod4(at[a][0] + r)
        k = third[a][r]
        wire.got(k[2], outs[a].at[:, mod4(n3 + 3), s2])
        wire.got(k[3], outs[a].at[:, mod4(n3 + 1), s2])
        wire.got(k[4], outs[a].at[0, mod4(n3 + 2), s2])
        wire.got(k[5], outs[a].at[1, mod4(n3 + 2), s2])
        return copy(outs[a].at[:, :, s2], chunk.at[a, turn[r]])

    def layer(a, r):
        s2 = mod4(at[a][0] + r)
        buf = turn[r]

        @pl.loop(0, 6)
        def _(i):
            j, n = i // 3, i % 3
            cols = pl.ds(pl.multiple_of(n * 256, 256), 256)
            rows = chunk[a, buf, j].reshape(128, D)
            if a == 2:
                got = lax.dot_general(rows, wd[j, cols, :], NT, preferred_element_type=F32)
                back[j, :, s2, :, :, cols] = got.reshape(4, 4, 8, 256)
            else:
                x, y = (pre, lin) if a == 0 else (dirg, diru)
                got = jnp.dot(rows, wg[j, :, cols], preferred_element_type=F32)
                x[j, :, s2, :, :, cols] = got.reshape(4, 4, 8, 256)
                got = jnp.dot(rows, wu[j, :, cols], preferred_element_type=F32)
                y[j, :, s2, :, :, cols] = got.reshape(4, 4, 8, 256)

    def layers(r):
        for a in range(3):
            if r in (3, 2):
                kept[a, r].wait()
        loads = [fetch(a, r) for a in range(3)]
        for a in range(3):
            loads[a].wait()
            layer(a, r)

    for a in range(3):
        n2, n1 = at[a]
        for i, by in enumerate((1, 2, 3)):
            wire.got(mk2[a][i], meta.at[a, mod4(n2 + 4 - by)])
    for a in range(3):
        pack(a, 0)
    for b in (1, 2):
        for a in range(3):
            pass_on(a, ORDERS[a][1], second[a][b], *views2(a, b))
            weigh(a, 2 * b - 2)
            weigh(a, 2 * b - 1)
    for a in range(3):
        pass_on(a, ORDERS[a][1], second[a][3], *views2(a, 3))
    for a in range(3):
        for b in range(4):
            rest(second[a][b], *views2(a, b))
        pack(a, 1)
    for a in range(3):
        relays(a, 0)
    for a in range(3):
        n2, n1 = at[a]
        for b in range(4):
            s1 = mod4(n1 + rel1[b])
            wire.got(second[a][b][2][0], half(a, mod4(n2 + 2), s1, 0))
            wire.got(second[a][b][2][1], half(a, mod4(n2 + 2), s1, 1))
    for a in range(3):
        pack(a, 3)
    for a in range(3):
        relays(a, 1)
    for c in heavy:
        c.wait()
    layers(0)
    for a in range(3):
        pack(a, 2)
    for a in range(3):
        relays(a, 3)
    layers(1)
    for a in range(3):
        relays(a, 2)
    layers(3)
    layers(2)
    wire.drain()

    written = []
    for j in range(2):

        @pl.loop(0, 24)
        def _(i):
            n, q = i % 3, i // 3
            zp, xp, yp = q // 4, (q // 2) % 2, q % 2
            cols = pl.ds(pl.multiple_of(n * 256, 256), 256)
            cols_up = pl.ds(pl.multiple_of(FF + n * 256, 256), 256)
            part = {}
            for dz in range(2):
                for dx in range(2):
                    for dy in range(2):
                        z, x, y = 2 * zp + dz, 2 * xp + dx, 2 * yp + dy
                        p, l = pre[j, z, x, y, :, cols], lin[j, z, x, y, :, cols]
                        pd, ld = dirg[j, y, z, x, :, cols], diru[j, y, z, x, :, cols]
                        b = back[j, x, y, z, :, cols]
                        s = jax.nn.sigmoid(p)
                        one = s * (1.0 + p * (1.0 - s))
                        two = s * (1.0 - s) * (2.0 + p * (1.0 - 2.0 * s))
                        part[dz, dx, dy] = (b * (ld * one + l * two * pd), b * one * pd)

            def put(a, hi, lo, d_hi, d_lo, inner, pair):
                rows = pl.ds(pl.multiple_of(16 * inner, 16), 16)
                for which, where in ((0, cols), (1, cols_up)):
                    value = jnp.concatenate([v[which] for v in pair], axis=0).astype(BF)
                    if j == 0:
                        chunk[a, hi, d_hi, 2 * lo + d_lo, rows, where] = value
                    else:
                        packed[a, hi, 2 * d_hi + lo, d_lo, rows, where] = value

            for u in range(2):
                for w in range(2):
                    put(0, zp, xp, u, w, yp, (part[u, w, 0], part[u, w, 1]))
                    put(1, yp, zp, u, w, xp, (part[w, 0, u], part[w, 1, u]))
                    put(2, xp, yp, u, w, zp, (part[0, u, w], part[1, u, w]))

        for a in range(3):
            src, dst = (chunk, p0) if j == 0 else (packed, p1)
            written.append(copy(src.at[a, :, :, :, :, pl.ds(0, 2 * FF)], dst.at[a]))
    for c in written:
        c.wait()
    for c in stored[-2:]:
        c.wait()


N_DISPATCH = 3 * 6 + 12 * 6 + 18 + 72


def dispatch(tok, tan, adj, ids, gates, wg, wu, wd):
    vmem = pl.BlockSpec(memory_space=pltpu.VMEM)
    hbm = pl.BlockSpec(memory_space=pl.ANY)
    rows = jax.ShapeDtypeStruct((2, 4, 4, 32, D), BF)
    out = pl.pallas_call(
        dispatch_kernel,
        out_shape=(
            rows, rows, rows,
            jax.ShapeDtypeStruct((3, 2, 2, 4, 32, 2 * FF), BF),
            jax.ShapeDtypeStruct((3, 2, 4, 2, 32, 2 * FF), BF),
            jax.ShapeDtypeStruct((3, 4, 2, 256, 256), BF),
        ),
        in_specs=[hbm] * 3 + [vmem] * 2 + [hbm] * 3,
        out_specs=(hbm,) * 6,
        scratch_shapes=[
            pltpu.VMEM((3, 4, 4, TOK, D), BF),
            pltpu.VMEM((3, 2, 4, 2, 32, D), BF),
            pltpu.VMEM((3, 4, 2, 32, D), BF),
            pltpu.VMEM((3, 4, 4, 8, 128), F32),
            pltpu.VMEM((3, 2, 2, 4, 32, D), BF),
            pltpu.VMEM((2, D, FF), BF),
            pltpu.VMEM((2, D, FF), BF),
            pltpu.VMEM((2, FF, D), BF),
        ]
        + [pltpu.VMEM((2, 4, 4, 4, 8, FF), F32)] * 5
        + [
            pltpu.VMEM((128, 128), F32),
            pltpu.VMEM((256, 256), BF),
            pltpu.VMEM((256, 256), F32),
            pltpu.VMEM((2, 2, 256, 256), BF),
            pltpu.SemaphoreType.DMA((N_DISPATCH,)),
            pltpu.SemaphoreType.DMA((N_DISPATCH,)),
            pltpu.SemaphoreType.DMA((64,)),
        ],
        compiler_params=pltpu.CompilerParams(
            collective_id=1, has_side_effects=True, vmem_limit_bytes=67043328
        ),
        name="dispatch",
    )(tok, tan, adj, ids, gates, wg, wu, wd)
    return out[3:]


def collect_kernel(p0, p1, wg_in, wu_in, grown_in, tan, hvp, ratio, *scratch):
    place = Place()
    n_part = 10
    parts = [scratch[i * n_part : (i + 1) * n_part] for i in range(9)]
    left, wg, wu, grown, sums, send, recv, local = scratch[9 * n_part :]
    wire = Wire(place, send, recv)
    spots = iter(range(64))

    def copy(src, dst):
        c = pltpu.make_async_copy(src, dst, local.at[next(spots)])
        c.start()
        return c

    loads = {}
    for q in range(3):
        for a, f0, n in PARTS[q]:
            got = []
            if q == 0:
                got = [copy(p0.at[a], left.at[0, a]), copy(p1.at[a], left.at[1, a])]
            rows = pl.ds(f0, n)
            got.append(copy(wg_in.at[:, rows], wg.at[:, rows]))
            got.append(copy(wu_in.at[:, rows], wu.at[:, rows]))
            loads[q, a] = got
        if q == 0:
            grown_load = copy(grown_in, grown)
    barrier(place, True)
    keys = [[[wire.take() for _ in range(14)] for _ in range(3)] for _ in range(3)]
    tot = [[wire.take() for _ in range(3)] for _ in range(3)]
    cross = wire.take()
    at = [tuple(place.at[d] for d in ORDERS[a]) for a in range(3)]
    moved = {}
    state = {"square": jnp.zeros((8, 128), F32)}

    def begin(q):
        for a, f0, n in PARTS[q]:
            out, back, relay = parts[3 * q + a][:3]
            for c in loads[q, a]:
                c.wait()
            for j in range(2):
                got = lax.dot_general(left[j, a, :, 0:FF], wg[j, f0 : f0 + n, :], NT, preferred_element_type=F32)
                got += lax.dot_general(left[j, a, :, FF : 2 * FF], wu[j, f0 : f0 + n, :], NT, preferred_element_type=F32)
                out[:, :, 32 * j : 32 * j + 32, :] = got.astype(BF).reshape(4, 4, 32, n)
            n3, dim = at[a][2], ORDERS[a][2]
            k = keys[q][a]
            far = mod4(n3 + 2)
            wire.go(k[0], out.at[far, pl.ds(0, 2)], relay.at[0], dim, 1)
            wire.go(k[1], out.at[far, pl.ds(2, 2)], relay.at[1], dim, 3)
            wire.go(k[2], out.at[mod4(n3 + 1)], back.at[:, n3], dim, 1)
            wire.go(k[3], out.at[mod4(n3 + 3)], back.at[:, n3], dim, 3)
            moved[q, a] = copy(out.at[n3], back.at[:, n3])

    def relays(q):
        for a, _, _ in PARTS[q]:
            back, relay = parts[3 * q + a][1:3]
            n3, dim = at[a][2], ORDERS[a][2]
            k = keys[q][a]
            wire.got(k[0], relay.at[0])
            wire.go(k[4], relay.at[0], back.at[pl.ds(0, 2), mod4(n3 + 3)], dim, 1)
            wire.got(k[1], relay.at[1])
            wire.go(k[5], relay.at[1], back.at[pl.ds(2, 2), mod4(n3 + 1)], dim, 3)

    def total(q, a, r):
        n = PARTS[q][a][2]
        rows = parts[3 * q + a][1][mod4(at[a][1] + r)].reshape(256, n)
        got = jnp.dot(grown[a, r, 0], rows, preferred_element_type=F32)
        got = got + jnp.dot(grown[a, r, 1], rows, preferred_element_type=F32)
        return got.reshape(4, 64, n)

    def far2(q):
        for a, _, n in PARTS[q]:
            back, relay, own, out2, mid2 = parts[3 * q + a][1:6]
            n3, dim = at[a][2], ORDERS[a][1]
            k = keys[q][a]
            moved[q, a].wait()
            wire.got(k[2], back.at[:, mod4(n3 + 3)])
            wire.got(k[3], back.at[:, mod4(n3 + 1)])
            wire.got(k[4], back.at[pl.ds(0, 2), mod4(n3 + 2)])
            wire.got(k[5], back.at[pl.ds(2, 2), mod4(n3 + 2)])
            out2[...] = total(q, a, 2).astype(BF)
            wire.go(k[6], out2.at[pl.ds(0, 2)], mid2.at[0], dim, 1)
            wire.go(k[7], out2.at[pl.ds(2, 2)], mid2.at[1], dim, 3)
        for a, _, n in PARTS[q]:
            parts[3 * q + a][3][...] = total(q, a, 0)

    def near2(q):
        for a, _, n in PARTS[q]:
            mid2, to2, in2 = parts[3 * q + a][5:8]
            k, dim = keys[q][a], ORDERS[a][1]
            for side, r in ((0, 1), (1, 3)):
                got = total(q, a, r)
                wire.got(k[6 + side], mid2.at[side])
                came = mid2[side].astype(F32)
                lo, hi = got[0:2], got[2:4]
                if side == 0:
                    lo = lo + came
                else:
                    hi = hi + came
                to2[side, 0:2] = lo.astype(BF)
                to2[side, 2:4] = hi.astype(BF)
                wire.go(k[8 + side], to2.at[side], in2.at[side], dim, r)

    def far1(q):
        for a, _, n in PARTS[q]:
            own, in2, out1, mid1 = (parts[3 * q + a][i] for i in (3, 7, 8, 9))
            n1, dim = at[a][0], ORDERS[a][0]
            k = keys[q][a]
            wire.got(k[8], in2.at[0])
            wire.got(k[9], in2.at[1])
            own[...] = own[...] + (in2[0].astype(F32) + in2[1].astype(F32))
            out1[0] = own[mod4(n1 + 2)].astype(BF)
            wire.go(k[10], out1.at[0, pl.ds(0, 32)], mid1.at[0, pl.ds(0, 32)], dim, 1)
            wire.go(k[11], out1.at[0, pl.ds(32, 32)], mid1.at[0, pl.ds(32, 32)], dim, 3)

    def near1(q):
        for a, _, n in PARTS[q]:
            own, in2, out1, mid1 = (parts[3 * q + a][i] for i in (3, 7, 8, 9))
            n1, dim = at[a][0], ORDERS[a][0]
            k = keys[q][a]
            for side, r in ((0, 1), (1, 3)):
                rows = pl.ds(32 * side, 32)
                rest = pl.ds(32 - 32 * side, 32)
                wire.got(k[10 + side], mid1.at[0, rows])
                s = mod4(n1 + r)
                out1[1 + side, rows] = (own[s, rows] + mid1[0, rows].astype(F32)).astype(BF)
                out1[1 + side, rest] = own[s, rest].astype(BF)
                wire.go(k[12 + side], out1.at[1 + side], mid1.at[1 + side], dim, r)

    def finish(q):
        for a, f0, n in PARTS[q]:
            own, mid1 = parts[3 * q + a][3], parts[3 * q + a][9]
            k = keys[q][a]
            wire.got(k[12], mid1.at[1])
            wire.got(k[13], mid1.at[2])
            got = own[at[a][0]] + (mid1[1].astype(F32) + mid1[2].astype(F32))
            hvp[:, f0 : f0 + n] = got
            state["square"] += jnp.sum((got * got).reshape(8, 8, n // 128, 128), axis=(0, 2))

    begin(0)
    begin(1)
    relays(0)
    begin(2)
    relays(1)
    grown_load.wait()
    far2(0)
    relays(2)
    near2(0)
    far2(1)
    far1(0)
    near2(1)
    far2(2)
    near1(0)
    far1(1)
    near2(2)
    t = tan[...].astype(F32)
    low = jnp.sum((t * t).reshape(8, 8, 16, 128), axis=(0, 2))
    finish(0)
    near1(1)
    far1(2)
    finish(1)
    near1(2)
    finish(2)

    value = (state["square"], low)
    for dim in range(3):
        c = place.at[dim]
        grid = sums.at[pl.ds(4 + 4 * dim, 4)]
        grid[c, 0] = value[0]
        grid[c, 1] = value[1]
        for i, by in enumerate((1, 2, 3)):
            wire.go(tot[dim][i], grid.at[c], grid.at[c], dim, by)
        for i, by in enumerate((1, 2, 3)):
            wire.got(tot[dim][i], grid.at[mod4(c + 4 - by)])
        value = tuple((grid[0, q] + grid[1, q]) + (grid[2, q] + grid[3, q]) for q in range(2))
    sums[place.dp, 0] = value[0]
    sums[place.dp, 1] = value[1]
    wire.cross(cross, sums.at[place.dp], sums.at[place.dp])
    wire.got(cross, sums.at[1 - place.dp])
    top = jnp.sum(sums[0, 0] + sums[1, 0])
    low = jnp.sum(sums[0, 1] + sums[1, 1])
    ratio[...] = jnp.full((8, 128), top, F32) / jnp.full((8, 128), low, F32)
    wire.drain()


N_COLLECT = 9 * 14 + 9 + 1


def collect(p0, p1, wg, wu, grown, tan):
    vmem = pl.BlockSpec(memory_space=pltpu.VMEM)
    hbm = pl.BlockSpec(memory_space=pl.ANY)
    scratch = []
    for q in range(3):
        for _, _, f in PARTS[q]:
            scratch += [
                pltpu.VMEM((4, 4, 64, f), BF),
                pltpu.VMEM((4, 4, 64, f), BF),
                pltpu.VMEM((2, 2, 64, f), BF),
                pltpu.VMEM((4, 64, f), F32),
                pltpu.VMEM((4, 64, f), BF),
                pltpu.VMEM((2, 2, 64, f), BF),
                pltpu.VMEM((2, 4, 64, f), BF),
                pltpu.VMEM((2, 4, 64, f), BF),
                pltpu.VMEM((3, 64, f), BF),
                pltpu.VMEM((3, 64, f), BF),
            ]
    scratch += [
        pltpu.VMEM((2, 3, 512, 2 * FF), BF),
        pltpu.VMEM((2, D, FF), BF),
        pltpu.VMEM((2, D, FF), BF),
        pltpu.VMEM((3, 4, 2, 256, 256), BF),
        pltpu.VMEM((16, 2, 8, 128), F32),
        pltpu.SemaphoreType.DMA((N_COLLECT,)),
        pltpu.SemaphoreType.DMA((N_COLLECT,)),
        pltpu.SemaphoreType.DMA((64,)),
    ]
    return pl.pallas_call(
        collect_kernel,
        out_shape=(jax.ShapeDtypeStruct((TOK, D), F32), jax.ShapeDtypeStruct((8, 128), F32)),
        in_specs=[hbm] * 5 + [vmem],
        out_specs=(vmem, vmem),
        scratch_shapes=scratch,
        compiler_params=pltpu.CompilerParams(
            collective_id=2, has_side_effects=True, vmem_limit_bytes=60 * 2**20
        ),
        name="collect",
    )(p0, p1, wg, wu, grown, tan)


def local(tokens, tangent, adjoint, gates, expert_ids, w_gate, w_up, w_down):
    p0, p1, grown = dispatch(tokens, tangent, adjoint, expert_ids, gates, w_gate, w_up, w_down)
    p0, p1 = p0.reshape(3, 512, 2 * FF), p1.reshape(3, 512, 2 * FF)
    hvp, ratio = collect(p0, p1, w_gate, w_up, grown, tangent)
    return hvp, ratio[0, 0]


def solution(mesh):
    rows = P(("dp", "expert"), None)
    weights = P("expert", None, None)
    return jax.shard_map(
        local,
        mesh=mesh,
        in_specs=(rows,) * 5 + (weights,) * 3,
        out_specs=(rows, P()),
        check_vma=False,
    )
```

```python
import functools

import jax
import jax.numpy as jnp
from jax import lax
from jax.experimental import pallas as pl
from jax.experimental.pallas import tpu as pltpu
from jax.sharding import PartitionSpec as P

MESH = pl.DeviceIdType.MESH
STRIDE = (16, 4, 1)
ORDERS = ((0, 1, 2), (1, 2, 0), (2, 0, 1))
PARTS = (
    ((0, 0, 256), (1, 768, 256), (2, 1408, 256)),
    ((0, 256, 256), (1, 1024, 256), (2, 1664, 256)),
    ((0, 512, 256), (1, 1280, 128), (2, 1920, 128)),
)
TOK, D, FF, R = 64, 2048, 768, 4
BF, F32 = jnp.bfloat16, jnp.float32


class Place:
    def __init__(self):
        self.me = lax.axis_index("expert")
        self.dp = lax.axis_index("dp")
        self.at = (self.me // 16, (self.me // 4) % 4, self.me % 4)

    def shifted(self, dim, by):
        c = self.at[dim]
        return self.me + (lax.rem(c + by, 4) - c) * STRIDE[dim]


def barrier(place):
    sem = pltpu.get_barrier_semaphore()
    for dim in range(3):
        for by in (1, 2, 3):
            pl.semaphore_signal(
                sem, inc=1, device_id=(place.dp, place.shifted(dim, by)), device_id_type=MESH
            )
    pl.semaphore_wait(sem, 9)


class Wire:
    def __init__(self, place, send, recv):
        self.place, self.send, self.recv, self.groups, self.taken = place, send, recv, 0, 0

    def group(self):
        self.groups += 1
        return self.groups - 1

    def take(self):
        self.taken += 1
        return self.taken - 1

    def _copy(self, sent, came, src, dst, target):
        return pltpu.make_async_remote_copy(
            src_ref=src, dst_ref=dst, send_sem=self.send.at[sent], recv_sem=self.recv.at[came],
            device_id=target, device_id_type=MESH,
        )

    def push(self, sent, came, src, dst, target):
        self._copy(sent, came, src, dst, target).start()

    def go(self, sent, came, src, dst, dim, by):
        self.push(sent, came, src, dst, (self.place.dp, self.place.shifted(dim, by)))

    def got(self, came, view):
        self._copy(0, came, view, view, (self.place.dp, self.place.shifted(0, 1))).wait_recv()

    def sent(self, group, view):
        self._copy(group, 0, view, view, (self.place.dp, self.place.shifted(0, 1))).wait_send()


def mod4(v):
    return lax.rem(v, 4)


def column_terms(meta, a, s2, place):
    dim = ORDERS[a][2]
    blocks = [meta[a, s2, s] for s in range(4)]
    low = lax.broadcasted_iota(jnp.int32, (8, 128), 1) < 64
    turn = [pltpu.roll(b, 64, 1) for b in blocks]
    ids = jnp.concatenate([jnp.where(low, blocks[0], turn[1]), jnp.where(low, blocks[2], turn[3])], axis=1)
    gates = jnp.concatenate([jnp.where(low, turn[0], blocks[1]), jnp.where(low, turn[2], blocks[3])], axis=1)
    row = lax.broadcasted_iota(jnp.int32, (8, 256), 0)
    named = jnp.zeros((8, 256), F32)
    weight = jnp.zeros((8, 256), F32)
    for r in range(8):
        e = 2 * (place.me + (r // 2 - place.at[dim]) * STRIDE[dim]) + r % 2
        hit = ids == e.astype(F32)
        n = jnp.sum(jnp.where(hit, 1.0, 0.0), axis=0, keepdims=True)
        g = jnp.sum(jnp.where(hit, gates, 0.0), axis=0, keepdims=True)
        named = jnp.where(row == r, n, named)
        weight = jnp.where(row == r, g, weight)
    i = lax.broadcasted_iota(jnp.int32, (256, 256), 0)
    l = lax.broadcasted_iota(jnp.int32, (256, 256), 1)
    upper = jnp.where((i // 64 == l // 64) & (i < l), 1.0, 0.0).astype(BF)
    before = jnp.dot(named.astype(BF), upper, preferred_element_type=F32)
    base = (lax.broadcasted_iota(jnp.int32, (8, 256), 1) // 64 * 8).astype(F32)
    return jnp.where(named > 0.5, base + before, -1.0), weight


NT = (((1,), (1,)), ((), ()))


def dispatch_kernel(tok, tan, adj, ids, gates, wg_in, wu_in, wd_in,
                    r0, r1, r2, b0, b1, b2, grown,
                    held, packed, relay, meta, chunk, wg, wu, wd, pre, lin, dirg, diru, back, parts,
                    o0, o1, o2, q0, q1, q2, picks, spin, grow, send, recv, local):
    place = Place()
    wire = Wire(place, send, recv)
    outs, backs, replies, passing = (r0, r1, r2), (b0, b1, b2), (o0, o1, o2), (q0, q1, q2)
    at = [(place.at[ORDERS[a][1]], place.at[ORDERS[a][0]]) for a in range(3)]

    def copy(src, dst, spot):
        c = pltpu.make_async_copy(src, dst, local.at[spot])
        c.start()
        return c

    own = [copy(src, held.at[a, at[a][0], at[a][1]], a) for a, src in enumerate((tok, tan, adj))]
    heavy = [copy(wg_in, wg, 3), copy(wu_in, wu, 4), copy(wd_in, wd, 5)]
    turned = jnp.concatenate([ids[...].astype(F32), gates[...]], axis=1)
    for a in range(3):
        meta[a, at[a][0], at[a][1]] = turned
    barrier(place)
    for c in own:
        c.wait()

    def half(a, s2, s1, h):
        return held.at[a, s2, s1, pl.ds(32 * h, 32)]

    def spread(a, dim, at2, at1, keys):
        plus, minus, rest, _, sent = keys
        wire.go(sent, plus, half(a, at2, at1, 0), half(a, at2, at1, 0), dim, 1)
        wire.go(sent, minus, half(a, at2, at1, 1), half(a, at2, at1, 1), dim, 3)
        wire.go(sent, rest, half(a, at2, at1, 1), half(a, at2, at1, 1), dim, 1)
        wire.go(sent, rest, half(a, at2, at1, 0), half(a, at2, at1, 0), dim, 3)

    first, second = [], []
    for a in range(3):
        sent = wire.group()
        first.append((wire.take(), wire.take(), wire.take(), wire.take(), sent))
        sent, rest_key, far_key = wire.group(), wire.take(), wire.take()
        second.append([(wire.take(), wire.take(), rest_key, far_key, sent) for _ in range(4)])
    rel1 = (0, 3, 1, 2)

    mk1 = [(wire.group(), wire.take()) for _ in range(3)]
    mk2 = [(wire.group(), wire.take()) for _ in range(3)]
    for a in range(3):
        n2, n1 = at[a]
        for by in (1, 2, 3):
            wire.go(*mk1[a], meta.at[a, n2, n1], meta.at[a, n2, n1], ORDERS[a][0], by)
    for a in range(3):
        n2, n1 = at[a]
        spread(a, ORDERS[a][0], n2, n1, first[a])
    for a in range(3):
        n2, n1 = at[a]
        spread(a, ORDERS[a][1], n2, n1, second[a][0])
    for a in range(3):
        n2, n1 = at[a]
        wire.got(mk1[a][1], meta.at[a, n2, pl.ds(0, 3)])
        for by in (1, 2, 3):
            wire.go(*mk2[a], meta.at[a, n2], meta.at[a, n2], ORDERS[a][1], by)

    def pass_on(a, dim, keys, minus, plus):
        from_minus, from_plus, _, far, sent = keys
        wire.got(from_minus, minus(0))
        wire.go(sent, far, minus(0), minus(0), dim, 1)
        wire.got(from_plus, plus(1))
        wire.go(sent, far, plus(1), plus(1), dim, 3)

    def views1(a):
        n2, n1 = at[a]
        return (lambda h: half(a, n2, mod4(n1 + 3), h)), (lambda h: half(a, n2, mod4(n1 + 1), h))

    def views2(a, b):
        n2, n1 = at[a]
        s1 = mod4(n1 + rel1[b])
        return (lambda h: half(a, mod4(n2 + 3), s1, h)), (lambda h: half(a, mod4(n2 + 1), s1, h))

    for a in range(3):
        pass_on(a, ORDERS[a][0], first[a], *views1(a))
    for a in range(3):
        n2, n1 = at[a]
        wire.got(first[a][2], held.at[a, n2, mod4(n1 + 1)])
        for b in (1, 2):
            spread(a, ORDERS[a][1], n2, mod4(n1 + rel1[b]), second[a][b])
    for a in range(3):
        pass_on(a, ORDERS[a][1], second[a][0], *views2(a, 0))
    for a in range(3):
        n2, n1 = at[a]
        wire.got(first[a][3], held.at[a, n2, mod4(n1 + 2)])
        spread(a, ORDERS[a][1], n2, mod4(n1 + 2), second[a][3])

    slots = lax.broadcasted_iota(jnp.int32, (32, 256), 0).astype(F32)
    stored = []

    def weigh(a, r):
        index, weight = column_terms(meta, a, mod4(at[a][0] + r), place)
        for e in range(8):
            spin[pl.ds(32 * e, 32), :] = jnp.where(index[e : e + 1, :] == slots, weight[e : e + 1, :], 0.0)
        w = spin[...].T
        high = w.astype(BF)
        for e in range(8):
            hit = jnp.where(index[e : e + 1, :] == slots, 1.0, 0.0)
            picks[a, r, e % 2, pl.ds(32 * (e // 2), 32), :] = hit.astype(BF)
        n = len(stored)
        if n >= 2:
            stored[n - 2].wait()
        grow[n % 2, 0] = high
        grow[n % 2, 1] = (w - high.astype(F32)).astype(BF)
        stored.append(copy(grow.at[n % 2], grown.at[a, r], 6 + n % 2))

    third = [[(wire.group(), wire.take(), wire.take()) for _ in range(8)] for _ in range(3)]
    fourth = [[(wire.group(), wire.take(), wire.take()) for _ in range(2)] for _ in range(3)]
    passed = [wire.group() for _ in range(3)]
    repassed = [wire.group() for _ in range(3)]
    kept = {}
    rels = (0, 1, 3, 2)

    def where(a, s):
        dim = ORDERS[a][2]
        return s // 4, place.at[dim], mod4(at[a][0] + rels[s % 4]), dim

    def settle(a, s):
        c = kept.pop((a, s), None)
        if c is not None:
            c.wait()

    def pack(s):
        for a in range(3):
            j, n3, s2, dim = where(a, s)
            buf = s % 3
            chosen = picks[a, rels[s % 4], j]
            if s >= 3:
                wire.sent(third[a][s - 3][0], packed.at[a, buf, pl.ds(0, 3)])
                settle(a, s - 3)

            @pl.loop(0, 4)
            def _(n):
                cols = pl.ds(pl.multiple_of(n * 512, 512), 512)
                rows = held[a, s2, :, :, cols].reshape(256, 512)
                got = jnp.dot(chosen, rows, preferred_element_type=F32).astype(BF)
                packed[a, buf, :, :, cols] = got.reshape(4, 32, 512)

            sent, early, _ = third[a][s]
            far = mod4(n3 + 2)
            wire.go(sent, early, packed.at[a, buf, far, pl.ds(0, 16)], relay.at[a, s, 0], dim, 1)
            wire.go(sent, early, packed.at[a, buf, far, pl.ds(16, 16)], relay.at[a, s, 1], dim, 3)

    def direct(s):
        for a in range(3):
            j, n3, s2, dim = where(a, s)
            buf = s % 3
            sent, _, late = third[a][s]
            wire.go(sent, late, packed.at[a, buf, mod4(n3 + 1)], outs[a].at[j, n3, s2], dim, 1)
            wire.go(sent, late, packed.at[a, buf, mod4(n3 + 3)], outs[a].at[j, n3, s2], dim, 3)
            kept[a, s] = copy(packed.at[a, buf, n3], outs[a].at[j, n3, s2], 8 + 3 * a + buf)

    def relays(s):
        for a in range(3):
            j, n3, s2, dim = where(a, s)
            _, early, late = third[a][s]
            sent = passed[a]
            wire.got(early, relay.at[a, s])
            wire.go(sent, late, relay.at[a, s, 0], outs[a].at[j, mod4(n3 + 3), s2, pl.ds(0, 16)], dim, 1)
            wire.go(sent, late, relay.at[a, s, 1], outs[a].at[j, mod4(n3 + 1), s2, pl.ds(16, 16)], dim, 3)

    loads = {}

    def fetch(s):
        for a in range(3):
            j, n3, s2, dim = where(a, s)
            wire.got(third[a][s][2], outs[a].at[j, pl.ds(0, 3), s2])
            settle(a, s)
            loads[a, s] = copy(outs[a].at[j, :, s2], chunk.at[a, s % 4], 17 + 4 * a + s % 4)

    def layer(s, stages):
        j, half2 = s // 4, s % 4
        for a in range(3):
            if 0 in stages:
                loads[a, s].wait()
                loads[a, s + 1].wait()
            spots2 = [where(a, s + i)[2] for i in range(2)]

            @pl.loop(min(stages), max(stages) + 1)
            def _(n):
                cols = pl.ds(pl.multiple_of(n * 256, 256), 256)
                rows = chunk[a, half2 : half2 + 2].reshape(256, D)

                def put(ref, value):
                    value = value.reshape(2, 4, 4, 8, 256)
                    for i in range(2):
                        ref[:, spots2[i], :, :, cols] = value[i]

                if a == 2:
                    put(back, lax.dot_general(rows, wd[j, cols, :], NT, preferred_element_type=F32))
                else:
                    x, y = (pre, lin) if a == 0 else (dirg, diru)
                    put(x, jnp.dot(rows, wg[j, :, cols], preferred_element_type=F32))
                    put(y, jnp.dot(rows, wu[j, :, cols], preferred_element_type=F32))

    def mix():
        @pl.loop(0, 24)
        def _(i):
            n, q = i % 3, i // 3
            zp, xp, yp = q // 4, (q // 2) % 2, q % 2
            cols = pl.ds(pl.multiple_of(n * 256, 256), 256)
            part = {}
            for dz in range(2):
                for dx in range(2):
                    for dy in range(2):
                        z, x, y = 2 * zp + dz, 2 * xp + dx, 2 * yp + dy
                        p, l = pre[z, x, y, :, cols], lin[z, x, y, :, cols]
                        pd, ld = dirg[y, z, x, :, cols], diru[y, z, x, :, cols]
                        b = back[x, y, z, :, cols]
                        s = jax.nn.sigmoid(p)
                        one = s * (1.0 + p * (1.0 - s))
                        two = s * (1.0 - s) * (2.0 + p * (1.0 - 2.0 * s))
                        part[dz, dx, dy] = (b * (ld * one + l * two * pd), b * one * pd)

            def put(a, hi, lo, inner, pair):
                at_row = pl.multiple_of(128 * hi + 32 * lo + 16 * inner, 16)
                for which in range(2):
                    value = jnp.concatenate([v[which] for v in pair], axis=0).astype(BF)
                    parts[a, which, pl.ds(at_row, 16), cols] = value

            for u in range(2):
                for w in range(2):
                    put(0, 2 * zp + u, 2 * xp + w, yp, (part[u, w, 0], part[u, w, 1]))
                    put(1, 2 * yp + u, 2 * zp + w, xp, (part[w, 0, u], part[w, 1, u]))
                    put(2, 2 * xp + u, 2 * yp + w, zp, (part[0, u, w], part[1, u, w]))

    replied = []

    def reply(j):
        for a in range(3):
            f0, f = SPANS[a]
            out = replies[a]
            if j == 1:
                wire.sent(fourth[a][0][0], out.at[pl.ds(0, 3)])
                replied[a].wait()
            done = 0
            while done < f:
                n = min(256, f - done)
                rows = pl.ds(f0 + done, n)
                got = lax.dot_general(parts[a, 0], wg[j, rows, :], NT, preferred_element_type=F32)
                got += lax.dot_general(parts[a, 1], wu[j, rows, :], NT, preferred_element_type=F32)
                out[:, :, :, done : done + n] = got.astype(BF).reshape(4, 4, 32, n)
                done += n
            n3, dim = place.at[ORDERS[a][2]], ORDERS[a][2]
            sent, early, late = fourth[a][j]
            far = mod4(n3 + 2)
            wire.go(sent, early, out.at[far, pl.ds(0, 2)], passing[a].at[j, 0], dim, 1)
            wire.go(sent, early, out.at[far, pl.ds(2, 2)], passing[a].at[j, 1], dim, 3)
            wire.go(sent, late, out.at[mod4(n3 + 1)], backs[a].at[:, n3, j], dim, 1)
            wire.go(sent, late, out.at[mod4(n3 + 3)], backs[a].at[:, n3, j], dim, 3)
            replied.append(copy(out.at[n3], backs[a].at[:, n3, j], 29 + 3 * j + a))

    def replays(j):
        for a in range(3):
            n3, dim = place.at[ORDERS[a][2]], ORDERS[a][2]
            hold = passing[a]
            _, early, late = fourth[a][j]
            wire.got(early, hold.at[j])
            wire.go(repassed[a], late, hold.at[j, 0], backs[a].at[pl.ds(0, 2), mod4(n3 + 3), j], dim, 1)
            wire.go(repassed[a], late, hold.at[j, 1], backs[a].at[pl.ds(2, 2), mod4(n3 + 1), j], dim, 3)

    for a in range(3):
        wire.got(mk2[a][1], meta.at[a, pl.ds(0, 3)])
    for b in (1, 2):
        for a in range(3):
            pass_on(a, ORDERS[a][1], second[a][b], *views2(a, b))
            weigh(a, 2 * b - 2)
            weigh(a, 2 * b - 1)
        if b == 1:
            pack(0)
    for a in range(3):
        pass_on(a, ORDERS[a][1], second[a][3], *views2(a, 3))
    for a in range(3):
        wire.got(second[a][0][2], held.at[a, 0])
    pack(1)
    direct(0)
    relays(0)
    pack(2)
    direct(1)
    relays(1)
    for a in range(3):
        wire.got(second[a][0][3], held.at[a, 0])
    pack(3)
    direct(2)
    relays(2)
    for c in heavy:
        c.wait()
    fetch(0)
    pack(4)
    direct(3)
    relays(3)
    fetch(1)
    layer(0, (0, 1, 2))
    pack(5)
    direct(4)
    relays(4)
    fetch(2)
    fetch(3)
    layer(2, (0,))
    pack(6)
    direct(5)
    relays(5)
    layer(2, (1, 2))
    pack(7)
    direct(6)
    relays(6)
    mix()
    direct(7)
    relays(7)
    fetch(4)
    fetch(5)
    layer(4, (0, 1, 2))
    reply(0)
    fetch(6)
    fetch(7)
    replays(0)
    layer(6, (0, 1, 2))
    mix()
    reply(1)
    replays(1)
    for a in range(3):
        for j in range(2):
            wire.got(fourth[a][j][2], backs[a].at[pl.ds(0, 3), :, j])
        wire.sent(first[a][4], held.at[a, 0, pl.ds(0, 3)])
        wire.sent(second[a][0][4], held.at[a, pl.ds(0, 3)])
        wire.sent(mk1[a][0], meta.at[a, 0, pl.ds(0, 3)])
        wire.sent(mk2[a][0], meta.at[a, pl.ds(0, 3)])
        for s in (5, 6, 7):
            wire.sent(third[a][s][0], packed.at[a, 0, pl.ds(0, 3)])
        wire.sent(passed[a], relay.at[a])
        wire.sent(fourth[a][1][0], replies[a].at[pl.ds(0, 3)])
        wire.sent(repassed[a], passing[a])
    for c in replied[3:] + stored[-2:]:
        c.wait()


N_GROUPS, N_TAKEN, N_LOCAL = 6 + 6 + 30 + 6, 42 + 6 + 48 + 12, 35
SPANS = ((0, 768), (768, 640), (1408, 640))


def dispatch(tok, tan, adj, ids, gates, wg, wu, wd):
    vmem = pl.BlockSpec(memory_space=pltpu.VMEM)
    hbm = pl.BlockSpec(memory_space=pl.ANY)
    rows = jax.ShapeDtypeStruct((2, 4, 4, 32, D), BF)
    out = pl.pallas_call(
        dispatch_kernel,
        out_shape=(rows, rows, rows)
        + tuple(jax.ShapeDtypeStruct((4, 4, 2, 32, f), BF) for _, f in SPANS)
        + (jax.ShapeDtypeStruct((3, 4, 2, 256, 256), BF),),
        in_specs=[hbm] * 3 + [vmem] * 2 + [hbm] * 3,
        out_specs=(hbm,) * 7,
        scratch_shapes=[
            pltpu.VMEM((3, 4, 4, TOK, D), BF),
            pltpu.VMEM((3, 3, 4, 32, D), BF),
            pltpu.VMEM((3, 8, 2, 16, D), BF),
            pltpu.VMEM((3, 4, 4, 8, 128), F32),
            pltpu.VMEM((3, 4, 4, 32, D), BF),
            pltpu.VMEM((2, D, FF), BF),
            pltpu.VMEM((2, D, FF), BF),
            pltpu.VMEM((2, FF, D), BF),
        ]
        + [pltpu.VMEM((4, 4, 4, 8, FF), F32)] * 5
        + [pltpu.VMEM((3, 2, 512, FF), BF)]
        + [pltpu.VMEM((4, 4, 32, f), BF) for _, f in SPANS]
        + [pltpu.VMEM((2, 2, 2, 32, f), BF) for _, f in SPANS]
        + [
            pltpu.VMEM((3, 4, 2, 128, 256), BF),
            pltpu.VMEM((256, 256), F32),
            pltpu.VMEM((2, 2, 256, 256), BF),
            pltpu.SemaphoreType.DMA((N_GROUPS,)),
            pltpu.SemaphoreType.DMA((N_TAKEN,)),
            pltpu.SemaphoreType.DMA((N_LOCAL,)),
        ],
        compiler_params=pltpu.CompilerParams(
            collective_id=1, has_side_effects=True, vmem_limit_bytes=67043328
        ),
        name="dispatch",
    )(tok, tan, adj, ids, gates, wg, wu, wd)
    return out[3:]


def collect_kernel(b0, b1, b2, grown_in, tan, hvp, ratio, *scratch):
    place = Place()
    n_part = 8
    parts = [scratch[i * n_part : (i + 1) * n_part] for i in range(9)]
    grown, plane, line, send, recv, local = scratch[9 * n_part :]
    wire = Wire(place, send, recv)
    spots = iter(range(12))
    backs = (b0, b1, b2)

    def copy(src, dst):
        c = pltpu.make_async_copy(src, dst, local.at[next(spots)])
        c.start()
        return c

    loads = {}
    for q in range(3):
        for a, f0, n in PARTS[q]:
            loads[q, a] = copy(backs[a].at[:, :, :, pl.ds(f0 - SPANS[a][0], n)], parts[3 * q + a][0])
            if q == 0:
                loads[a] = copy(grown_in.at[a], grown.at[a])
    y, x, z = place.at
    near = [(place.dp, lax.rem(y + i // 4, 4) * 16 + lax.rem(x + i % 4, 4) * 4 + z) for i in range(1, 16)]
    tall = [(lax.rem(place.dp + i // 4, 2), place.shifted(2, i % 4)) for i in range(1, 8)]
    sem = pltpu.get_barrier_semaphore()
    for other in near + tall:
        pl.semaphore_signal(sem, inc=1, device_id=other, device_id_type=MESH)
    pl.semaphore_wait(sem, 22)
    keys = [[[wire.group(), wire.group()] + [wire.take() for _ in range(6)] for _ in range(3)] for _ in range(3)]
    at = [tuple(place.at[d] for d in ORDERS[a]) for a in range(3)]
    state = {"square": jnp.zeros((8, 128), F32)}

    def total(q, a, r):
        n = PARTS[q][a][2]
        rows = parts[3 * q + a][0][mod4(at[a][1] + r)].reshape(256, n)
        got = jnp.dot(grown[a, r, 0], rows, preferred_element_type=F32)
        got = got + jnp.dot(grown[a, r, 1], rows, preferred_element_type=F32)
        return got.reshape(4, 64, n)

    def far2(q):
        for a, _, n in PARTS[q]:
            own, out2, mid2 = parts[3 * q + a][1:4]
            dim = ORDERS[a][1]
            k = keys[q][a]
            loads[q, a].wait()
            if q == 0:
                loads[a].wait()
            out2[...] = total(q, a, 2).astype(BF)
            wire.go(k[0], k[2], out2.at[pl.ds(0, 2)], mid2.at[0], dim, 1)
            wire.go(k[0], k[3], out2.at[pl.ds(2, 2)], mid2.at[1], dim, 3)
        for a, _, n in PARTS[q]:
            parts[3 * q + a][1][...] = total(q, a, 0)

    def near2(q):
        for a, _, n in PARTS[q]:
            mid2, to2, in2 = parts[3 * q + a][3:6]
            k, dim = keys[q][a], ORDERS[a][1]
            for side, r in ((0, 1), (1, 3)):
                got = total(q, a, r)
                wire.got(k[2 + side], mid2.at[side])
                came = mid2[side].astype(F32)
                lo, hi = got[0:2], got[2:4]
                if side == 0:
                    lo = lo + came
                else:
                    hi = hi + came
                to2[side, 0:2] = lo.astype(BF)
                to2[side, 2:4] = hi.astype(BF)
                wire.go(k[0], k[4], to2.at[side], in2.at[side], dim, r)

    def far1(q):
        for a, _, n in PARTS[q]:
            own, in2, out1, mid1 = (parts[3 * q + a][i] for i in (1, 5, 6, 7))
            n1, dim = at[a][0], ORDERS[a][0]
            k = keys[q][a]
            wire.got(k[4], in2)
            own[...] = own[...] + (in2[0].astype(F32) + in2[1].astype(F32))
            out1[0] = own[mod4(n1 + 2)].astype(BF)
            wire.go(k[1], k[5], out1.at[0, pl.ds(0, 32)], mid1.at[0, pl.ds(0, 32)], dim, 1)
            wire.go(k[1], k[6], out1.at[0, pl.ds(32, 32)], mid1.at[0, pl.ds(32, 32)], dim, 3)

    def near1(q):
        for a, _, n in PARTS[q]:
            own, in2, out1, mid1 = (parts[3 * q + a][i] for i in (1, 5, 6, 7))
            n1, dim = at[a][0], ORDERS[a][0]
            k = keys[q][a]
            for side, r in ((0, 1), (1, 3)):
                rows = pl.ds(32 * side, 32)
                rest = pl.ds(32 - 32 * side, 32)
                wire.got(k[5 + side], mid1.at[0, rows])
                s = mod4(n1 + r)
                out1[1 + side, rows] = (own[s, rows] + mid1[0, rows].astype(F32)).astype(BF)
                out1[1 + side, rest] = own[s, rest].astype(BF)
                wire.go(k[1], k[7], out1.at[1 + side], mid1.at[1 + side], dim, r)

    def finish(q):
        for a, f0, n in PARTS[q]:
            own, mid1 = parts[3 * q + a][1], parts[3 * q + a][7]
            k = keys[q][a]
            wire.got(k[7], mid1.at[pl.ds(1, 2)])
            got = own[at[a][0]] + (mid1[1].astype(F32) + mid1[2].astype(F32))
            hvp[:, f0 : f0 + n] = got
            state["square"] += jnp.sum((got * got).reshape(8, 8, n // 128, 128), axis=(0, 2))

    far2(0)
    far2(1)
    near2(0)
    far2(2)
    far1(0)
    near2(1)
    near1(0)
    t = tan[...].astype(F32)
    low = jnp.sum((t * t).reshape(8, 8, 16, 128), axis=(0, 2))
    far1(1)
    near2(2)
    finish(0)
    near1(1)
    far1(2)
    finish(1)
    near1(2)
    finish(2)

    def share(table, value, spot, others):
        table[spot, 0] = value[0]
        table[spot, 1] = value[1]
        sent, came = wire.group(), wire.take()
        for other in others:
            wire.push(sent, came, table.at[spot], table.at[spot], other)
        wire.got(came, table.at[pl.ds(0, len(others))])
        wire.sent(sent, table.at[pl.ds(0, len(others))])
        return jnp.sum(table[...], axis=0)

    full = share(plane, (state["square"], low), y * 4 + x, near)
    full = share(line, (full[0], full[1]), place.dp * 4 + z, tall)
    top, low = jnp.sum(full[0]), jnp.sum(full[1])
    ratio[...] = jnp.full((8, 128), top, F32) / jnp.full((8, 128), low, F32)
    for q in range(3):
        for a in range(3):
            back, _, _, _, _, _, out1, _ = parts[3 * q + a]
            wire.sent(keys[q][a][0], back.at[pl.ds(0, 3)])
            wire.sent(keys[q][a][1], out1)


N_SENT, N_CAME = 18 + 2, 54 + 2


def collect(backs, grown, tan):
    vmem = pl.BlockSpec(memory_space=pltpu.VMEM)
    hbm = pl.BlockSpec(memory_space=pl.ANY)
    scratch = []
    for q in range(3):
        for _, _, f in PARTS[q]:
            scratch += [
                pltpu.VMEM((4, 4, 64, f), BF),
                pltpu.VMEM((4, 64, f), F32),
                pltpu.VMEM((4, 64, f), BF),
                pltpu.VMEM((2, 2, 64, f), BF),
                pltpu.VMEM((2, 4, 64, f), BF),
                pltpu.VMEM((2, 4, 64, f), BF),
                pltpu.VMEM((3, 64, f), BF),
                pltpu.VMEM((3, 64, f), BF),
            ]
    scratch += [
        pltpu.VMEM((3, 4, 2, 256, 256), BF),
        pltpu.VMEM((16, 2, 8, 128), F32),
        pltpu.VMEM((8, 2, 8, 128), F32),
        pltpu.SemaphoreType.DMA((N_SENT,)),
        pltpu.SemaphoreType.DMA((N_CAME,)),
        pltpu.SemaphoreType.DMA((12,)),
    ]
    return pl.pallas_call(
        collect_kernel,
        out_shape=(jax.ShapeDtypeStruct((TOK, D), F32), jax.ShapeDtypeStruct((8, 128), F32)),
        in_specs=[hbm] * 4 + [vmem],
        out_specs=(vmem, vmem),
        scratch_shapes=scratch,
        compiler_params=pltpu.CompilerParams(
            collective_id=2, has_side_effects=True, vmem_limit_bytes=67043328
        ),
        name="collect",
    )(*backs, grown, tan)


def local(tokens, tangent, adjoint, gates, expert_ids, w_gate, w_up, w_down):
    *backs, grown = dispatch(tokens, tangent, adjoint, expert_ids.T, gates.T, w_gate, w_up, w_down)
    backs = [b.reshape(4, 4, 64, b.shape[-1]) for b in backs]
    hvp, ratio = collect(backs, grown, tangent)
    return hvp, ratio[0, 0]


def solution(mesh):
    rows = P(("dp", "expert"), None)
    weights = P("expert", None, None)
    return jax.shard_map(
        local,
        mesh=mesh,
        in_specs=(rows,) * 5 + (weights,) * 3,
        out_specs=(rows, P()),
        check_vma=False,
    )
```

```python
import functools

import jax
import jax.numpy as jnp
from jax import lax
from jax.experimental import pallas as pl
from jax.experimental.pallas import tpu as pltpu
from jax.sharding import PartitionSpec as P

MESH = pl.DeviceIdType.MESH
STRIDE = (16, 4, 1)
ORDERS = ((0, 1, 2), (1, 2, 0), (2, 0, 1))
PARTS = (
    ((0, 0, 256), (1, 768, 256), (2, 1408, 256)),
    ((0, 256, 256), (1, 1024, 256), (2, 1664, 256)),
    ((0, 512, 256), (1, 1280, 128), (2, 1920, 128)),
)
TOK, D, FF, R = 64, 2048, 768, 4
BF, F32 = jnp.bfloat16, jnp.float32


class Place:
    def __init__(self):
        self.me = lax.axis_index("expert")
        self.dp = lax.axis_index("dp")
        self.at = (self.me // 16, (self.me // 4) % 4, self.me % 4)

    def shifted(self, dim, by):
        c = self.at[dim]
        return self.me + (lax.rem(c + by, 4) - c) * STRIDE[dim]


def barrier(place):
    sem = pltpu.get_barrier_semaphore()
    for dim in range(3):
        for by in (1, 2, 3):
            pl.semaphore_signal(
                sem, inc=1, device_id=(place.dp, place.shifted(dim, by)), device_id_type=MESH
            )
    pl.semaphore_wait(sem, 9)


class Wire:
    def __init__(self, place, send, recv):
        self.place, self.send, self.recv, self.groups, self.taken = place, send, recv, 0, 0

    def group(self):
        self.groups += 1
        return self.groups - 1

    def take(self):
        self.taken += 1
        return self.taken - 1

    def _copy(self, sent, came, src, dst, target):
        return pltpu.make_async_remote_copy(
            src_ref=src, dst_ref=dst, send_sem=self.send.at[sent], recv_sem=self.recv.at[came],
            device_id=target, device_id_type=MESH,
        )

    def push(self, sent, came, src, dst, target):
        self._copy(sent, came, src, dst, target).start()

    def go(self, sent, came, src, dst, dim, by):
        self.push(sent, came, src, dst, (self.place.dp, self.place.shifted(dim, by)))

    def got(self, came, view):
        self._copy(0, came, view, view, (self.place.dp, self.place.shifted(0, 1))).wait_recv()

    def sent(self, group, view):
        self._copy(group, 0, view, view, (self.place.dp, self.place.shifted(0, 1))).wait_send()


def mod4(v):
    return lax.rem(v, 4)


def column_terms(meta, a, s2, place):
    dim = ORDERS[a][2]
    blocks = [meta[a, s2, s] for s in range(4)]
    low = lax.broadcasted_iota(jnp.int32, (8, 128), 1) < 64
    turn = [pltpu.roll(b, 64, 1) for b in blocks]
    ids = jnp.concatenate([jnp.where(low, blocks[0], turn[1]), jnp.where(low, blocks[2], turn[3])], axis=1)
    gates = jnp.concatenate([jnp.where(low, turn[0], blocks[1]), jnp.where(low, turn[2], blocks[3])], axis=1)
    row = lax.broadcasted_iota(jnp.int32, (8, 256), 0)
    named = jnp.zeros((8, 256), F32)
    weight = jnp.zeros((8, 256), F32)
    for r in range(8):
        e = 2 * (place.me + (r // 2 - place.at[dim]) * STRIDE[dim]) + r % 2
        hit = ids == e.astype(F32)
        n = jnp.sum(jnp.where(hit, 1.0, 0.0), axis=0, keepdims=True)
        g = jnp.sum(jnp.where(hit, gates, 0.0), axis=0, keepdims=True)
        named = jnp.where(row == r, n, named)
        weight = jnp.where(row == r, g, weight)
    i = lax.broadcasted_iota(jnp.int32, (256, 256), 0)
    l = lax.broadcasted_iota(jnp.int32, (256, 256), 1)
    upper = jnp.where((i // 64 == l // 64) & (i < l), 1.0, 0.0).astype(BF)
    before = jnp.dot(named.astype(BF), upper, preferred_element_type=F32)
    base = (lax.broadcasted_iota(jnp.int32, (8, 256), 1) // 64 * 8).astype(F32)
    return jnp.where(named > 0.5, base + before, -1.0), weight


NT = (((1,), (1,)), ((), ()))


def dispatch_kernel(tok, tan, adj, ids, gates, wg_in, wu_in, wd_in,
                    r0, r1, r2, b0, b1, b2, grown,
                    held, packed, relay, meta, chunk, wg, wu, wd, pre, lin, dirg, diru, back, parts,
                    o0, o1, o2, q0, q1, q2, picks, spin, grow, send, recv, local):
    place = Place()
    wire = Wire(place, send, recv)
    outs, backs, replies, passing = (r0, r1, r2), (b0, b1, b2), (o0, o1, o2), (q0, q1, q2)
    at = [(place.at[ORDERS[a][1]], place.at[ORDERS[a][0]]) for a in range(3)]

    def copy(src, dst, spot):
        c = pltpu.make_async_copy(src, dst, local.at[spot])
        c.start()
        return c

    own = [copy(src, held.at[a, at[a][0], at[a][1]], a) for a, src in enumerate((tok, tan, adj))]
    heavy = [copy(wg_in, wg, 3), copy(wu_in, wu, 4), copy(wd_in, wd, 5)]
    turned = jnp.concatenate([ids[...].astype(F32), gates[...]], axis=1)
    for a in range(3):
        meta[a, at[a][0], at[a][1]] = turned
    barrier(place)
    for c in own:
        c.wait()

    def half(a, s2, s1, h):
        return held.at[a, s2, s1, pl.ds(32 * h, 32)]

    def spread(a, dim, at2, at1, keys):
        plus, minus, rest, _, sent = keys
        wire.go(sent, plus, half(a, at2, at1, 0), half(a, at2, at1, 0), dim, 1)
        wire.go(sent, minus, half(a, at2, at1, 1), half(a, at2, at1, 1), dim, 3)
        wire.go(sent, rest, half(a, at2, at1, 1), half(a, at2, at1, 1), dim, 1)
        wire.go(sent, rest, half(a, at2, at1, 0), half(a, at2, at1, 0), dim, 3)

    first, second = [], []
    for a in range(3):
        sent = wire.group()
        first.append((wire.take(), wire.take(), wire.take(), wire.take(), sent))
        sent, rest_key, far_key = wire.group(), wire.take(), wire.take()
        second.append([(wire.take(), wire.take(), rest_key, far_key, sent) for _ in range(4)])
    rel1 = (0, 3, 1, 2)

    mk1 = [(wire.group(), wire.take()) for _ in range(3)]
    mk2 = [(wire.group(), wire.take()) for _ in range(3)]
    for a in range(3):
        n2, n1 = at[a]
        for by in (1, 2, 3):
            wire.go(*mk1[a], meta.at[a, n2, n1], meta.at[a, n2, n1], ORDERS[a][0], by)
    for a in range(3):
        n2, n1 = at[a]
        spread(a, ORDERS[a][0], n2, n1, first[a])
    for a in range(3):
        n2, n1 = at[a]
        spread(a, ORDERS[a][1], n2, n1, second[a][0])
    for a in range(3):
        n2, n1 = at[a]
        wire.got(mk1[a][1], meta.at[a, n2, pl.ds(0, 3)])
        for by in (1, 2, 3):
            wire.go(*mk2[a], meta.at[a, n2], meta.at[a, n2], ORDERS[a][1], by)

    def pass_on(a, dim, keys, minus, plus):
        from_minus, from_plus, _, far, sent = keys
        wire.got(from_minus, minus(0))
        wire.go(sent, far, minus(0), minus(0), dim, 1)
        wire.got(from_plus, plus(1))
        wire.go(sent, far, plus(1), plus(1), dim, 3)

    def views1(a):
        n2, n1 = at[a]
        return (lambda h: half(a, n2, mod4(n1 + 3), h)), (lambda h: half(a, n2, mod4(n1 + 1), h))

    def views2(a, b):
        n2, n1 = at[a]
        s1 = mod4(n1 + rel1[b])
        return (lambda h: half(a, mod4(n2 + 3), s1, h)), (lambda h: half(a, mod4(n2 + 1), s1, h))

    for a in range(3):
        pass_on(a, ORDERS[a][0], first[a], *views1(a))
    for a in range(3):
        n2, n1 = at[a]
        wire.got(first[a][2], held.at[a, n2, mod4(n1 + 1)])
        for b in (1, 2):
            spread(a, ORDERS[a][1], n2, mod4(n1 + rel1[b]), second[a][b])
    for a in range(3):
        pass_on(a, ORDERS[a][1], second[a][0], *views2(a, 0))
    for a in range(3):
        n2, n1 = at[a]
        wire.got(first[a][3], held.at[a, n2, mod4(n1 + 2)])
        spread(a, ORDERS[a][1], n2, mod4(n1 + 2), second[a][3])

    slots = lax.broadcasted_iota(jnp.int32, (32, 256), 0).astype(F32)
    stored = []

    def weigh(a, r):
        index, weight = column_terms(meta, a, mod4(at[a][0] + r), place)
        for e in range(8):
            spin[pl.ds(32 * e, 32), :] = jnp.where(index[e : e + 1, :] == slots, weight[e : e + 1, :], 0.0)
        w = spin[...].T
        for e in range(8):
            hit = jnp.where(index[e : e + 1, :] == slots, 1.0, 0.0)
            picks[a, r, e % 2, pl.ds(32 * (e // 2), 32), :] = hit.astype(BF)
        n = len(stored)
        if n >= 2:
            stored[n - 2].wait()
        grow[n % 2] = w.astype(BF)
        stored.append(copy(grow.at[n % 2], grown.at[a, r], 6 + n % 2))

    third = [[(wire.group(), wire.take(), wire.take()) for _ in range(8)] for _ in range(3)]
    fourth = [[(wire.group(), wire.take(), wire.take()) for _ in range(2)] for _ in range(3)]
    passed = [wire.group() for _ in range(3)]
    repassed = [wire.group() for _ in range(3)]
    kept = {}
    rels = (0, 1, 3, 2)

    def where(a, s):
        dim = ORDERS[a][2]
        return s // 4, place.at[dim], mod4(at[a][0] + rels[s % 4]), dim

    def settle(a, s):
        c = kept.pop((a, s), None)
        if c is not None:
            c.wait()

    def pack(s):
        for a in range(3):
            j, n3, s2, dim = where(a, s)
            buf = s % 3
            chosen = picks[a, rels[s % 4], j]
            if s >= 3:
                wire.sent(third[a][s - 3][0], packed.at[a, buf, pl.ds(0, 3)])
                settle(a, s - 3)

            @pl.loop(0, 4)
            def _(n):
                cols = pl.ds(pl.multiple_of(n * 512, 512), 512)
                rows = held[a, s2, :, :, cols].reshape(256, 512)
                got = jnp.dot(chosen, rows, preferred_element_type=F32).astype(BF)
                packed[a, buf, :, :, cols] = got.reshape(4, 32, 512)

            sent, early, _ = third[a][s]
            far = mod4(n3 + 2)
            wire.go(sent, early, packed.at[a, buf, far, pl.ds(0, 16)], relay.at[a, s, 0], dim, 1)
            wire.go(sent, early, packed.at[a, buf, far, pl.ds(16, 16)], relay.at[a, s, 1], dim, 3)

    def direct(s):
        for a in range(3):
            j, n3, s2, dim = where(a, s)
            buf = s % 3
            sent, _, late = third[a][s]
            wire.go(sent, late, packed.at[a, buf, mod4(n3 + 1)], outs[a].at[j, n3, s2], dim, 1)
            wire.go(sent, late, packed.at[a, buf, mod4(n3 + 3)], outs[a].at[j, n3, s2], dim, 3)
            kept[a, s] = copy(packed.at[a, buf, n3], outs[a].at[j, n3, s2], 8 + 3 * a + buf)

    def relays(s):
        for a in range(3):
            j, n3, s2, dim = where(a, s)
            _, early, late = third[a][s]
            sent = passed[a]
            wire.got(early, relay.at[a, s])
            wire.go(sent, late, relay.at[a, s, 0], outs[a].at[j, mod4(n3 + 3), s2, pl.ds(0, 16)], dim, 1)
            wire.go(sent, late, relay.at[a, s, 1], outs[a].at[j, mod4(n3 + 1), s2, pl.ds(16, 16)], dim, 3)

    loads = {}

    def fetch(s):
        for a in range(3):
            j, n3, s2, dim = where(a, s)
            wire.got(third[a][s][2], outs[a].at[j, pl.ds(0, 3), s2])
            settle(a, s)
            loads[a, s] = copy(outs[a].at[j, :, s2], chunk.at[a, s % 4], 17 + 4 * a + s % 4)

    def layer(s, stages):
        j, half2 = s // 4, s % 4
        for a in range(3):
            if 0 in stages:
                loads[a, s].wait()
                loads[a, s + 1].wait()
            spots2 = [where(a, s + i)[2] for i in range(2)]

            @pl.loop(min(stages), max(stages) + 1)
            def _(n):
                cols = pl.ds(pl.multiple_of(n * 256, 256), 256)
                rows = chunk[a, half2 : half2 + 2].reshape(256, D)

                def put(ref, value):
                    value = value.reshape(2, 4, 4, 8, 256)
                    for i in range(2):
                        ref[:, spots2[i], :, :, cols] = value[i]

                if a == 2:
                    put(back, lax.dot_general(rows, wd[j, cols, :], NT, preferred_element_type=F32))
                else:
                    x, y = (pre, lin) if a == 0 else (dirg, diru)
                    put(x, jnp.dot(rows, wg[j, :, cols], preferred_element_type=F32))
                    put(y, jnp.dot(rows, wu[j, :, cols], preferred_element_type=F32))

    def mix():
        @pl.loop(0, 24)
        def _(i):
            n, q = i % 3, i // 3
            zp, xp, yp = q // 4, (q // 2) % 2, q % 2
            cols = pl.ds(pl.multiple_of(n * 256, 256), 256)
            part = {}
            for dz in range(2):
                for dx in range(2):
                    for dy in range(2):
                        z, x, y = 2 * zp + dz, 2 * xp + dx, 2 * yp + dy
                        p, l = pre[z, x, y, :, cols], lin[z, x, y, :, cols]
                        pd, ld = dirg[y, z, x, :, cols], diru[y, z, x, :, cols]
                        b = back[x, y, z, :, cols]
                        s = jax.nn.sigmoid(p)
                        one = s * (1.0 + p * (1.0 - s))
                        two = s * (1.0 - s) * (2.0 + p * (1.0 - 2.0 * s))
                        part[dz, dx, dy] = (b * (ld * one + l * two * pd), b * one * pd)

            def put(a, hi, lo, inner, pair):
                at_row = pl.multiple_of(128 * hi + 32 * lo + 16 * inner, 16)
                for which in range(2):
                    value = jnp.concatenate([v[which] for v in pair], axis=0).astype(BF)
                    parts[a, which, pl.ds(at_row, 16), cols] = value

            for u in range(2):
                for w in range(2):
                    put(0, 2 * zp + u, 2 * xp + w, yp, (part[u, w, 0], part[u, w, 1]))
                    put(1, 2 * yp + u, 2 * zp + w, xp, (part[w, 0, u], part[w, 1, u]))
                    put(2, 2 * xp + u, 2 * yp + w, zp, (part[0, u, w], part[1, u, w]))

    replied = []

    def reply(j):
        for a in range(3):
            f0, f = SPANS[a]
            out = replies[a]
            if j == 1:
                wire.sent(fourth[a][0][0], out.at[pl.ds(0, 3)])
                replied[a].wait()
            done = 0
            while done < f:
                n = min(256, f - done)
                rows = pl.ds(f0 + done, n)
                got = lax.dot_general(parts[a, 0], wg[j, rows, :], NT, preferred_element_type=F32)
                got += lax.dot_general(parts[a, 1], wu[j, rows, :], NT, preferred_element_type=F32)
                out[:, :, :, done : done + n] = got.astype(BF).reshape(4, 4, 32, n)
                done += n
            n3, dim = place.at[ORDERS[a][2]], ORDERS[a][2]
            sent, early, late = fourth[a][j]
            far = mod4(n3 + 2)
            wire.go(sent, early, out.at[far, pl.ds(0, 2)], passing[a].at[j, 0], dim, 1)
            wire.go(sent, early, out.at[far, pl.ds(2, 2)], passing[a].at[j, 1], dim, 3)
            wire.go(sent, late, out.at[mod4(n3 + 1)], backs[a].at[:, n3, j], dim, 1)
            wire.go(sent, late, out.at[mod4(n3 + 3)], backs[a].at[:, n3, j], dim, 3)
            replied.append(copy(out.at[n3], backs[a].at[:, n3, j], 29 + 3 * j + a))

    def replays(j):
        for a in range(3):
            n3, dim = place.at[ORDERS[a][2]], ORDERS[a][2]
            hold = passing[a]
            _, early, late = fourth[a][j]
            wire.got(early, hold.at[j])
            wire.go(repassed[a], late, hold.at[j, 0], backs[a].at[pl.ds(0, 2), mod4(n3 + 3), j], dim, 1)
            wire.go(repassed[a], late, hold.at[j, 1], backs[a].at[pl.ds(2, 2), mod4(n3 + 1), j], dim, 3)

    for a in range(3):
        wire.got(mk2[a][1], meta.at[a, pl.ds(0, 3)])
    for b in (1, 2):
        for a in range(3):
            pass_on(a, ORDERS[a][1], second[a][b], *views2(a, b))
            weigh(a, 2 * b - 2)
            weigh(a, 2 * b - 1)
        if b == 1:
            pack(0)
    for a in range(3):
        pass_on(a, ORDERS[a][1], second[a][3], *views2(a, 3))
    for a in range(3):
        wire.got(second[a][0][2], held.at[a, 0])
    pack(1)
    direct(0)
    relays(0)
    pack(2)
    direct(1)
    relays(1)
    for a in range(3):
        wire.got(second[a][0][3], held.at[a, 0])
    pack(3)
    direct(2)
    relays(2)
    for c in heavy:
        c.wait()
    pack(4)
    direct(3)
    relays(3)
    fetch(0)
    pack(5)
    direct(4)
    relays(4)
    fetch(1)
    layer(0, (0, 1, 2))
    pack(6)
    direct(5)
    relays(5)
    fetch(2)
    fetch(3)
    layer(2, (0, 1, 2))
    pack(7)
    direct(6)
    relays(6)
    direct(7)
    mix()
    relays(7)
    fetch(4)
    fetch(5)
    layer(4, (0, 1, 2))
    reply(0)
    fetch(6)
    fetch(7)
    replays(0)
    layer(6, (0, 1, 2))
    mix()
    reply(1)
    replays(1)
    for a in range(3):
        for j in range(2):
            wire.got(fourth[a][j][2], backs[a].at[pl.ds(0, 3), :, j])
        wire.sent(first[a][4], held.at[a, 0, pl.ds(0, 3)])
        wire.sent(second[a][0][4], held.at[a, pl.ds(0, 3)])
        wire.sent(mk1[a][0], meta.at[a, 0, pl.ds(0, 3)])
        wire.sent(mk2[a][0], meta.at[a, pl.ds(0, 3)])
        for s in (5, 6, 7):
            wire.sent(third[a][s][0], packed.at[a, 0, pl.ds(0, 3)])
        wire.sent(passed[a], relay.at[a])
        wire.sent(fourth[a][1][0], replies[a].at[pl.ds(0, 3)])
        wire.sent(repassed[a], passing[a])
    for c in replied[3:] + stored[-2:]:
        c.wait()


N_GROUPS, N_TAKEN, N_LOCAL = 6 + 6 + 30 + 6, 42 + 6 + 48 + 12, 35
SPANS = ((0, 768), (768, 640), (1408, 640))


def dispatch(tok, tan, adj, ids, gates, wg, wu, wd):
    vmem = pl.BlockSpec(memory_space=pltpu.VMEM)
    hbm = pl.BlockSpec(memory_space=pl.ANY)
    rows = jax.ShapeDtypeStruct((2, 4, 4, 32, D), BF)
    out = pl.pallas_call(
        dispatch_kernel,
        out_shape=(rows, rows, rows)
        + tuple(jax.ShapeDtypeStruct((4, 4, 2, 32, f), BF) for _, f in SPANS)
        + (jax.ShapeDtypeStruct((3, 4, 256, 256), BF),),
        in_specs=[hbm] * 3 + [vmem] * 2 + [hbm] * 3,
        out_specs=(hbm,) * 7,
        scratch_shapes=[
            pltpu.VMEM((3, 4, 4, TOK, D), BF),
            pltpu.VMEM((3, 3, 4, 32, D), BF),
            pltpu.VMEM((3, 8, 2, 16, D), BF),
            pltpu.VMEM((3, 4, 4, 8, 128), F32),
            pltpu.VMEM((3, 4, 4, 32, D), BF),
            pltpu.VMEM((2, D, FF), BF),
            pltpu.VMEM((2, D, FF), BF),
            pltpu.VMEM((2, FF, D), BF),
        ]
        + [pltpu.VMEM((4, 4, 4, 8, FF), F32)] * 5
        + [pltpu.VMEM((3, 2, 512, FF), BF)]
        + [pltpu.VMEM((4, 4, 32, f), BF) for _, f in SPANS]
        + [pltpu.VMEM((2, 2, 2, 32, f), BF) for _, f in SPANS]
        + [
            pltpu.VMEM((3, 4, 2, 128, 256), BF),
            pltpu.VMEM((256, 256), F32),
            pltpu.VMEM((2, 256, 256), BF),
            pltpu.SemaphoreType.DMA((N_GROUPS,)),
            pltpu.SemaphoreType.DMA((N_TAKEN,)),
            pltpu.SemaphoreType.DMA((N_LOCAL,)),
        ],
        compiler_params=pltpu.CompilerParams(
            collective_id=1, has_side_effects=True, vmem_limit_bytes=67043328
        ),
        name="dispatch",
    )(tok, tan, adj, ids, gates, wg, wu, wd)
    return out[3:]


def collect_kernel(b0, b1, b2, grown_in, tan, hvp, ratio, *scratch):
    place = Place()
    n_part = 8
    parts = [scratch[i * n_part : (i + 1) * n_part] for i in range(9)]
    grown, plane, line, send, recv, local = scratch[9 * n_part :]
    wire = Wire(place, send, recv)
    spots = iter(range(12))
    backs = (b0, b1, b2)

    def copy(src, dst):
        c = pltpu.make_async_copy(src, dst, local.at[next(spots)])
        c.start()
        return c

    loads = {}
    for q in range(3):
        for a, f0, n in PARTS[q]:
            loads[q, a] = copy(backs[a].at[:, :, :, pl.ds(f0 - SPANS[a][0], n)], parts[3 * q + a][0])
            if q == 0:
                loads[a] = copy(grown_in.at[a], grown.at[a])
    y, x, z = place.at
    near = [(place.dp, lax.rem(y + i // 4, 4) * 16 + lax.rem(x + i % 4, 4) * 4 + z) for i in range(1, 16)]
    tall = [(lax.rem(place.dp + i // 4, 2), place.shifted(2, i % 4)) for i in range(1, 8)]
    sem = pltpu.get_barrier_semaphore()
    for other in near + tall:
        pl.semaphore_signal(sem, inc=1, device_id=other, device_id_type=MESH)
    pl.semaphore_wait(sem, 22)
    keys = [[[wire.group(), wire.group()] + [wire.take() for _ in range(6)] for _ in range(3)] for _ in range(3)]
    at = [tuple(place.at[d] for d in ORDERS[a]) for a in range(3)]
    state = {"square": jnp.zeros((8, 128), F32)}

    def total(q, a, r):
        n = PARTS[q][a][2]
        rows = parts[3 * q + a][0][mod4(at[a][1] + r)].reshape(256, n)
        got = jnp.dot(grown[a, r], rows, preferred_element_type=F32)
        return got.reshape(4, 64, n)

    def far2(q):
        for a, _, n in PARTS[q]:
            own, out2, mid2 = parts[3 * q + a][1:4]
            dim = ORDERS[a][1]
            k = keys[q][a]
            loads[q, a].wait()
            if q == 0:
                loads[a].wait()
            out2[...] = total(q, a, 2).astype(BF)
            wire.go(k[0], k[2], out2.at[pl.ds(0, 2)], mid2.at[0], dim, 1)
            wire.go(k[0], k[3], out2.at[pl.ds(2, 2)], mid2.at[1], dim, 3)
        for a, _, n in PARTS[q]:
            parts[3 * q + a][1][...] = total(q, a, 0)

    def near2(q):
        for a, _, n in PARTS[q]:
            mid2, to2, in2 = parts[3 * q + a][3:6]
            k, dim = keys[q][a], ORDERS[a][1]
            for side, r in ((0, 1), (1, 3)):
                got = total(q, a, r)
                wire.got(k[2 + side], mid2.at[side])
                came = mid2[side].astype(F32)
                lo, hi = got[0:2], got[2:4]
                if side == 0:
                    lo = lo + came
                else:
                    hi = hi + came
                to2[side, 0:2] = lo.astype(BF)
                to2[side, 2:4] = hi.astype(BF)
                wire.go(k[0], k[4], to2.at[side], in2.at[side], dim, r)

    def far1(q):
        for a, _, n in PARTS[q]:
            own, in2, out1, mid1 = (parts[3 * q + a][i] for i in (1, 5, 6, 7))
            n1, dim = at[a][0], ORDERS[a][0]
            k = keys[q][a]
            wire.got(k[4], in2)
            own[...] = own[...] + (in2[0].astype(F32) + in2[1].astype(F32))
            out1[0] = own[mod4(n1 + 2)].astype(BF)
            wire.go(k[1], k[5], out1.at[0, pl.ds(0, 32)], mid1.at[0, pl.ds(0, 32)], dim, 1)
            wire.go(k[1], k[6], out1.at[0, pl.ds(32, 32)], mid1.at[0, pl.ds(32, 32)], dim, 3)

    def near1(q):
        for a, _, n in PARTS[q]:
            own, in2, out1, mid1 = (parts[3 * q + a][i] for i in (1, 5, 6, 7))
            n1, dim = at[a][0], ORDERS[a][0]
            k = keys[q][a]
            for side, r in ((0, 1), (1, 3)):
                rows = pl.ds(32 * side, 32)
                rest = pl.ds(32 - 32 * side, 32)
                wire.got(k[5 + side], mid1.at[0, rows])
                s = mod4(n1 + r)
                out1[1 + side, rows] = (own[s, rows] + mid1[0, rows].astype(F32)).astype(BF)
                out1[1 + side, rest] = own[s, rest].astype(BF)
                wire.go(k[1], k[7], out1.at[1 + side], mid1.at[1 + side], dim, r)

    def finish(q):
        for a, f0, n in PARTS[q]:
            own, mid1 = parts[3 * q + a][1], parts[3 * q + a][7]
            k = keys[q][a]
            wire.got(k[7], mid1.at[pl.ds(1, 2)])
            got = own[at[a][0]] + (mid1[1].astype(F32) + mid1[2].astype(F32))
            hvp[:, f0 : f0 + n] = got
            state["square"] += jnp.sum((got * got).reshape(8, 8, n // 128, 128), axis=(0, 2))

    far2(0)
    far2(1)
    near2(0)
    far2(2)
    far1(0)
    near2(1)
    near1(0)
    t = tan[...].astype(F32)
    low = jnp.sum((t * t).reshape(8, 8, 16, 128), axis=(0, 2))
    far1(1)
    near2(2)
    finish(0)
    near1(1)
    far1(2)
    finish(1)
    near1(2)
    finish(2)

    def share(table, value, spot, others):
        table[spot, 0] = value[0]
        table[spot, 1] = value[1]
        sent, came = wire.group(), wire.take()
        for other in others:
            wire.push(sent, came, table.at[spot], table.at[spot], other)
        wire.got(came, table.at[pl.ds(0, len(others))])
        wire.sent(sent, table.at[pl.ds(0, len(others))])
        return jnp.sum(table[...], axis=0)

    full = share(plane, (state["square"], low), y * 4 + x, near)
    full = share(line, (full[0], full[1]), place.dp * 4 + z, tall)
    top, low = jnp.sum(full[0]), jnp.sum(full[1])
    ratio[...] = jnp.full((1, 1), top, F32) / jnp.full((1, 1), low, F32)
    for q in range(3):
        for a in range(3):
            back, _, _, _, _, _, out1, _ = parts[3 * q + a]
            wire.sent(keys[q][a][0], back.at[pl.ds(0, 3)])
            wire.sent(keys[q][a][1], out1)


N_SENT, N_CAME = 18 + 2, 54 + 2


def collect(backs, grown, tan):
    vmem = pl.BlockSpec(memory_space=pltpu.VMEM)
    hbm = pl.BlockSpec(memory_space=pl.ANY)
    scratch = []
    for q in range(3):
        for _, _, f in PARTS[q]:
            scratch += [
                pltpu.VMEM((4, 4, 64, f), BF),
                pltpu.VMEM((4, 64, f), F32),
                pltpu.VMEM((4, 64, f), BF),
                pltpu.VMEM((2, 2, 64, f), BF),
                pltpu.VMEM((2, 4, 64, f), BF),
                pltpu.VMEM((2, 4, 64, f), BF),
                pltpu.VMEM((3, 64, f), BF),
                pltpu.VMEM((3, 64, f), BF),
            ]
    scratch += [
        pltpu.VMEM((3, 4, 256, 256), BF),
        pltpu.VMEM((16, 2, 8, 128), F32),
        pltpu.VMEM((8, 2, 8, 128), F32),
        pltpu.SemaphoreType.DMA((N_SENT,)),
        pltpu.SemaphoreType.DMA((N_CAME,)),
        pltpu.SemaphoreType.DMA((12,)),
    ]
    return pl.pallas_call(
        collect_kernel,
        out_shape=(jax.ShapeDtypeStruct((TOK, D), F32), jax.ShapeDtypeStruct((1, 1), F32)),
        in_specs=[hbm] * 4 + [vmem],
        out_specs=(vmem, vmem),
        scratch_shapes=scratch,
        compiler_params=pltpu.CompilerParams(
            collective_id=2, has_side_effects=True, vmem_limit_bytes=64100000
        ),
        name="collect",
    )(*backs, grown, tan)


def local(tokens, tangent, adjoint, gates, expert_ids, w_gate, w_up, w_down):
    *backs, grown = dispatch(tokens, tangent, adjoint, expert_ids.T, gates.T, w_gate, w_up, w_down)
    backs = [b.reshape(4, 4, 64, b.shape[-1]) for b in backs]
    hvp, ratio = collect(backs, grown, tangent)
    return hvp, ratio[0, 0]


def solution(mesh):
    rows = P(("dp", "expert"), None)
    weights = P("expert", None, None)
    return jax.shard_map(
        local,
        mesh=mesh,
        in_specs=(rows,) * 5 + (weights,) * 3,
        out_specs=(rows, P()),
        check_vma=False,
    )
```

```python
import functools

import jax
import jax.numpy as jnp
from jax import lax
from jax.experimental import pallas as pl
from jax.experimental.pallas import tpu as pltpu
from jax.sharding import PartitionSpec as P

MESH = pl.DeviceIdType.MESH
STRIDE = (16, 4, 1)
ORDERS = ((0, 1, 2), (1, 2, 0), (2, 0, 1))
PARTS = (
    ((0, 0, 256), (1, 768, 256), (2, 1408, 256)),
    ((0, 256, 256), (1, 1024, 256), (2, 1664, 256)),
    ((0, 512, 256), (1, 1280, 128), (2, 1920, 128)),
)
TOK, D, FF, R = 64, 2048, 768, 4
BF, F32 = jnp.bfloat16, jnp.float32


class Place:
    def __init__(self):
        self.me = lax.axis_index("expert")
        self.dp = lax.axis_index("dp")
        self.at = (self.me // 16, (self.me // 4) % 4, self.me % 4)

    def shifted(self, dim, by):
        c = self.at[dim]
        return self.me + (lax.rem(c + by, 4) - c) * STRIDE[dim]


def barrier(place):
    sem = pltpu.get_barrier_semaphore()
    for dim in range(3):
        for by in (1, 2, 3):
            pl.semaphore_signal(
                sem, inc=1, device_id=(place.dp, place.shifted(dim, by)), device_id_type=MESH
            )
    pl.semaphore_wait(sem, 9)


class Wire:
    def __init__(self, place, send, recv):
        self.place, self.send, self.recv, self.groups, self.taken = place, send, recv, 0, 0

    def group(self):
        self.groups += 1
        return self.groups - 1

    def take(self):
        self.taken += 1
        return self.taken - 1

    def _copy(self, sent, came, src, dst, target):
        return pltpu.make_async_remote_copy(
            src_ref=src, dst_ref=dst, send_sem=self.send.at[sent], recv_sem=self.recv.at[came],
            device_id=target, device_id_type=MESH,
        )

    def push(self, sent, came, src, dst, target):
        self._copy(sent, came, src, dst, target).start()

    def go(self, sent, came, src, dst, dim, by):
        self.push(sent, came, src, dst, (self.place.dp, self.place.shifted(dim, by)))

    def got(self, came, view):
        self._copy(0, came, view, view, (self.place.dp, self.place.shifted(0, 1))).wait_recv()

    def sent(self, group, view):
        self._copy(group, 0, view, view, (self.place.dp, self.place.shifted(0, 1))).wait_send()


def mod4(v):
    return lax.rem(v, 4)


def column_terms(meta, a, s2, place):
    dim = ORDERS[a][2]
    blocks = [meta[a, s2, s] for s in range(4)]
    low = lax.broadcasted_iota(jnp.int32, (8, 128), 1) < 64
    turn = [pltpu.roll(b, 64, 1) for b in blocks]
    ids = jnp.concatenate([jnp.where(low, blocks[0], turn[1]), jnp.where(low, blocks[2], turn[3])], axis=1)
    gates = jnp.concatenate([jnp.where(low, turn[0], blocks[1]), jnp.where(low, turn[2], blocks[3])], axis=1)
    row = lax.broadcasted_iota(jnp.int32, (8, 256), 0)
    named = jnp.zeros((8, 256), F32)
    weight = jnp.zeros((8, 256), F32)
    for r in range(8):
        e = 2 * (place.me + (r // 2 - place.at[dim]) * STRIDE[dim]) + r % 2
        hit = ids == e.astype(F32)
        n = jnp.sum(jnp.where(hit, 1.0, 0.0), axis=0, keepdims=True)
        g = jnp.sum(jnp.where(hit, gates, 0.0), axis=0, keepdims=True)
        named = jnp.where(row == r, n, named)
        weight = jnp.where(row == r, g, weight)
    i = lax.broadcasted_iota(jnp.int32, (256, 256), 0)
    l = lax.broadcasted_iota(jnp.int32, (256, 256), 1)
    upper = jnp.where((i // 64 == l // 64) & (i < l), 1.0, 0.0).astype(BF)
    before = jnp.dot(named.astype(BF), upper, preferred_element_type=F32)
    base = (lax.broadcasted_iota(jnp.int32, (8, 256), 1) // 64 * 8).astype(F32)
    return jnp.where(named > 0.5, base + before, -1.0), weight


NT = (((1,), (1,)), ((), ()))


def dispatch_kernel(tok, tan, adj, ids, gates, wg_in, wu_in, wd_in,
                    r0, r1, r2, b0, b1, b2, grown,
                    held, packed, relay, meta, chunk, wg, wu, wd, pre, lin, dirg, diru, back, parts,
                    o0, o1, o2, q0, q1, q2, picks, spin, grow, send, recv, local):
    place = Place()
    wire = Wire(place, send, recv)
    outs, backs, replies, passing = (r0, r1, r2), (b0, b1, b2), (o0, o1, o2), (q0, q1, q2)
    at = [(place.at[ORDERS[a][1]], place.at[ORDERS[a][0]]) for a in range(3)]

    def copy(src, dst, spot):
        c = pltpu.make_async_copy(src, dst, local.at[spot])
        c.start()
        return c

    own = [copy(src, held.at[a, at[a][0], at[a][1]], a) for a, src in enumerate((tok, tan, adj))]
    heavy = [copy(wg_in, wg, 3), copy(wu_in, wu, 4), copy(wd_in, chunk, 5)]
    turned = jnp.concatenate([ids[...].astype(F32), gates[...]], axis=1)
    for a in range(3):
        meta[a, at[a][0], at[a][1]] = turned
    barrier(place)
    for c in own:
        c.wait()

    def half(a, s2, s1, h):
        return held.at[a, s2, s1, pl.ds(32 * h, 32)]

    def spread(a, dim, at2, at1, keys):
        plus, minus, rest, _, sent = keys
        wire.go(sent, plus, half(a, at2, at1, 0), half(a, at2, at1, 0), dim, 1)
        wire.go(sent, minus, half(a, at2, at1, 1), half(a, at2, at1, 1), dim, 3)
        wire.go(sent, rest, half(a, at2, at1, 1), half(a, at2, at1, 1), dim, 1)
        wire.go(sent, rest, half(a, at2, at1, 0), half(a, at2, at1, 0), dim, 3)

    first, second = [], []
    for a in range(3):
        sent = wire.group()
        first.append((wire.take(), wire.take(), wire.take(), wire.take(), sent))
        sent, rest_key, far_key = wire.group(), wire.take(), wire.take()
        second.append([(wire.take(), wire.take(), rest_key, far_key, sent) for _ in range(4)])
    rel1 = (0, 3, 1, 2)

    mk1 = [(wire.group(), wire.take()) for _ in range(3)]
    mk2 = [(wire.group(), wire.take()) for _ in range(3)]
    for a in range(3):
        n2, n1 = at[a]
        for by in (1, 2, 3):
            wire.go(*mk1[a], meta.at[a, n2, n1], meta.at[a, n2, n1], ORDERS[a][0], by)
    for a in range(3):
        n2, n1 = at[a]
        spread(a, ORDERS[a][0], n2, n1, first[a])
    for a in range(3):
        n2, n1 = at[a]
        spread(a, ORDERS[a][1], n2, n1, second[a][0])
    for a in range(3):
        n2, n1 = at[a]
        wire.got(mk1[a][1], meta.at[a, n2, pl.ds(0, 3)])
        for by in (1, 2, 3):
            wire.go(*mk2[a], meta.at[a, n2], meta.at[a, n2], ORDERS[a][1], by)

    def pass_on(a, dim, keys, minus, plus):
        from_minus, from_plus, _, far, sent = keys
        wire.got(from_minus, minus(0))
        wire.go(sent, far, minus(0), minus(0), dim, 1)
        wire.got(from_plus, plus(1))
        wire.go(sent, far, plus(1), plus(1), dim, 3)

    def views1(a):
        n2, n1 = at[a]
        return (lambda h: half(a, n2, mod4(n1 + 3), h)), (lambda h: half(a, n2, mod4(n1 + 1), h))

    def views2(a, b):
        n2, n1 = at[a]
        s1 = mod4(n1 + rel1[b])
        return (lambda h: half(a, mod4(n2 + 3), s1, h)), (lambda h: half(a, mod4(n2 + 1), s1, h))

    for a in range(3):
        pass_on(a, ORDERS[a][0], first[a], *views1(a))
    for a in range(3):
        n2, n1 = at[a]
        wire.got(first[a][2], held.at[a, n2, mod4(n1 + 1)])
        for b in (1, 2):
            spread(a, ORDERS[a][1], n2, mod4(n1 + rel1[b]), second[a][b])
    for a in range(3):
        pass_on(a, ORDERS[a][1], second[a][0], *views2(a, 0))
    for a in range(3):
        n2, n1 = at[a]
        wire.got(first[a][3], held.at[a, n2, mod4(n1 + 2)])
        spread(a, ORDERS[a][1], n2, mod4(n1 + 2), second[a][3])

    slots = lax.broadcasted_iota(jnp.int32, (32, 256), 0).astype(F32)
    stored = []

    def weigh(a, r):
        index, weight = column_terms(meta, a, mod4(at[a][0] + r), place)
        for e in range(8):
            spin[pl.ds(32 * e, 32), :] = jnp.where(index[e : e + 1, :] == slots, weight[e : e + 1, :], 0.0)
        w = spin[...].T
        high = w.astype(BF)
        for e in range(8):
            hit = jnp.where(index[e : e + 1, :] == slots, 1.0, 0.0)
            picks[a, r, e % 2, pl.ds(32 * (e // 2), 32), :] = hit.astype(BF)
        n = len(stored)
        if n >= 2:
            stored[n - 2].wait()
        grow[n % 2, 0] = high
        grow[n % 2, 1] = (w - high.astype(F32)).astype(BF)
        stored.append(copy(grow.at[n % 2], grown.at[a, r], 6 + n % 2))

    third = [[(wire.group(), wire.take(), wire.take()) for _ in range(8)] for _ in range(3)]
    fourth = [[(wire.group(), [wire.take() for _ in range(3)], wire.take()) for _ in range(2)] for _ in range(3)]
    passed = [wire.group() for _ in range(3)]
    repassed = [wire.group() for _ in range(3)]
    kept = {}
    rels = (0, 1, 3, 2)

    def where(a, s):
        dim = ORDERS[a][2]
        return s // 4, place.at[dim], mod4(at[a][0] + rels[s % 4]), dim

    def settle(a, s):
        c = kept.pop((a, s), None)
        if c is not None:
            c.wait()

    def pack(s):
        for a in range(3):
            j, n3, s2, dim = where(a, s)
            buf = s % 3
            chosen = picks[a, rels[s % 4], j]
            if s >= 3:
                wire.sent(third[a][s - 3][0], packed.at[a, buf, pl.ds(0, 3)])
                settle(a, s - 3)

            @pl.loop(0, 4)
            def _(n):
                cols = pl.ds(pl.multiple_of(n * 512, 512), 512)
                rows = held[a, s2, :, :, cols].reshape(256, 512)
                got = jnp.dot(chosen, rows, preferred_element_type=F32).astype(BF)
                packed[a, buf, :, :, cols] = got.reshape(4, 32, 512)

            sent, early, _ = third[a][s]
            far = mod4(n3 + 2)
            wire.go(sent, early, packed.at[a, buf, far, pl.ds(0, 16)], relay.at[a, s, 0], dim, 1)
            wire.go(sent, early, packed.at[a, buf, far, pl.ds(16, 16)], relay.at[a, s, 1], dim, 3)

    def direct(s):
        for a in range(3):
            j, n3, s2, dim = where(a, s)
            buf = s % 3
            sent, _, late = third[a][s]
            wire.go(sent, late, packed.at[a, buf, mod4(n3 + 1)], outs[a].at[j, n3, s2], dim, 1)
            wire.go(sent, late, packed.at[a, buf, mod4(n3 + 3)], outs[a].at[j, n3, s2], dim, 3)
            kept[a, s] = copy(packed.at[a, buf, n3], outs[a].at[j, n3, s2], 8 + 3 * a + buf)

    def relays(s):
        for a in range(3):
            j, n3, s2, dim = where(a, s)
            _, early, late = third[a][s]
            sent = passed[a]
            wire.got(early, relay.at[a, s])
            wire.go(sent, late, relay.at[a, s, 0], outs[a].at[j, mod4(n3 + 3), s2, pl.ds(0, 16)], dim, 1)
            wire.go(sent, late, relay.at[a, s, 1], outs[a].at[j, mod4(n3 + 1), s2, pl.ds(16, 16)], dim, 3)

    loads = {}

    def fetch(s):
        for a in range(3):
            j, n3, s2, dim = where(a, s)
            wire.got(third[a][s][2], outs[a].at[j, pl.ds(0, 3), s2])
            settle(a, s)
            loads[a, s] = copy(outs[a].at[j, :, s2], chunk.at[a, s % 4], 17 + 4 * a + s % 4)

    def layer(s, stages):
        j, half2 = s // 4, s % 4
        for a in range(3):
            if 0 in stages:
                loads[a, s].wait()
                loads[a, s + 1].wait()
            spots2 = [where(a, s + i)[2] for i in range(2)]

            @pl.loop(min(stages), max(stages) + 1)
            def _(n):
                cols = pl.ds(pl.multiple_of(n * 256, 256), 256)
                rows = chunk[a, half2 : half2 + 2].reshape(256, D)

                def put(ref, value):
                    value = value.reshape(2, 4, 4, 8, 256)
                    for i in range(2):
                        ref[:, spots2[i], :, :, cols] = value[i]

                if a == 2:
                    put(back, jnp.dot(rows, wd[j, :, cols], preferred_element_type=F32))
                else:
                    x, y = (pre, lin) if a == 0 else (dirg, diru)
                    put(x, jnp.dot(rows, wg[j, :, cols], preferred_element_type=F32))
                    put(y, jnp.dot(rows, wu[j, :, cols], preferred_element_type=F32))

    def mix():
        @pl.loop(0, 24)
        def _(i):
            n, q = i % 3, i // 3
            zp, xp, yp = q // 4, (q // 2) % 2, q % 2
            cols = pl.ds(pl.multiple_of(n * 256, 256), 256)
            part = {}
            for dz in range(2):
                for dx in range(2):
                    for dy in range(2):
                        z, x, y = 2 * zp + dz, 2 * xp + dx, 2 * yp + dy
                        p, l = pre[z, x, y, :, cols], lin[z, x, y, :, cols]
                        pd, ld = dirg[y, z, x, :, cols], diru[y, z, x, :, cols]
                        b = back[x, y, z, :, cols]
                        s = jax.nn.sigmoid(p)
                        one = s * (1.0 + p * (1.0 - s))
                        two = s * (1.0 - s) * (2.0 + p * (1.0 - 2.0 * s))
                        part[dz, dx, dy] = (b * (ld * one + l * two * pd), b * one * pd)

            def put(a, hi, lo, inner, pair):
                at_row = pl.multiple_of(128 * hi + 32 * lo + 16 * inner, 16)
                for which in range(2):
                    value = jnp.concatenate([v[which] for v in pair], axis=0).astype(BF)
                    parts[a, which, pl.ds(at_row, 16), cols] = value

            for u in range(2):
                for w in range(2):
                    put(0, 2 * zp + u, 2 * xp + w, yp, (part[u, w, 0], part[u, w, 1]))
                    put(1, 2 * yp + u, 2 * zp + w, xp, (part[w, 0, u], part[w, 1, u]))
                    put(2, 2 * xp + u, 2 * yp + w, zp, (part[0, u, w], part[1, u, w]))

    replied = []

    def reply(j):
        for c, pieces in enumerate(PARTS):
            for a, start, n in pieces:
                f0, f = SPANS[a]
                out = replies[a]
                if j == 1 and c == 0:
                    wire.sent(fourth[a][0][0], out.at[pl.ds(0, 3)])
                    replied[a].wait()
                rows = pl.ds(start, n)
                got = lax.dot_general(parts[a, 0], wg[j, rows, :], NT, preferred_element_type=F32)
                got += lax.dot_general(parts[a, 1], wu[j, rows, :], NT, preferred_element_type=F32)
                cols = pl.ds(start - f0, n)
                out[:, :, :, cols] = got.astype(BF).reshape(4, 4, 32, n)
                n3, dim = place.at[ORDERS[a][2]], ORDERS[a][2]
                sent, early, late = fourth[a][j]
                far = mod4(n3 + 2)
                here = out.at[:, :, :, cols]
                there = backs[a].at[:, n3, j, :, cols]
                hold = passing[a].at[j, :, :, :, cols]
                wire.go(sent, early[c], here.at[far, pl.ds(0, 2)], hold.at[0], dim, 1)
                wire.go(sent, early[c], here.at[far, pl.ds(2, 2)], hold.at[1], dim, 3)
                wire.go(sent, late, here.at[mod4(n3 + 1)], there, dim, 1)
                wire.go(sent, late, here.at[mod4(n3 + 3)], there, dim, 3)
                if c == 2:
                    replied.append(copy(out.at[n3], backs[a].at[:, n3, j], 29 + 3 * j + a))

    def replays(j):
        for c, pieces in enumerate(PARTS):
            for a, start, n in pieces:
                n3, dim = place.at[ORDERS[a][2]], ORDERS[a][2]
                cols = pl.ds(start - SPANS[a][0], n)
                hold = passing[a].at[j, :, :, :, cols]
                _, early, late = fourth[a][j]
                wire.got(early[c], hold)
                there = backs[a].at[:, :, j, :, cols]
                wire.go(repassed[a], late, hold.at[0], there.at[pl.ds(0, 2), mod4(n3 + 3)], dim, 1)
                wire.go(repassed[a], late, hold.at[1], there.at[pl.ds(2, 2), mod4(n3 + 1)], dim, 3)

    for a in range(3):
        wire.got(mk2[a][1], meta.at[a, pl.ds(0, 3)])
    def turn_over(k):
        if k == 0:
            heavy[2].wait()

        @pl.loop(0, 8)
        def _(m):
            cols = pl.ds(pl.multiple_of(m * 256, 256), 256)
            block = chunk[k // 2, 2 * (k % 2) : 2 * (k % 2) + 2, :, :, cols].reshape(256, 256)
            wd[k // 3, cols, 256 * (k % 3) : 256 * (k % 3) + 256] = block.T

    for b in (1, 2):
        for a in range(3):
            pass_on(a, ORDERS[a][1], second[a][b], *views2(a, b))
            weigh(a, 2 * b - 2)
            weigh(a, 2 * b - 1)
            turn_over(3 * b - 3 + a)
        if b == 1:
            pack(0)
    for a in range(3):
        pass_on(a, ORDERS[a][1], second[a][3], *views2(a, 3))
    for a in range(3):
        wire.got(second[a][0][2], held.at[a, 0])
    pack(1)
    direct(0)
    relays(0)
    pack(2)
    direct(1)
    relays(1)
    for a in range(3):
        wire.got(second[a][0][3], held.at[a, 0])
    pack(3)
    direct(2)
    relays(2)
    heavy[0].wait()
    heavy[1].wait()
    fetch(0)
    pack(4)
    direct(3)
    relays(3)
    fetch(1)
    layer(0, (0, 1, 2))
    pack(5)
    direct(4)
    relays(4)
    fetch(2)
    fetch(3)
    layer(2, (0,))
    pack(6)
    direct(5)
    relays(5)
    layer(2, (1, 2))
    pack(7)
    direct(6)
    relays(6)
    direct(7)
    mix()
    relays(7)
    fetch(4)
    fetch(5)
    layer(4, (0, 1, 2))
    reply(0)
    fetch(6)
    fetch(7)
    replays(0)
    layer(6, (0, 1, 2))
    mix()
    reply(1)
    replays(1)
    for a in range(3):
        for j in range(2):
            wire.got(fourth[a][j][2], backs[a].at[pl.ds(0, 3), :, j])
        wire.sent(first[a][4], held.at[a, 0, pl.ds(0, 3)])
        wire.sent(second[a][0][4], held.at[a, pl.ds(0, 3)])
        wire.sent(mk1[a][0], meta.at[a, 0, pl.ds(0, 3)])
        wire.sent(mk2[a][0], meta.at[a, pl.ds(0, 3)])
        for s in (5, 6, 7):
            wire.sent(third[a][s][0], packed.at[a, 0, pl.ds(0, 3)])
        wire.sent(passed[a], relay.at[a])
        wire.sent(fourth[a][1][0], replies[a].at[pl.ds(0, 3)])
        wire.sent(repassed[a], passing[a])
    for c in replied[3:] + stored[-2:]:
        c.wait()


N_GROUPS, N_TAKEN, N_LOCAL = 6 + 6 + 30 + 6, 42 + 6 + 48 + 24, 35
SPANS = ((0, 768), (768, 640), (1408, 640))


def dispatch(tok, tan, adj, ids, gates, wg, wu, wd):
    vmem = pl.BlockSpec(memory_space=pltpu.VMEM)
    hbm = pl.BlockSpec(memory_space=pl.ANY)
    rows = jax.ShapeDtypeStruct((2, 4, 4, 32, D), BF)
    out = pl.pallas_call(
        dispatch_kernel,
        out_shape=(rows, rows, rows)
        + tuple(jax.ShapeDtypeStruct((4, 4, 2, 32, f), BF) for _, f in SPANS)
        + (jax.ShapeDtypeStruct((3, 4, 2, 256, 256), BF),),
        in_specs=[hbm] * 3 + [vmem] * 2 + [hbm] * 3,
        out_specs=(hbm,) * 7,
        scratch_shapes=[
            pltpu.VMEM((3, 4, 4, TOK, D), BF),
            pltpu.VMEM((3, 3, 4, 32, D), BF),
            pltpu.VMEM((3, 8, 2, 16, D), BF),
            pltpu.VMEM((3, 4, 4, 8, 128), F32),
            pltpu.VMEM((3, 4, 4, 32, D), BF),
            pltpu.VMEM((2, D, FF), BF),
            pltpu.VMEM((2, D, FF), BF),
            pltpu.VMEM((2, D, FF), BF),
        ]
        + [pltpu.VMEM((4, 4, 4, 8, FF), F32)] * 5
        + [pltpu.VMEM((3, 2, 512, FF), BF)]
        + [pltpu.VMEM((4, 4, 32, f), BF) for _, f in SPANS]
        + [pltpu.VMEM((2, 2, 2, 32, f), BF) for _, f in SPANS]
        + [
            pltpu.VMEM((3, 4, 2, 128, 256), BF),
            pltpu.VMEM((256, 256), F32),
            pltpu.VMEM((2, 2, 256, 256), BF),
            pltpu.SemaphoreType.DMA((N_GROUPS,)),
            pltpu.SemaphoreType.DMA((N_TAKEN,)),
            pltpu.SemaphoreType.DMA((N_LOCAL,)),
        ],
        compiler_params=pltpu.CompilerParams(
            collective_id=1, has_side_effects=True, vmem_limit_bytes=67043328
        ),
        name="dispatch",
    )(tok, tan, adj, ids, gates, wg, wu, wd)
    return out[3:]


def collect_kernel(b0, b1, b2, grown_in, tan, hvp, ratio, *scratch):
    place = Place()
    n_part = 8
    parts = [scratch[i * n_part : (i + 1) * n_part] for i in range(9)]
    grown, plane, line, send, recv, local = scratch[9 * n_part :]
    wire = Wire(place, send, recv)
    spots = iter(range(12))
    backs = (b0, b1, b2)

    def copy(src, dst):
        c = pltpu.make_async_copy(src, dst, local.at[next(spots)])
        c.start()
        return c

    loads = {}
    for q in range(3):
        for a, f0, n in PARTS[q]:
            loads[q, a] = copy(backs[a].at[:, :, :, pl.ds(f0 - SPANS[a][0], n)], parts[3 * q + a][0])
            if q == 0:
                loads[a] = copy(grown_in.at[a], grown.at[a])
    y, x, z = place.at
    near = [(place.dp, lax.rem(y + i // 4, 4) * 16 + lax.rem(x + i % 4, 4) * 4 + z) for i in range(1, 16)]
    tall = [(lax.rem(place.dp + i // 4, 2), place.shifted(2, i % 4)) for i in range(1, 8)]
    sem = pltpu.get_barrier_semaphore()
    for other in near + tall:
        pl.semaphore_signal(sem, inc=1, device_id=other, device_id_type=MESH)
    pl.semaphore_wait(sem, 22)
    keys = [[[wire.group(), wire.group()] + [wire.take() for _ in range(4)] for _ in range(3)] for _ in range(3)]
    at = [tuple(place.at[d] for d in ORDERS[a]) for a in range(3)]
    state = {"square": jnp.zeros((8, 128), F32)}

    def total(q, a, r):
        n = PARTS[q][a][2]
        rows = parts[3 * q + a][0][mod4(at[a][1] + r)].reshape(256, n)
        got = jnp.dot(grown[a, r, 0], rows, preferred_element_type=F32)
        got = got + jnp.dot(grown[a, r, 1], rows, preferred_element_type=F32)
        return got.reshape(4, 64, n)

    def far2(q):
        for a, _, n in PARTS[q]:
            own, out2, mid2 = parts[3 * q + a][1:4]
            dim = ORDERS[a][1]
            k = keys[q][a]
            loads[q, a].wait()
            if q == 0:
                loads[a].wait()
            out2[...] = total(q, a, 2).astype(BF)
            wire.go(k[0], k[2], out2.at[pl.ds(0, 2)], mid2.at[0], dim, 1)
            wire.go(k[0], k[3], out2.at[pl.ds(2, 2)], mid2.at[1], dim, 3)
        for a, _, n in PARTS[q]:
            parts[3 * q + a][1][...] = total(q, a, 0)

    def near2(q):
        for a, _, n in PARTS[q]:
            mid2, to2, in2 = parts[3 * q + a][3:6]
            k, dim = keys[q][a], ORDERS[a][1]
            for side, r in ((0, 1), (1, 3)):
                got = total(q, a, r)
                wire.got(k[2 + side], mid2.at[side])
                came = mid2[side].astype(F32)
                lo, hi = got[0:2], got[2:4]
                if side == 0:
                    lo = lo + came
                else:
                    hi = hi + came
                to2[side, 0:2] = lo.astype(BF)
                to2[side, 2:4] = hi.astype(BF)
                wire.go(k[0], k[4], to2.at[side], in2.at[side], dim, r)

    def last(q):
        for a, _, n in PARTS[q]:
            own, in2, out1, mid1 = (parts[3 * q + a][i] for i in (1, 5, 6, 7))
            n1, dim = at[a][0], ORDERS[a][0]
            k = keys[q][a]
            wire.got(k[4], in2)
            own[...] = own[...] + (in2[0].astype(F32) + in2[1].astype(F32))
            for by in (2, 1, 3):
                out1[by - 1] = own[mod4(n1 + by)].astype(BF)
                wire.go(k[1], k[5], out1.at[by - 1], mid1.at[by - 1], dim, by)

    def finish(q):
        for a, f0, n in PARTS[q]:
            own, mid1 = parts[3 * q + a][1], parts[3 * q + a][7]
            k = keys[q][a]
            wire.got(k[5], mid1)
            got = own[at[a][0]] + (mid1[0].astype(F32) + mid1[1].astype(F32) + mid1[2].astype(F32))
            hvp[:, f0 : f0 + n] = got
            state["square"] += jnp.sum((got * got).reshape(8, 8, n // 128, 128), axis=(0, 2))

    far2(0)
    far2(1)
    near2(0)
    far2(2)
    last(0)
    near2(1)
    t = tan[...].astype(F32)
    low = jnp.sum((t * t).reshape(8, 8, 16, 128), axis=(0, 2))
    near2(2)
    finish(0)
    last(1)
    finish(1)
    last(2)
    finish(2)

    def share(table, value, spot, others):
        table[spot, 0] = value[0]
        table[spot, 1] = value[1]
        sent, came = wire.group(), wire.take()
        for other in others:
            wire.push(sent, came, table.at[spot], table.at[spot], other)
        wire.got(came, table.at[pl.ds(0, len(others))])
        wire.sent(sent, table.at[pl.ds(0, len(others))])
        return jnp.sum(table[...], axis=0)

    full = share(plane, (state["square"], low), y * 4 + x, near)
    full = share(line, (full[0], full[1]), place.dp * 4 + z, tall)
    top, low = jnp.sum(full[0]), jnp.sum(full[1])
    ratio[...] = jnp.full((1, 1), top, F32) / jnp.full((1, 1), low, F32)
    for q in range(3):
        for a in range(3):
            back, _, _, _, _, _, out1, _ = parts[3 * q + a]
            wire.sent(keys[q][a][0], back.at[pl.ds(0, 3)])
            wire.sent(keys[q][a][1], out1)


N_SENT, N_CAME = 18 + 2, 36 + 2


def collect(backs, grown, tan):
    vmem = pl.BlockSpec(memory_space=pltpu.VMEM)
    hbm = pl.BlockSpec(memory_space=pl.ANY)
    scratch = []
    for q in range(3):
        for _, _, f in PARTS[q]:
            scratch += [
                pltpu.VMEM((4, 4, 64, f), BF),
                pltpu.VMEM((4, 64, f), F32),
                pltpu.VMEM((4, 64, f), BF),
                pltpu.VMEM((2, 2, 64, f), BF),
                pltpu.VMEM((2, 4, 64, f), BF),
                pltpu.VMEM((2, 4, 64, f), BF),
                pltpu.VMEM((3, 64, f), BF),
                pltpu.VMEM((3, 64, f), BF),
            ]
    scratch += [
        pltpu.VMEM((3, 4, 2, 256, 256), BF),
        pltpu.VMEM((16, 2, 8, 128), F32),
        pltpu.VMEM((8, 2, 8, 128), F32),
        pltpu.SemaphoreType.DMA((N_SENT,)),
        pltpu.SemaphoreType.DMA((N_CAME,)),
        pltpu.SemaphoreType.DMA((12,)),
    ]
    return pl.pallas_call(
        collect_kernel,
        out_shape=(jax.ShapeDtypeStruct((TOK, D), F32), jax.ShapeDtypeStruct((1, 1), F32)),
        in_specs=[hbm] * 4 + [vmem],
        out_specs=(vmem, vmem),
        scratch_shapes=scratch,
        compiler_params=pltpu.CompilerParams(
            collective_id=2, has_side_effects=True, vmem_limit_bytes=67043328
        ),
        name="collect",
    )(*backs, grown, tan)


def local(tokens, tangent, adjoint, gates, expert_ids, w_gate, w_up, w_down):
    w_down = w_down.reshape(3, 4, 4, 32, D)
    *backs, grown = dispatch(tokens, tangent, adjoint, expert_ids.T, gates.T, w_gate, w_up, w_down)
    backs = [b.reshape(4, 4, 64, b.shape[-1]) for b in backs]
    hvp, ratio = collect(backs, grown, tangent)
    return hvp, ratio[0, 0]


def solution(mesh):
    rows = P(("dp", "expert"), None)
    weights = P("expert", None, None)
    return jax.shard_map(
        local,
        mesh=mesh,
        in_specs=(rows,) * 5 + (weights,) * 3,
        out_specs=(rows, P()),
        check_vma=False,
    )
```

```python
import functools

import jax
import jax.numpy as jnp
from jax import lax
from jax.experimental import pallas as pl
from jax.experimental.pallas import tpu as pltpu
from jax.sharding import PartitionSpec as P

MESH = pl.DeviceIdType.MESH
STRIDE = (16, 4, 1)
ORDERS = ((0, 1, 2), (1, 2, 0), (2, 0, 1))
PARTS = (
    ((0, 0, 256), (1, 768, 256), (2, 1408, 256)),
    ((0, 256, 256), (1, 1024, 256), (2, 1664, 256)),
    ((0, 512, 256), (1, 1280, 128), (2, 1920, 128)),
)
TOK, D, FF, R = 64, 2048, 768, 4
BF, F32 = jnp.bfloat16, jnp.float32


class Place:
    def __init__(self):
        self.me = lax.axis_index("expert")
        self.dp = lax.axis_index("dp")
        self.at = (self.me // 16, (self.me // 4) % 4, self.me % 4)

    def shifted(self, dim, by):
        c = self.at[dim]
        return self.me + (lax.rem(c + by, 4) - c) * STRIDE[dim]


def barrier(place):
    sem = pltpu.get_barrier_semaphore()
    for dim in range(3):
        for by in (1, 2, 3):
            pl.semaphore_signal(
                sem, inc=1, device_id=(place.dp, place.shifted(dim, by)), device_id_type=MESH
            )
    pl.semaphore_wait(sem, 9)


class Wire:
    def __init__(self, place, send, recv):
        self.place, self.send, self.recv, self.groups, self.taken = place, send, recv, 0, 0

    def group(self):
        self.groups += 1
        return self.groups - 1

    def take(self):
        self.taken += 1
        return self.taken - 1

    def _copy(self, sent, came, src, dst, target):
        return pltpu.make_async_remote_copy(
            src_ref=src, dst_ref=dst, send_sem=self.send.at[sent], recv_sem=self.recv.at[came],
            device_id=target, device_id_type=MESH,
        )

    def push(self, sent, came, src, dst, target):
        self._copy(sent, came, src, dst, target).start()

    def go(self, sent, came, src, dst, dim, by):
        self.push(sent, came, src, dst, (self.place.dp, self.place.shifted(dim, by)))

    def got(self, came, view):
        self._copy(0, came, view, view, (self.place.dp, self.place.shifted(0, 1))).wait_recv()

    def sent(self, group, view):
        self._copy(group, 0, view, view, (self.place.dp, self.place.shifted(0, 1))).wait_send()


def mod4(v):
    return lax.rem(v, 4)


def column_terms(meta, a, s2, place):
    dim = ORDERS[a][2]
    blocks = [meta[a, s2, s] for s in range(4)]
    low = lax.broadcasted_iota(jnp.int32, (8, 128), 1) < 64
    turn = [pltpu.roll(b, 64, 1) for b in blocks]
    ids = jnp.concatenate([jnp.where(low, blocks[0], turn[1]), jnp.where(low, blocks[2], turn[3])], axis=1)
    gates = jnp.concatenate([jnp.where(low, turn[0], blocks[1]), jnp.where(low, turn[2], blocks[3])], axis=1)
    row = lax.broadcasted_iota(jnp.int32, (8, 256), 0)
    named = jnp.zeros((8, 256), F32)
    weight = jnp.zeros((8, 256), F32)
    for r in range(8):
        e = 2 * (place.me + (r // 2 - place.at[dim]) * STRIDE[dim]) + r % 2
        hit = ids == e.astype(F32)
        n = jnp.sum(jnp.where(hit, 1.0, 0.0), axis=0, keepdims=True)
        g = jnp.sum(jnp.where(hit, gates, 0.0), axis=0, keepdims=True)
        named = jnp.where(row == r, n, named)
        weight = jnp.where(row == r, g, weight)
    i = lax.broadcasted_iota(jnp.int32, (256, 256), 0)
    l = lax.broadcasted_iota(jnp.int32, (256, 256), 1)
    upper = jnp.where((i // 64 == l // 64) & (i < l), 1.0, 0.0).astype(BF)
    before = jnp.dot(named.astype(BF), upper, preferred_element_type=F32)
    base = (lax.broadcasted_iota(jnp.int32, (8, 256), 1) // 64 * 8).astype(F32)
    return jnp.where(named > 0.5, base + before, -1.0), weight


NT = (((1,), (1,)), ((), ()))


def dispatch_kernel(tok, tan, adj, ids, gates, wg_in, wu_in, wd_in,
                    r0, r1, r2, b0, b1, b2, grown,
                    held, packed, relay, meta, chunk, wg, wu, wd, pre, lin, dirg, diru, back, parts,
                    o0, o1, o2, q0, q1, q2, picks, spin, grow, send, recv, local):
    place = Place()
    wire = Wire(place, send, recv)
    outs, backs, replies, passing = (r0, r1, r2), (b0, b1, b2), (o0, o1, o2), (q0, q1, q2)
    at = [(place.at[ORDERS[a][1]], place.at[ORDERS[a][0]]) for a in range(3)]

    def copy(src, dst, spot):
        c = pltpu.make_async_copy(src, dst, local.at[spot])
        c.start()
        return c

    own = [copy(src, held.at[a, at[a][0], at[a][1]], a) for a, src in enumerate((tok, tan, adj))]
    heavy = [copy(wg_in, wg, 3), copy(wu_in, wu, 4), copy(wd_in, chunk, 5)]
    turned = jnp.concatenate([ids[...].astype(F32), gates[...]], axis=1)
    for a in range(3):
        meta[a, at[a][0], at[a][1]] = turned
    barrier(place)
    for c in own:
        c.wait()

    def half(a, s2, s1, h):
        return held.at[a, s2, s1, pl.ds(32 * h, 32)]

    def spread(a, dim, at2, at1, keys):
        plus, minus, rest, _, sent = keys
        wire.go(sent, plus, half(a, at2, at1, 0), half(a, at2, at1, 0), dim, 1)
        wire.go(sent, minus, half(a, at2, at1, 1), half(a, at2, at1, 1), dim, 3)
        wire.go(sent, rest, half(a, at2, at1, 1), half(a, at2, at1, 1), dim, 1)
        wire.go(sent, rest, half(a, at2, at1, 0), half(a, at2, at1, 0), dim, 3)

    first, second = [], []
    for a in range(3):
        sent = wire.group()
        first.append((wire.take(), wire.take(), wire.take(), wire.take(), sent))
        sent, rest_key, far_key = wire.group(), wire.take(), wire.take()
        second.append([(wire.take(), wire.take(), rest_key, far_key, sent) for _ in range(4)])
    rel1 = (0, 3, 1, 2)

    mk1 = [(wire.group(), wire.take()) for _ in range(3)]
    mk2 = [(wire.group(), wire.take()) for _ in range(3)]
    for a in range(3):
        n2, n1 = at[a]
        for by in (1, 2, 3):
            wire.go(*mk1[a], meta.at[a, n2, n1], meta.at[a, n2, n1], ORDERS[a][0], by)
    for a in range(3):
        n2, n1 = at[a]
        spread(a, ORDERS[a][0], n2, n1, first[a])
    for a in range(3):
        n2, n1 = at[a]
        spread(a, ORDERS[a][1], n2, n1, second[a][0])
    for a in range(3):
        n2, n1 = at[a]
        wire.got(mk1[a][1], meta.at[a, n2, pl.ds(0, 3)])
        for by in (1, 2, 3):
            wire.go(*mk2[a], meta.at[a, n2], meta.at[a, n2], ORDERS[a][1], by)

    def pass_on(a, dim, keys, minus, plus):
        from_minus, from_plus, _, far, sent = keys
        wire.got(from_minus, minus(0))
        wire.go(sent, far, minus(0), minus(0), dim, 1)
        wire.got(from_plus, plus(1))
        wire.go(sent, far, plus(1), plus(1), dim, 3)

    def views1(a):
        n2, n1 = at[a]
        return (lambda h: half(a, n2, mod4(n1 + 3), h)), (lambda h: half(a, n2, mod4(n1 + 1), h))

    def views2(a, b):
        n2, n1 = at[a]
        s1 = mod4(n1 + rel1[b])
        return (lambda h: half(a, mod4(n2 + 3), s1, h)), (lambda h: half(a, mod4(n2 + 1), s1, h))

    for a in range(3):
        pass_on(a, ORDERS[a][0], first[a], *views1(a))
    for a in range(3):
        n2, n1 = at[a]
        wire.got(first[a][2], held.at[a, n2, mod4(n1 + 1)])
        for b in (1, 2):
            spread(a, ORDERS[a][1], n2, mod4(n1 + rel1[b]), second[a][b])
    for a in range(3):
        pass_on(a, ORDERS[a][1], second[a][0], *views2(a, 0))
    for a in range(3):
        n2, n1 = at[a]
        wire.got(first[a][3], held.at[a, n2, mod4(n1 + 2)])
        spread(a, ORDERS[a][1], n2, mod4(n1 + 2), second[a][3])

    slots = lax.broadcasted_iota(jnp.int32, (32, 256), 0).astype(F32)
    stored = []

    def weigh(a, r):
        index, weight = column_terms(meta, a, mod4(at[a][0] + r), place)
        for e in range(8):
            spin[pl.ds(32 * e, 32), :] = jnp.where(index[e : e + 1, :] == slots, weight[e : e + 1, :], 0.0)
        w = spin[...].T
        high = w.astype(BF)
        for e in range(8):
            hit = jnp.where(index[e : e + 1, :] == slots, 1.0, 0.0)
            picks[a, r, e % 2, pl.ds(32 * (e // 2), 32), :] = hit.astype(BF)
        n = len(stored)
        if n >= 2:
            stored[n - 2].wait()
        grow[n % 2, 0] = high
        grow[n % 2, 1] = (w - high.astype(F32)).astype(BF)
        stored.append(copy(grow.at[n % 2], grown.at[a, r], 6 + n % 2))

    third = [[(wire.group(), wire.take(), wire.take()) for _ in range(8)] for _ in range(3)]
    fourth = [[(wire.group(), wire.take(), wire.take()) for _ in range(2)] for _ in range(3)]
    passed = [wire.group() for _ in range(3)]
    repassed = [wire.group() for _ in range(3)]
    kept = {}
    rels = (0, 1, 3, 2)

    def where(a, s):
        dim = ORDERS[a][2]
        return s // 4, place.at[dim], mod4(at[a][0] + rels[s % 4]), dim

    def settle(a, s):
        c = kept.pop((a, s), None)
        if c is not None:
            c.wait()

    def pack(s):
        for a in range(3):
            j, n3, s2, dim = where(a, s)
            buf = s % 3
            chosen = picks[a, rels[s % 4], j]
            if s >= 3:
                wire.sent(third[a][s - 3][0], packed.at[a, buf, pl.ds(0, 3)])
                settle(a, s - 3)

            @pl.loop(0, 4)
            def _(n):
                cols = pl.ds(pl.multiple_of(n * 512, 512), 512)
                rows = held[a, s2, :, :, cols].reshape(256, 512)
                got = jnp.dot(chosen, rows, preferred_element_type=F32).astype(BF)
                packed[a, buf, :, :, cols] = got.reshape(4, 32, 512)

            sent, early, _ = third[a][s]
            far = mod4(n3 + 2)
            wire.go(sent, early, packed.at[a, buf, far, pl.ds(0, 16)], relay.at[a, s, 0], dim, 1)
            wire.go(sent, early, packed.at[a, buf, far, pl.ds(16, 16)], relay.at[a, s, 1], dim, 3)

    def direct(s):
        for a in range(3):
            j, n3, s2, dim = where(a, s)
            buf = s % 3
            sent, _, late = third[a][s]
            wire.go(sent, late, packed.at[a, buf, mod4(n3 + 1)], outs[a].at[j, n3, s2], dim, 1)
            wire.go(sent, late, packed.at[a, buf, mod4(n3 + 3)], outs[a].at[j, n3, s2], dim, 3)
            kept[a, s] = copy(packed.at[a, buf, n3], outs[a].at[j, n3, s2], 8 + 3 * a + buf)

    def relays(s):
        for a in range(3):
            j, n3, s2, dim = where(a, s)
            _, early, late = third[a][s]
            sent = passed[a]
            wire.got(early, relay.at[a, s])
            wire.go(sent, late, relay.at[a, s, 0], outs[a].at[j, mod4(n3 + 3), s2, pl.ds(0, 16)], dim, 1)
            wire.go(sent, late, relay.at[a, s, 1], outs[a].at[j, mod4(n3 + 1), s2, pl.ds(16, 16)], dim, 3)

    loads = {}

    def fetch(s):
        for a in range(3):
            j, n3, s2, dim = where(a, s)
            wire.got(third[a][s][2], outs[a].at[j, pl.ds(0, 3), s2])
            settle(a, s)
            loads[a, s] = copy(outs[a].at[j, :, s2], chunk.at[a, s % 4], 17 + 4 * a + s % 4)

    def layer(s, stages):
        j, half2 = s // 4, s % 4
        for a in range(3):
            if 0 in stages:
                loads[a, s].wait()
                loads[a, s + 1].wait()
            spots2 = [where(a, s + i)[2] for i in range(2)]

            @pl.loop(min(stages), max(stages) + 1)
            def _(n):
                cols = pl.ds(pl.multiple_of(n * 256, 256), 256)
                rows = chunk[a, half2 : half2 + 2].reshape(256, D)

                def put(ref, value):
                    value = value.reshape(2, 4, 4, 8, 256)
                    for i in range(2):
                        ref[:, spots2[i], :, :, cols] = value[i]

                if a == 2:
                    put(back, jnp.dot(rows, wd[j, :, cols], preferred_element_type=F32))
                else:
                    x, y = (pre, lin) if a == 0 else (dirg, diru)
                    put(x, jnp.dot(rows, wg[j, :, cols], preferred_element_type=F32))
                    put(y, jnp.dot(rows, wu[j, :, cols], preferred_element_type=F32))

    def mix():
        @pl.loop(0, 24)
        def _(i):
            n, q = i % 3, i // 3
            zp, xp, yp = q // 4, (q // 2) % 2, q % 2
            cols = pl.ds(pl.multiple_of(n * 256, 256), 256)
            part = {}
            for dz in range(2):
                for dx in range(2):
                    for dy in range(2):
                        z, x, y = 2 * zp + dz, 2 * xp + dx, 2 * yp + dy
                        p, l = pre[z, x, y, :, cols], lin[z, x, y, :, cols]
                        pd, ld = dirg[y, z, x, :, cols], diru[y, z, x, :, cols]
                        b = back[x, y, z, :, cols]
                        s = jax.nn.sigmoid(p)
                        one = s * (1.0 + p * (1.0 - s))
                        two = s * (1.0 - s) * (2.0 + p * (1.0 - 2.0 * s))
                        part[dz, dx, dy] = (b * (ld * one + l * two * pd), b * one * pd)

            def put(a, hi, lo, inner, pair):
                at_row = pl.multiple_of(128 * hi + 32 * lo + 16 * inner, 16)
                for which in range(2):
                    value = jnp.concatenate([v[which] for v in pair], axis=0).astype(BF)
                    parts[a, which, pl.ds(at_row, 16), cols] = value

            for u in range(2):
                for w in range(2):
                    put(0, 2 * zp + u, 2 * xp + w, yp, (part[u, w, 0], part[u, w, 1]))
                    put(1, 2 * yp + u, 2 * zp + w, xp, (part[w, 0, u], part[w, 1, u]))
                    put(2, 2 * xp + u, 2 * yp + w, zp, (part[0, u, w], part[1, u, w]))

    replied = []

    def reply(j):
        for a in range(3):
            f0, f = SPANS[a]
            out = replies[a]
            if j == 1:
                wire.sent(fourth[a][0][0], out.at[pl.ds(0, 3)])
                replied[a].wait()
            done = 0
            while done < f:
                n = min(256, f - done)
                rows = pl.ds(f0 + done, n)
                got = lax.dot_general(parts[a, 0], wg[j, rows, :], NT, preferred_element_type=F32)
                got += lax.dot_general(parts[a, 1], wu[j, rows, :], NT, preferred_element_type=F32)
                out[:, :, :, done : done + n] = got.astype(BF).reshape(4, 4, 32, n)
                done += n
            n3, dim = place.at[ORDERS[a][2]], ORDERS[a][2]
            sent, early, late = fourth[a][j]
            far = mod4(n3 + 2)
            wire.go(sent, early, out.at[far, pl.ds(0, 2)], passing[a].at[j, 0], dim, 1)
            wire.go(sent, early, out.at[far, pl.ds(2, 2)], passing[a].at[j, 1], dim, 3)
            wire.go(sent, late, out.at[mod4(n3 + 1)], backs[a].at[:, n3, j], dim, 1)
            wire.go(sent, late, out.at[mod4(n3 + 3)], backs[a].at[:, n3, j], dim, 3)
            replied.append(copy(out.at[n3], backs[a].at[:, n3, j], 29 + 3 * j + a))

    def replays(j):
        for a in range(3):
            n3, dim = place.at[ORDERS[a][2]], ORDERS[a][2]
            hold = passing[a]
            _, early, late = fourth[a][j]
            wire.got(early, hold.at[j])
            wire.go(repassed[a], late, hold.at[j, 0], backs[a].at[pl.ds(0, 2), mod4(n3 + 3), j], dim, 1)
            wire.go(repassed[a], late, hold.at[j, 1], backs[a].at[pl.ds(2, 2), mod4(n3 + 1), j], dim, 3)

    for a in range(3):
        wire.got(mk2[a][1], meta.at[a, pl.ds(0, 3)])
    def turn_over(k):
        if k == 0:
            heavy[2].wait()

        @pl.loop(0, 8)
        def _(m):
            cols = pl.ds(pl.multiple_of(m * 256, 256), 256)
            block = chunk[k // 2, 2 * (k % 2) : 2 * (k % 2) + 2, :, :, cols].reshape(256, 256)
            wd[k // 3, cols, 256 * (k % 3) : 256 * (k % 3) + 256] = block.T

    for b in (1, 2):
        for a in range(3):
            pass_on(a, ORDERS[a][1], second[a][b], *views2(a, b))
            weigh(a, 2 * b - 2)
            weigh(a, 2 * b - 1)
            turn_over(3 * b - 3 + a)
        if b == 1:
            pack(0)
    for a in range(3):
        pass_on(a, ORDERS[a][1], second[a][3], *views2(a, 3))
    for a in range(3):
        wire.got(second[a][0][2], held.at[a, 0])
    pack(1)
    direct(0)
    relays(0)
    pack(2)
    direct(1)
    relays(1)
    for a in range(3):
        wire.got(second[a][0][3], held.at[a, 0])
    pack(3)
    direct(2)
    relays(2)
    heavy[0].wait()
    heavy[1].wait()
    fetch(0)
    pack(4)
    direct(3)
    relays(3)
    fetch(1)
    layer(0, (0, 1, 2))
    pack(5)
    direct(4)
    relays(4)
    fetch(2)
    fetch(3)
    layer(2, (0,))
    pack(6)
    direct(5)
    relays(5)
    layer(2, (1, 2))
    pack(7)
    direct(6)
    relays(6)
    mix()
    direct(7)
    relays(7)
    fetch(4)
    fetch(5)
    layer(4, (0, 1, 2))
    reply(0)
    fetch(6)
    fetch(7)
    replays(0)
    layer(6, (0, 1, 2))
    mix()
    reply(1)
    replays(1)
    for a in range(3):
        for j in range(2):
            wire.got(fourth[a][j][2], backs[a].at[pl.ds(0, 3), :, j])
        wire.sent(first[a][4], held.at[a, 0, pl.ds(0, 3)])
        wire.sent(second[a][0][4], held.at[a, pl.ds(0, 3)])
        wire.sent(mk1[a][0], meta.at[a, 0, pl.ds(0, 3)])
        wire.sent(mk2[a][0], meta.at[a, pl.ds(0, 3)])
        for s in (5, 6, 7):
            wire.sent(third[a][s][0], packed.at[a, 0, pl.ds(0, 3)])
        wire.sent(passed[a], relay.at[a])
        wire.sent(fourth[a][1][0], replies[a].at[pl.ds(0, 3)])
        wire.sent(repassed[a], passing[a])
    for c in replied[3:] + stored[-2:]:
        c.wait()


N_GROUPS, N_TAKEN, N_LOCAL = 6 + 6 + 30 + 6, 42 + 6 + 48 + 12, 35
SPANS = ((0, 768), (768, 640), (1408, 640))


def dispatch(tok, tan, adj, ids, gates, wg, wu, wd):
    vmem = pl.BlockSpec(memory_space=pltpu.VMEM)
    hbm = pl.BlockSpec(memory_space=pl.ANY)
    rows = jax.ShapeDtypeStruct((2, 4, 4, 32, D), BF)
    out = pl.pallas_call(
        dispatch_kernel,
        out_shape=(rows, rows, rows)
        + tuple(jax.ShapeDtypeStruct((4, 4, 2, 32, f), BF) for _, f in SPANS)
        + (jax.ShapeDtypeStruct((3, 4, 2, 256, 256), BF),),
        in_specs=[hbm] * 3 + [vmem] * 2 + [hbm] * 3,
        out_specs=(hbm,) * 7,
        scratch_shapes=[
            pltpu.VMEM((3, 4, 4, TOK, D), BF),
            pltpu.VMEM((3, 3, 4, 32, D), BF),
            pltpu.VMEM((3, 8, 2, 16, D), BF),
            pltpu.VMEM((3, 4, 4, 8, 128), F32),
            pltpu.VMEM((3, 4, 4, 32, D), BF),
            pltpu.VMEM((2, D, FF), BF),
            pltpu.VMEM((2, D, FF), BF),
            pltpu.VMEM((2, D, FF), BF),
        ]
        + [pltpu.VMEM((4, 4, 4, 8, FF), F32)] * 5
        + [pltpu.VMEM((3, 2, 512, FF), BF)]
        + [pltpu.VMEM((4, 4, 32, f), BF) for _, f in SPANS]
        + [pltpu.VMEM((2, 2, 2, 32, f), BF) for _, f in SPANS]
        + [
            pltpu.VMEM((3, 4, 2, 128, 256), BF),
            pltpu.VMEM((256, 256), F32),
            pltpu.VMEM((2, 2, 256, 256), BF),
            pltpu.SemaphoreType.DMA((N_GROUPS,)),
            pltpu.SemaphoreType.DMA((N_TAKEN,)),
            pltpu.SemaphoreType.DMA((N_LOCAL,)),
        ],
        compiler_params=pltpu.CompilerParams(
            collective_id=1, has_side_effects=True, vmem_limit_bytes=67043328
        ),
        name="dispatch",
    )(tok, tan, adj, ids, gates, wg, wu, wd)
    return out[3:]


def collect_kernel(b0, b1, b2, grown_in, tan, hvp, ratio, *scratch):
    place = Place()
    n_part = 8
    parts = [scratch[i * n_part : (i + 1) * n_part] for i in range(9)]
    grown, plane, line, send, recv, local = scratch[9 * n_part :]
    wire = Wire(place, send, recv)
    spots = iter(range(12))
    backs = (b0, b1, b2)

    def copy(src, dst):
        c = pltpu.make_async_copy(src, dst, local.at[next(spots)])
        c.start()
        return c

    loads = {}
    for q in range(3):
        for a, f0, n in PARTS[q]:
            loads[q, a] = copy(backs[a].at[:, :, :, pl.ds(f0 - SPANS[a][0], n)], parts[3 * q + a][0])
            if q == 0:
                loads[a] = copy(grown_in.at[a], grown.at[a])
    y, x, z = place.at
    near = [(place.dp, lax.rem(y + i // 4, 4) * 16 + lax.rem(x + i % 4, 4) * 4 + z) for i in range(1, 16)]
    tall = [(lax.rem(place.dp + i // 4, 2), place.shifted(2, i % 4)) for i in range(1, 8)]
    sem = pltpu.get_barrier_semaphore()
    for other in near + tall:
        pl.semaphore_signal(sem, inc=1, device_id=other, device_id_type=MESH)
    pl.semaphore_wait(sem, 22)
    keys = [[[wire.group(), wire.group()] + [wire.take() for _ in range(4)] for _ in range(3)] for _ in range(3)]
    at = [tuple(place.at[d] for d in ORDERS[a]) for a in range(3)]
    state = {"square": jnp.zeros((8, 128), F32)}

    def total(q, a, r):
        n = PARTS[q][a][2]
        rows = parts[3 * q + a][0][mod4(at[a][1] + r)].reshape(256, n)
        got = jnp.dot(grown[a, r, 0], rows, preferred_element_type=F32)
        got = got + jnp.dot(grown[a, r, 1], rows, preferred_element_type=F32)
        return got.reshape(4, 64, n)

    def far2(q):
        for a, _, n in PARTS[q]:
            own, out2, mid2 = parts[3 * q + a][1:4]
            dim = ORDERS[a][1]
            k = keys[q][a]
            loads[q, a].wait()
            if q == 0:
                loads[a].wait()
            out2[...] = total(q, a, 2).astype(BF)
            wire.go(k[0], k[2], out2.at[pl.ds(0, 2)], mid2.at[0], dim, 1)
            wire.go(k[0], k[3], out2.at[pl.ds(2, 2)], mid2.at[1], dim, 3)
        for a, _, n in PARTS[q]:
            parts[3 * q + a][1][...] = total(q, a, 0)

    def near2(q):
        for a, _, n in PARTS[q]:
            mid2, to2, in2 = parts[3 * q + a][3:6]
            k, dim = keys[q][a], ORDERS[a][1]
            for side, r in ((0, 1), (1, 3)):
                got = total(q, a, r)
                wire.got(k[2 + side], mid2.at[side])
                came = mid2[side].astype(F32)
                lo, hi = got[0:2], got[2:4]
                if side == 0:
                    lo = lo + came
                else:
                    hi = hi + came
                to2[side, 0:2] = lo.astype(BF)
                to2[side, 2:4] = hi.astype(BF)
                wire.go(k[0], k[4], to2.at[side], in2.at[side], dim, r)

    def last(q):
        for a, _, n in PARTS[q]:
            own, in2, out1, mid1 = (parts[3 * q + a][i] for i in (1, 5, 6, 7))
            n1, dim = at[a][0], ORDERS[a][0]
            k = keys[q][a]
            wire.got(k[4], in2)
            own[...] = own[...] + (in2[0].astype(F32) + in2[1].astype(F32))
            for by in (2, 1, 3):
                out1[by - 1] = own[mod4(n1 + by)].astype(BF)
                wire.go(k[1], k[5], out1.at[by - 1], mid1.at[by - 1], dim, by)

    def finish(q):
        for a, f0, n in PARTS[q]:
            own, mid1 = parts[3 * q + a][1], parts[3 * q + a][7]
            k = keys[q][a]
            wire.got(k[5], mid1)
            got = own[at[a][0]] + (mid1[0].astype(F32) + mid1[1].astype(F32) + mid1[2].astype(F32))
            hvp[:, f0 : f0 + n] = got
            state["square"] += jnp.sum((got * got).reshape(8, 8, n // 128, 128), axis=(0, 2))

    far2(0)
    far2(1)
    near2(0)
    far2(2)
    last(0)
    near2(1)
    t = tan[...].astype(F32)
    low = jnp.sum((t * t).reshape(8, 8, 16, 128), axis=(0, 2))
    near2(2)
    finish(0)
    last(1)
    finish(1)
    last(2)
    finish(2)

    def share(table, value, spot, others):
        table[spot, 0] = value[0]
        table[spot, 1] = value[1]
        sent, came = wire.group(), wire.take()
        for other in others:
            wire.push(sent, came, table.at[spot], table.at[spot], other)
        wire.got(came, table.at[pl.ds(0, len(others))])
        wire.sent(sent, table.at[pl.ds(0, len(others))])
        return jnp.sum(table[...], axis=0)

    full = share(plane, (state["square"], low), y * 4 + x, near)
    full = share(line, (full[0], full[1]), place.dp * 4 + z, tall)
    top, low = jnp.sum(full[0]), jnp.sum(full[1])
    ratio[...] = jnp.full((1, 1), top, F32) / jnp.full((1, 1), low, F32)
    for q in range(3):
        for a in range(3):
            back, _, _, _, _, _, out1, _ = parts[3 * q + a]
            wire.sent(keys[q][a][0], back.at[pl.ds(0, 3)])
            wire.sent(keys[q][a][1], out1)


N_SENT, N_CAME = 18 + 2, 36 + 2


def collect(backs, grown, tan):
    vmem = pl.BlockSpec(memory_space=pltpu.VMEM)
    hbm = pl.BlockSpec(memory_space=pl.ANY)
    scratch = []
    for q in range(3):
        for _, _, f in PARTS[q]:
            scratch += [
                pltpu.VMEM((4, 4, 64, f), BF),
                pltpu.VMEM((4, 64, f), F32),
                pltpu.VMEM((4, 64, f), BF),
                pltpu.VMEM((2, 2, 64, f), BF),
                pltpu.VMEM((2, 4, 64, f), BF),
                pltpu.VMEM((2, 4, 64, f), BF),
                pltpu.VMEM((3, 64, f), BF),
                pltpu.VMEM((3, 64, f), BF),
            ]
    scratch += [
        pltpu.VMEM((3, 4, 2, 256, 256), BF),
        pltpu.VMEM((16, 2, 8, 128), F32),
        pltpu.VMEM((8, 2, 8, 128), F32),
        pltpu.SemaphoreType.DMA((N_SENT,)),
        pltpu.SemaphoreType.DMA((N_CAME,)),
        pltpu.SemaphoreType.DMA((12,)),
    ]
    return pl.pallas_call(
        collect_kernel,
        out_shape=(jax.ShapeDtypeStruct((TOK, D), F32), jax.ShapeDtypeStruct((1, 1), F32)),
        in_specs=[hbm] * 4 + [vmem],
        out_specs=(vmem, vmem),
        scratch_shapes=scratch,
        compiler_params=pltpu.CompilerParams(
            collective_id=2, has_side_effects=True, vmem_limit_bytes=67043328
        ),
        name="collect",
    )(*backs, grown, tan)


def local(tokens, tangent, adjoint, gates, expert_ids, w_gate, w_up, w_down):
    w_down = w_down.reshape(3, 4, 4, 32, D)
    *backs, grown = dispatch(tokens, tangent, adjoint, expert_ids.T, gates.T, w_gate, w_up, w_down)
    backs = [b.reshape(4, 4, 64, b.shape[-1]) for b in backs]
    hvp, ratio = collect(backs, grown, tangent)
    return hvp, ratio[0, 0]


def solution(mesh):
    rows = P(("dp", "expert"), None)
    weights = P("expert", None, None)
    return jax.shard_map(
        local,
        mesh=mesh,
        in_specs=(rows,) * 5 + (weights,) * 3,
        out_specs=(rows, P()),
        check_vma=False,
    )
```

```python
import functools

import jax
import jax.numpy as jnp
from jax import lax
from jax.experimental import pallas as pl
from jax.experimental.pallas import tpu as pltpu
from jax.sharding import PartitionSpec as P

MESH = pl.DeviceIdType.MESH
STRIDE = (16, 4, 1)
ORDERS = ((0, 1, 2), (1, 2, 0), (2, 0, 1))
PARTS = (
    ((0, 0, 256), (1, 768, 256), (2, 1408, 256)),
    ((0, 256, 256), (1, 1024, 256), (2, 1664, 256)),
    ((0, 512, 256), (1, 1280, 128), (2, 1920, 128)),
)
TOK, D, FF, R = 64, 2048, 768, 4
BF, F32 = jnp.bfloat16, jnp.float32


class Place:
    def __init__(self):
        self.me = lax.axis_index("expert")
        self.dp = lax.axis_index("dp")
        self.at = (self.me // 16, (self.me // 4) % 4, self.me % 4)

    def shifted(self, dim, by):
        c = self.at[dim]
        return self.me + (lax.rem(c + by, 4) - c) * STRIDE[dim]


def barrier(place):
    sem = pltpu.get_barrier_semaphore()
    for dim in range(3):
        for by in (1, 2, 3):
            pl.semaphore_signal(
                sem, inc=1, device_id=(place.dp, place.shifted(dim, by)), device_id_type=MESH
            )
    pl.semaphore_wait(sem, 9)


class Wire:
    def __init__(self, place, send, recv):
        self.place, self.send, self.recv, self.groups, self.taken = place, send, recv, 0, 0

    def group(self):
        self.groups += 1
        return self.groups - 1

    def take(self):
        self.taken += 1
        return self.taken - 1

    def _copy(self, sent, came, src, dst, target):
        return pltpu.make_async_remote_copy(
            src_ref=src, dst_ref=dst, send_sem=self.send.at[sent], recv_sem=self.recv.at[came],
            device_id=target, device_id_type=MESH,
        )

    def push(self, sent, came, src, dst, target):
        self._copy(sent, came, src, dst, target).start()

    def go(self, sent, came, src, dst, dim, by):
        self.push(sent, came, src, dst, (self.place.dp, self.place.shifted(dim, by)))

    def got(self, came, view):
        self._copy(0, came, view, view, (self.place.dp, self.place.shifted(0, 1))).wait_recv()

    def sent(self, group, view):
        self._copy(group, 0, view, view, (self.place.dp, self.place.shifted(0, 1))).wait_send()


def mod4(v):
    return lax.rem(v, 4)


def column_terms(meta, a, s2, place):
    dim = ORDERS[a][2]
    blocks = [meta[a, s2, s] for s in range(4)]
    low = lax.broadcasted_iota(jnp.int32, (8, 128), 1) < 64
    turn = [pltpu.roll(b, 64, 1) for b in blocks]
    ids = jnp.concatenate([jnp.where(low, blocks[0], turn[1]), jnp.where(low, blocks[2], turn[3])], axis=1)
    gates = jnp.concatenate([jnp.where(low, turn[0], blocks[1]), jnp.where(low, turn[2], blocks[3])], axis=1)
    row = lax.broadcasted_iota(jnp.int32, (8, 256), 0)
    named = jnp.zeros((8, 256), F32)
    weight = jnp.zeros((8, 256), F32)
    for r in range(8):
        e = 2 * (place.me + (r // 2 - place.at[dim]) * STRIDE[dim]) + r % 2
        hit = ids == e.astype(F32)
        n = jnp.sum(jnp.where(hit, 1.0, 0.0), axis=0, keepdims=True)
        g = jnp.sum(jnp.where(hit, gates, 0.0), axis=0, keepdims=True)
        named = jnp.where(row == r, n, named)
        weight = jnp.where(row == r, g, weight)
    i = lax.broadcasted_iota(jnp.int32, (256, 256), 0)
    l = lax.broadcasted_iota(jnp.int32, (256, 256), 1)
    upper = jnp.where((i // 64 == l // 64) & (i < l), 1.0, 0.0).astype(BF)
    before = jnp.dot(named.astype(BF), upper, preferred_element_type=F32)
    base = (lax.broadcasted_iota(jnp.int32, (8, 256), 1) // 64 * 8).astype(F32)
    return jnp.where(named > 0.5, base + before, -1.0), weight


NT = (((1,), (1,)), ((), ()))


def dispatch_kernel(tok, tan, adj, ids, gates, wg_in, wu_in, wd_in,
                    r0, r1, r2, b0, b1, b2, grown,
                    held, packed, relay, meta, chunk, wg, wu, wd, pre, lin, dirg, diru, back, parts,
                    o0, o1, o2, q0, q1, q2, picks, spin, grow, send, recv, local):
    place = Place()
    wire = Wire(place, send, recv)
    outs, backs, replies, passing = (r0, r1, r2), (b0, b1, b2), (o0, o1, o2), (q0, q1, q2)
    at = [(place.at[ORDERS[a][1]], place.at[ORDERS[a][0]]) for a in range(3)]

    def copy(src, dst, spot):
        c = pltpu.make_async_copy(src, dst, local.at[spot])
        c.start()
        return c

    own = [copy(src, held.at[a, at[a][0], at[a][1]], a) for a, src in enumerate((tok, tan, adj))]
    heavy = [copy(wg_in, wg, 3), copy(wu_in, wu, 4), copy(wd_in, chunk, 5)]
    turned = jnp.concatenate([ids[...].astype(F32), gates[...]], axis=1)
    for a in range(3):
        meta[a, at[a][0], at[a][1]] = turned
    barrier(place)
    for c in own:
        c.wait()

    def half(a, s2, s1, h):
        return held.at[a, s2, s1, pl.ds(32 * h, 32)]

    def spread(a, dim, at2, at1, keys):
        plus, minus, rest, _, sent = keys
        wire.go(sent, plus, half(a, at2, at1, 0), half(a, at2, at1, 0), dim, 1)
        wire.go(sent, minus, half(a, at2, at1, 1), half(a, at2, at1, 1), dim, 3)
        wire.go(sent, rest, half(a, at2, at1, 1), half(a, at2, at1, 1), dim, 1)
        wire.go(sent, rest, half(a, at2, at1, 0), half(a, at2, at1, 0), dim, 3)

    first, second = [], []
    for a in range(3):
        sent = wire.group()
        first.append((wire.take(), wire.take(), wire.take(), wire.take(), sent))
        sent, rest_key, far_key = wire.group(), wire.take(), wire.take()
        second.append([(wire.take(), wire.take(), rest_key, far_key, sent) for _ in range(4)])
    rel1 = (0, 3, 1, 2)

    mk1 = [(wire.group(), wire.take()) for _ in range(3)]
    mk2 = [(wire.group(), wire.take()) for _ in range(3)]
    for a in range(3):
        n2, n1 = at[a]
        for by in (1, 2, 3):
            wire.go(*mk1[a], meta.at[a, n2, n1], meta.at[a, n2, n1], ORDERS[a][0], by)
    for a in range(3):
        n2, n1 = at[a]
        spread(a, ORDERS[a][0], n2, n1, first[a])
    for a in range(3):
        n2, n1 = at[a]
        spread(a, ORDERS[a][1], n2, n1, second[a][0])
    for a in range(3):
        n2, n1 = at[a]
        wire.got(mk1[a][1], meta.at[a, n2, pl.ds(0, 3)])
        for by in (1, 2, 3):
            wire.go(*mk2[a], meta.at[a, n2], meta.at[a, n2], ORDERS[a][1], by)

    def pass_on(a, dim, keys, minus, plus):
        from_minus, from_plus, _, far, sent = keys
        wire.got(from_minus, minus(0))
        wire.go(sent, far, minus(0), minus(0), dim, 1)
        wire.got(from_plus, plus(1))
        wire.go(sent, far, plus(1), plus(1), dim, 3)

    def views1(a):
        n2, n1 = at[a]
        return (lambda h: half(a, n2, mod4(n1 + 3), h)), (lambda h: half(a, n2, mod4(n1 + 1), h))

    def views2(a, b):
        n2, n1 = at[a]
        s1 = mod4(n1 + rel1[b])
        return (lambda h: half(a, mod4(n2 + 3), s1, h)), (lambda h: half(a, mod4(n2 + 1), s1, h))

    for a in range(3):
        pass_on(a, ORDERS[a][0], first[a], *views1(a))
    for a in range(3):
        n2, n1 = at[a]
        wire.got(first[a][2], held.at[a, n2, mod4(n1 + 1)])
        for b in (1, 2):
            spread(a, ORDERS[a][1], n2, mod4(n1 + rel1[b]), second[a][b])
    for a in range(3):
        pass_on(a, ORDERS[a][1], second[a][0], *views2(a, 0))
    for a in range(3):
        n2, n1 = at[a]
        wire.got(first[a][3], held.at[a, n2, mod4(n1 + 2)])
        spread(a, ORDERS[a][1], n2, mod4(n1 + 2), second[a][3])

    slots = lax.broadcasted_iota(jnp.int32, (32, 256), 0).astype(F32)
    stored = []

    def weigh(a, r):
        index, weight = column_terms(meta, a, mod4(at[a][0] + r), place)
        for e in range(8):
            spin[pl.ds(32 * e, 32), :] = jnp.where(index[e : e + 1, :] == slots, weight[e : e + 1, :], 0.0)
        w = spin[...].T
        high = w.astype(BF)
        for e in range(8):
            hit = jnp.where(index[e : e + 1, :] == slots, 1.0, 0.0)
            picks[a, r, e % 2, pl.ds(32 * (e // 2), 32), :] = hit.astype(BF)
        n = len(stored)
        if n >= 2:
            stored[n - 2].wait()
        grow[n % 2, 0] = high
        grow[n % 2, 1] = (w - high.astype(F32)).astype(BF)
        stored.append(copy(grow.at[n % 2], grown.at[a, r], 6 + n % 2))

    third = [[(wire.group(), wire.take(), wire.take()) for _ in range(8)] for _ in range(3)]
    fourth = [[(wire.group(), wire.take(), wire.take()) for _ in range(2)] for _ in range(3)]
    passed = [wire.group() for _ in range(3)]
    repassed = [wire.group() for _ in range(3)]
    kept = {}
    rels = (0, 1, 3, 2)

    def where(a, s):
        dim = ORDERS[a][2]
        return s // 4, place.at[dim], mod4(at[a][0] + rels[s % 4]), dim

    def settle(a, s):
        c = kept.pop((a, s), None)
        if c is not None:
            c.wait()

    def pack(s):
        for a in range(3):
            j, n3, s2, dim = where(a, s)
            buf = s % 3
            chosen = picks[a, rels[s % 4], j]
            if s >= 3:
                wire.sent(third[a][s - 3][0], packed.at[a, buf, pl.ds(0, 3)])
                settle(a, s - 3)

            @pl.loop(0, 4)
            def _(n):
                cols = pl.ds(pl.multiple_of(n * 512, 512), 512)
                rows = held[a, s2, :, :, cols].reshape(256, 512)
                got = jnp.dot(chosen, rows, preferred_element_type=F32).astype(BF)
                packed[a, buf, :, :, cols] = got.reshape(4, 32, 512)

            sent, early, _ = third[a][s]
            far = mod4(n3 + 2)
            wire.go(sent, early, packed.at[a, buf, far, pl.ds(0, 16)], relay.at[a, s, 0], dim, 1)
            wire.go(sent, early, packed.at[a, buf, far, pl.ds(16, 16)], relay.at[a, s, 1], dim, 3)

    def direct(s):
        for a in range(3):
            j, n3, s2, dim = where(a, s)
            buf = s % 3
            sent, _, late = third[a][s]
            wire.go(sent, late, packed.at[a, buf, mod4(n3 + 1)], outs[a].at[j, n3, s2], dim, 1)
            wire.go(sent, late, packed.at[a, buf, mod4(n3 + 3)], outs[a].at[j, n3, s2], dim, 3)
            kept[a, s] = copy(packed.at[a, buf, n3], outs[a].at[j, n3, s2], 8 + 3 * a + buf)

    def relays(s):
        for a in range(3):
            j, n3, s2, dim = where(a, s)
            _, early, late = third[a][s]
            sent = passed[a]
            wire.got(early, relay.at[a, s])
            wire.go(sent, late, relay.at[a, s, 0], outs[a].at[j, mod4(n3 + 3), s2, pl.ds(0, 16)], dim, 1)
            wire.go(sent, late, relay.at[a, s, 1], outs[a].at[j, mod4(n3 + 1), s2, pl.ds(16, 16)], dim, 3)

    loads = {}

    def fetch(s):
        for a in range(3):
            j, n3, s2, dim = where(a, s)
            wire.got(third[a][s][2], outs[a].at[j, pl.ds(0, 3), s2])
            settle(a, s)
            loads[a, s] = copy(outs[a].at[j, :, s2], chunk.at[a, s % 4], 17 + 4 * a + s % 4)

    def layer(s, stages):
        j, half2 = s // 4, s % 4
        for a in range(3):
            if 0 in stages:
                loads[a, s].wait()
                loads[a, s + 1].wait()
            spots2 = [where(a, s + i)[2] for i in range(2)]

            @pl.loop(min(stages), max(stages) + 1)
            def _(n):
                cols = pl.ds(pl.multiple_of(n * 256, 256), 256)
                rows = chunk[a, half2 : half2 + 2].reshape(256, D)

                def put(ref, value):
                    value = value.reshape(2, 4, 4, 8, 256)
                    for i in range(2):
                        ref[:, spots2[i], :, :, cols] = value[i]

                if a == 2:
                    put(back, jnp.dot(rows, wd[j, :, cols], preferred_element_type=F32))
                else:
                    x, y = (pre, lin) if a == 0 else (dirg, diru)
                    put(x, jnp.dot(rows, wg[j, :, cols], preferred_element_type=F32))
                    put(y, jnp.dot(rows, wu[j, :, cols], preferred_element_type=F32))

    def mix():
        @pl.loop(0, 24)
        def _(i):
            n, q = i % 3, i // 3
            zp, xp, yp = q // 4, (q // 2) % 2, q % 2
            cols = pl.ds(pl.multiple_of(n * 256, 256), 256)
            part = {}
            for dz in range(2):
                for dx in range(2):
                    for dy in range(2):
                        z, x, y = 2 * zp + dz, 2 * xp + dx, 2 * yp + dy
                        p, l = pre[z, x, y, :, cols], lin[z, x, y, :, cols]
                        pd, ld = dirg[y, z, x, :, cols], diru[y, z, x, :, cols]
                        b = back[x, y, z, :, cols]
                        s = jax.nn.sigmoid(p)
                        one = s * (1.0 + p * (1.0 - s))
                        two = s * (1.0 - s) * (2.0 + p * (1.0 - 2.0 * s))
                        part[dz, dx, dy] = (b * (ld * one + l * two * pd), b * one * pd)

            def put(a, hi, lo, inner, pair):
                at_row = pl.multiple_of(128 * hi + 32 * lo + 16 * inner, 16)
                for which in range(2):
                    value = jnp.concatenate([v[which] for v in pair], axis=0).astype(BF)
                    parts[a, which, pl.ds(at_row, 16), cols] = value

            for u in range(2):
                for w in range(2):
                    put(0, 2 * zp + u, 2 * xp + w, yp, (part[u, w, 0], part[u, w, 1]))
                    put(1, 2 * yp + u, 2 * zp + w, xp, (part[w, 0, u], part[w, 1, u]))
                    put(2, 2 * xp + u, 2 * yp + w, zp, (part[0, u, w], part[1, u, w]))

    replied = []

    def reply(j):
        for a in range(3):
            f0, f = SPANS[a]
            out = replies[a]
            if j == 1:
                wire.sent(fourth[a][0][0], out.at[pl.ds(0, 3)])
                replied[a].wait()
            done = 0
            while done < f:
                n = min(256, f - done)
                rows = pl.ds(f0 + done, n)
                got = lax.dot_general(parts[a, 0], wg[j, rows, :], NT, preferred_element_type=F32)
                got += lax.dot_general(parts[a, 1], wu[j, rows, :], NT, preferred_element_type=F32)
                out[:, :, :, done : done + n] = got.astype(BF).reshape(4, 4, 32, n)
                done += n
            n3, dim = place.at[ORDERS[a][2]], ORDERS[a][2]
            sent, early, late = fourth[a][j]
            far = mod4(n3 + 2)
            wire.go(sent, early, out.at[far, pl.ds(0, 2)], passing[a].at[j, 0], dim, 1)
            wire.go(sent, early, out.at[far, pl.ds(2, 2)], passing[a].at[j, 1], dim, 3)
            wire.go(sent, late, out.at[mod4(n3 + 1)], backs[a].at[:, n3, j], dim, 1)
            wire.go(sent, late, out.at[mod4(n3 + 3)], backs[a].at[:, n3, j], dim, 3)
            replied.append(copy(out.at[n3], backs[a].at[:, n3, j], 29 + 3 * j + a))

    def replays(j):
        for a in range(3):
            n3, dim = place.at[ORDERS[a][2]], ORDERS[a][2]
            hold = passing[a]
            _, early, late = fourth[a][j]
            wire.got(early, hold.at[j])
            wire.go(repassed[a], late, hold.at[j, 0], backs[a].at[pl.ds(0, 2), mod4(n3 + 3), j], dim, 1)
            wire.go(repassed[a], late, hold.at[j, 1], backs[a].at[pl.ds(2, 2), mod4(n3 + 1), j], dim, 3)

    for a in range(3):
        wire.got(mk2[a][1], meta.at[a, pl.ds(0, 3)])
    def turn_over(k):
        if k == 0:
            heavy[2].wait()

        @pl.loop(0, 8)
        def _(m):
            cols = pl.ds(pl.multiple_of(m * 256, 256), 256)
            block = chunk[k // 2, 2 * (k % 2) : 2 * (k % 2) + 2, :, :, cols].reshape(256, 256)
            wd[k // 3, cols, 256 * (k % 3) : 256 * (k % 3) + 256] = block.T

    for b in (1, 2):
        for a in range(3):
            pass_on(a, ORDERS[a][1], second[a][b], *views2(a, b))
            weigh(a, 2 * b - 2)
            weigh(a, 2 * b - 1)
            turn_over(3 * b - 3 + a)
        if b == 1:
            pack(0)
    for a in range(3):
        pass_on(a, ORDERS[a][1], second[a][3], *views2(a, 3))
    for a in range(3):
        wire.got(second[a][0][2], held.at[a, 0])
    pack(1)
    direct(0)
    relays(0)
    pack(2)
    direct(1)
    relays(1)
    for a in range(3):
        wire.got(second[a][0][3], held.at[a, 0])
    pack(3)
    direct(2)
    relays(2)
    heavy[0].wait()
    heavy[1].wait()
    fetch(0)
    pack(4)
    direct(3)
    relays(3)
    fetch(1)
    layer(0, (0, 1, 2))
    pack(5)
    direct(4)
    relays(4)
    fetch(2)
    fetch(3)
    layer(2, (0,))
    pack(6)
    direct(5)
    relays(5)
    layer(2, (1, 2))
    pack(7)
    direct(6)
    relays(6)
    fetch(4)
    direct(7)
    mix()
    relays(7)
    fetch(5)
    layer(4, (0, 1, 2))
    fetch(6)
    reply(0)
    fetch(7)
    layer(6, (0, 1, 2))
    replays(0)
    mix()
    reply(1)
    replays(1)
    for a in range(3):
        for j in range(2):
            wire.got(fourth[a][j][2], backs[a].at[pl.ds(0, 3), :, j])
        wire.sent(first[a][4], held.at[a, 0, pl.ds(0, 3)])
        wire.sent(second[a][0][4], held.at[a, pl.ds(0, 3)])
        wire.sent(mk1[a][0], meta.at[a, 0, pl.ds(0, 3)])
        wire.sent(mk2[a][0], meta.at[a, pl.ds(0, 3)])
        for s in (5, 6, 7):
            wire.sent(third[a][s][0], packed.at[a, 0, pl.ds(0, 3)])
        wire.sent(passed[a], relay.at[a])
        wire.sent(fourth[a][1][0], replies[a].at[pl.ds(0, 3)])
        wire.sent(repassed[a], passing[a])
    for c in replied[3:] + stored[-2:]:
        c.wait()


N_GROUPS, N_TAKEN, N_LOCAL = 6 + 6 + 30 + 6, 42 + 6 + 48 + 12, 35
SPANS = ((0, 768), (768, 640), (1408, 640))


def dispatch(tok, tan, adj, ids, gates, wg, wu, wd):
    vmem = pl.BlockSpec(memory_space=pltpu.VMEM)
    hbm = pl.BlockSpec(memory_space=pl.ANY)
    rows = jax.ShapeDtypeStruct((2, 4, 4, 32, D), BF)
    out = pl.pallas_call(
        dispatch_kernel,
        out_shape=(rows, rows, rows)
        + tuple(jax.ShapeDtypeStruct((4, 4, 2, 32, f), BF) for _, f in SPANS)
        + (jax.ShapeDtypeStruct((3, 4, 2, 256, 256), BF),),
        in_specs=[hbm] * 3 + [vmem] * 2 + [hbm] * 3,
        out_specs=(hbm,) * 7,
        scratch_shapes=[
            pltpu.VMEM((3, 4, 4, TOK, D), BF),
            pltpu.VMEM((3, 3, 4, 32, D), BF),
            pltpu.VMEM((3, 8, 2, 16, D), BF),
            pltpu.VMEM((3, 4, 4, 8, 128), F32),
            pltpu.VMEM((3, 4, 4, 32, D), BF),
            pltpu.VMEM((2, D, FF), BF),
            pltpu.VMEM((2, D, FF), BF),
            pltpu.VMEM((2, D, FF), BF),
        ]
        + [pltpu.VMEM((4, 4, 4, 8, FF), F32)] * 5
        + [pltpu.VMEM((3, 2, 512, FF), BF)]
        + [pltpu.VMEM((4, 4, 32, f), BF) for _, f in SPANS]
        + [pltpu.VMEM((2, 2, 2, 32, f), BF) for _, f in SPANS]
        + [
            pltpu.VMEM((3, 4, 2, 128, 256), BF),
            pltpu.VMEM((256, 256), F32),
            pltpu.VMEM((2, 2, 256, 256), BF),
            pltpu.SemaphoreType.DMA((N_GROUPS,)),
            pltpu.SemaphoreType.DMA((N_TAKEN,)),
            pltpu.SemaphoreType.DMA((N_LOCAL,)),
        ],
        compiler_params=pltpu.CompilerParams(
            collective_id=1, has_side_effects=True, vmem_limit_bytes=67043328
        ),
        name="dispatch",
    )(tok, tan, adj, ids, gates, wg, wu, wd)
    return out[3:]


def collect_kernel(b0, b1, b2, grown_in, tan, hvp, ratio, *scratch):
    place = Place()
    n_part = 8
    parts = [scratch[i * n_part : (i + 1) * n_part] for i in range(9)]
    grown, plane, line, send, recv, local = scratch[9 * n_part :]
    wire = Wire(place, send, recv)
    spots = iter(range(12))
    backs = (b0, b1, b2)

    def copy(src, dst):
        c = pltpu.make_async_copy(src, dst, local.at[next(spots)])
        c.start()
        return c

    loads = {}
    for q in range(3):
        for a, f0, n in PARTS[q]:
            loads[q, a] = copy(backs[a].at[:, :, :, pl.ds(f0 - SPANS[a][0], n)], parts[3 * q + a][0])
            if q == 0:
                loads[a] = copy(grown_in.at[a], grown.at[a])
    y, x, z = place.at
    near = [(place.dp, lax.rem(y + i // 4, 4) * 16 + lax.rem(x + i % 4, 4) * 4 + z) for i in range(1, 16)]
    tall = [(lax.rem(place.dp + i // 4, 2), place.shifted(2, i % 4)) for i in range(1, 8)]
    sem = pltpu.get_barrier_semaphore()
    for other in near + tall:
        pl.semaphore_signal(sem, inc=1, device_id=other, device_id_type=MESH)
    pl.semaphore_wait(sem, 22)
    keys = [[[wire.group(), wire.group()] + [wire.take() for _ in range(4)] for _ in range(3)] for _ in range(3)]
    at = [tuple(place.at[d] for d in ORDERS[a]) for a in range(3)]
    state = {"square": jnp.zeros((8, 128), F32)}

    def total(q, a, r):
        n = PARTS[q][a][2]
        rows = parts[3 * q + a][0][mod4(at[a][1] + r)].reshape(256, n)
        got = jnp.dot(grown[a, r, 0], rows, preferred_element_type=F32)
        got = got + jnp.dot(grown[a, r, 1], rows, preferred_element_type=F32)
        return got.reshape(4, 64, n)

    def far2(q):
        for a, _, n in PARTS[q]:
            own, out2, mid2 = parts[3 * q + a][1:4]
            dim = ORDERS[a][1]
            k = keys[q][a]
            loads[q, a].wait()
            if q == 0:
                loads[a].wait()
            out2[...] = total(q, a, 2).astype(BF)
            wire.go(k[0], k[2], out2.at[pl.ds(0, 2)], mid2.at[0], dim, 1)
            wire.go(k[0], k[3], out2.at[pl.ds(2, 2)], mid2.at[1], dim, 3)
        for a, _, n in PARTS[q]:
            parts[3 * q + a][1][...] = total(q, a, 0)

    def near2(q):
        for a, _, n in PARTS[q]:
            mid2, to2, in2 = parts[3 * q + a][3:6]
            k, dim = keys[q][a], ORDERS[a][1]
            for side, r in ((0, 1), (1, 3)):
                got = total(q, a, r)
                wire.got(k[2 + side], mid2.at[side])
                came = mid2[side].astype(F32)
                lo, hi = got[0:2], got[2:4]
                if side == 0:
                    lo = lo + came
                else:
                    hi = hi + came
                to2[side, 0:2] = lo.astype(BF)
                to2[side, 2:4] = hi.astype(BF)
                wire.go(k[0], k[4], to2.at[side], in2.at[side], dim, r)

    def last(q):
        for a, _, n in PARTS[q]:
            own, in2, out1, mid1 = (parts[3 * q + a][i] for i in (1, 5, 6, 7))
            n1, dim = at[a][0], ORDERS[a][0]
            k = keys[q][a]
            wire.got(k[4], in2)
            own[...] = own[...] + (in2[0].astype(F32) + in2[1].astype(F32))
            for by in (2, 1, 3):
                out1[by - 1] = own[mod4(n1 + by)].astype(BF)
                wire.go(k[1], k[5], out1.at[by - 1], mid1.at[by - 1], dim, by)

    def finish(q):
        for a, f0, n in PARTS[q]:
            own, mid1 = parts[3 * q + a][1], parts[3 * q + a][7]
            k = keys[q][a]
            wire.got(k[5], mid1)
            got = own[at[a][0]] + (mid1[0].astype(F32) + mid1[1].astype(F32) + mid1[2].astype(F32))
            hvp[:, f0 : f0 + n] = got
            state["square"] += jnp.sum((got * got).reshape(8, 8, n // 128, 128), axis=(0, 2))

    far2(0)
    far2(1)
    near2(0)
    far2(2)
    last(0)
    near2(1)
    t = tan[...].astype(F32)
    low = jnp.sum((t * t).reshape(8, 8, 16, 128), axis=(0, 2))
    near2(2)
    finish(0)
    last(1)
    finish(1)
    last(2)
    finish(2)

    def share(table, value, spot, others):
        table[spot, 0] = value[0]
        table[spot, 1] = value[1]
        sent, came = wire.group(), wire.take()
        for other in others:
            wire.push(sent, came, table.at[spot], table.at[spot], other)
        wire.got(came, table.at[pl.ds(0, len(others))])
        wire.sent(sent, table.at[pl.ds(0, len(others))])
        return jnp.sum(table[...], axis=0)

    full = share(plane, (state["square"], low), y * 4 + x, near)
    full = share(line, (full[0], full[1]), place.dp * 4 + z, tall)
    top, low = jnp.sum(full[0]), jnp.sum(full[1])
    ratio[...] = jnp.full((1, 1), top, F32) / jnp.full((1, 1), low, F32)
    for q in range(3):
        for a in range(3):
            back, _, _, _, _, _, out1, _ = parts[3 * q + a]
            wire.sent(keys[q][a][0], back.at[pl.ds(0, 3)])
            wire.sent(keys[q][a][1], out1)


N_SENT, N_CAME = 18 + 2, 36 + 2


def collect(backs, grown, tan):
    vmem = pl.BlockSpec(memory_space=pltpu.VMEM)
    hbm = pl.BlockSpec(memory_space=pl.ANY)
    scratch = []
    for q in range(3):
        for _, _, f in PARTS[q]:
            scratch += [
                pltpu.VMEM((4, 4, 64, f), BF),
                pltpu.VMEM((4, 64, f), F32),
                pltpu.VMEM((4, 64, f), BF),
                pltpu.VMEM((2, 2, 64, f), BF),
                pltpu.VMEM((2, 4, 64, f), BF),
                pltpu.VMEM((2, 4, 64, f), BF),
                pltpu.VMEM((3, 64, f), BF),
                pltpu.VMEM((3, 64, f), BF),
            ]
    scratch += [
        pltpu.VMEM((3, 4, 2, 256, 256), BF),
        pltpu.VMEM((16, 2, 8, 128), F32),
        pltpu.VMEM((8, 2, 8, 128), F32),
        pltpu.SemaphoreType.DMA((N_SENT,)),
        pltpu.SemaphoreType.DMA((N_CAME,)),
        pltpu.SemaphoreType.DMA((12,)),
    ]
    return pl.pallas_call(
        collect_kernel,
        out_shape=(jax.ShapeDtypeStruct((TOK, D), F32), jax.ShapeDtypeStruct((1, 1), F32)),
        in_specs=[hbm] * 4 + [vmem],
        out_specs=(vmem, vmem),
        scratch_shapes=scratch,
        compiler_params=pltpu.CompilerParams(
            collective_id=2, has_side_effects=True, vmem_limit_bytes=67043328
        ),
        name="collect",
    )(*backs, grown, tan)


def local(tokens, tangent, adjoint, gates, expert_ids, w_gate, w_up, w_down):
    w_down = w_down.reshape(3, 4, 4, 32, D)
    *backs, grown = dispatch(tokens, tangent, adjoint, expert_ids.T, gates.T, w_gate, w_up, w_down)
    backs = [b.reshape(4, 4, 64, b.shape[-1]) for b in backs]
    hvp, ratio = collect(backs, grown, tangent)
    return hvp, ratio[0, 0]


def solution(mesh):
    rows = P(("dp", "expert"), None)
    weights = P("expert", None, None)
    return jax.shard_map(
        local,
        mesh=mesh,
        in_specs=(rows,) * 5 + (weights,) * 3,
        out_specs=(rows, P()),
        check_vma=False,
    )
```

```python
import functools

import jax
import jax.numpy as jnp
from jax import lax
from jax.experimental import pallas as pl
from jax.experimental.pallas import tpu as pltpu
from jax.sharding import PartitionSpec as P

MESH = pl.DeviceIdType.MESH
STRIDE = (16, 4, 1)
ORDERS = ((0, 1, 2), (1, 2, 0), (2, 0, 1))
PARTS = (
    ((0, 0, 256), (1, 768, 256), (2, 1408, 256)),
    ((0, 256, 256), (1, 1024, 256), (2, 1664, 256)),
    ((0, 512, 256), (1, 1280, 128), (2, 1920, 128)),
)
TOK, D, FF, R = 64, 2048, 768, 4
BF, F32 = jnp.bfloat16, jnp.float32


class Place:
    def __init__(self):
        self.me = lax.axis_index("expert")
        self.dp = lax.axis_index("dp")
        self.at = (self.me // 16, (self.me // 4) % 4, self.me % 4)

    def shifted(self, dim, by):
        c = self.at[dim]
        return self.me + (lax.rem(c + by, 4) - c) * STRIDE[dim]


def barrier(place):
    sem = pltpu.get_barrier_semaphore()
    for dim in range(3):
        for by in (1, 2, 3):
            pl.semaphore_signal(
                sem, inc=1, device_id=(place.dp, place.shifted(dim, by)), device_id_type=MESH
            )
    pl.semaphore_wait(sem, 9)


class Wire:
    def __init__(self, place, send, recv):
        self.place, self.send, self.recv, self.groups, self.taken = place, send, recv, 0, 0

    def group(self):
        self.groups += 1
        return self.groups - 1

    def take(self):
        self.taken += 1
        return self.taken - 1

    def _copy(self, sent, came, src, dst, target):
        return pltpu.make_async_remote_copy(
            src_ref=src, dst_ref=dst, send_sem=self.send.at[sent], recv_sem=self.recv.at[came],
            device_id=target, device_id_type=MESH,
        )

    def push(self, sent, came, src, dst, target):
        self._copy(sent, came, src, dst, target).start()

    def go(self, sent, came, src, dst, dim, by):
        self.push(sent, came, src, dst, (self.place.dp, self.place.shifted(dim, by)))

    def got(self, came, view):
        self._copy(0, came, view, view, (self.place.dp, self.place.shifted(0, 1))).wait_recv()

    def sent(self, group, view):
        self._copy(group, 0, view, view, (self.place.dp, self.place.shifted(0, 1))).wait_send()


def mod4(v):
    return lax.rem(v, 4)


def column_terms(meta, a, s2, place):
    dim = ORDERS[a][2]
    blocks = [meta[a, s2, s] for s in range(4)]
    low = lax.broadcasted_iota(jnp.int32, (8, 128), 1) < 64
    turn = [pltpu.roll(b, 64, 1) for b in blocks]
    ids = jnp.concatenate([jnp.where(low, blocks[0], turn[1]), jnp.where(low, blocks[2], turn[3])], axis=1)
    gates = jnp.concatenate([jnp.where(low, turn[0], blocks[1]), jnp.where(low, turn[2], blocks[3])], axis=1)
    row = lax.broadcasted_iota(jnp.int32, (8, 256), 0)
    named = jnp.zeros((8, 256), F32)
    weight = jnp.zeros((8, 256), F32)
    for r in range(8):
        e = 2 * (place.me + (r // 2 - place.at[dim]) * STRIDE[dim]) + r % 2
        hit = ids == e.astype(F32)
        n = jnp.sum(jnp.where(hit, 1.0, 0.0), axis=0, keepdims=True)
        g = jnp.sum(jnp.where(hit, gates, 0.0), axis=0, keepdims=True)
        named = jnp.where(row == r, n, named)
        weight = jnp.where(row == r, g, weight)
    i = lax.broadcasted_iota(jnp.int32, (256, 256), 0)
    l = lax.broadcasted_iota(jnp.int32, (256, 256), 1)
    upper = jnp.where((i // 64 == l // 64) & (i < l), 1.0, 0.0).astype(BF)
    before = jnp.dot(named.astype(BF), upper, preferred_element_type=F32)
    base = (lax.broadcasted_iota(jnp.int32, (8, 256), 1) // 64 * 8).astype(F32)
    return jnp.where(named > 0.5, base + before, -1.0), weight


NT = (((1,), (1,)), ((), ()))


def dispatch_kernel(tok, tan, adj, ids, gates, wg_in, wu_in, wd_in,
                    r0, r1, r2, b0, b1, b2, grown,
                    held, packed, relay, meta, chunk, wg, wu, wd, pre, lin, dirg, diru, back, parts,
                    o0, o1, o2, q0, q1, q2, picks, spin, grow, send, recv, local):
    place = Place()
    wire = Wire(place, send, recv)
    outs, backs, replies, passing = (r0, r1, r2), (b0, b1, b2), (o0, o1, o2), (q0, q1, q2)
    at = [(place.at[ORDERS[a][1]], place.at[ORDERS[a][0]]) for a in range(3)]

    def copy(src, dst, spot):
        c = pltpu.make_async_copy(src, dst, local.at[spot])
        c.start()
        return c

    own = [copy(src, held.at[a, at[a][0], at[a][1]], a) for a, src in enumerate((tok, tan, adj))]
    heavy = [copy(wg_in, wg, 3), copy(wu_in, wu, 4), copy(wd_in, chunk, 5)]
    turned = jnp.concatenate([ids[...].astype(F32), gates[...]], axis=1)
    for a in range(3):
        meta[a, at[a][0], at[a][1]] = turned
    barrier(place)
    for c in own:
        c.wait()

    def half(a, s2, s1, h):
        return held.at[a, s2, s1, pl.ds(32 * h, 32)]

    def spread(a, dim, at2, at1, keys):
        plus, minus, rest, _, sent = keys
        wire.go(sent, plus, half(a, at2, at1, 0), half(a, at2, at1, 0), dim, 1)
        wire.go(sent, minus, half(a, at2, at1, 1), half(a, at2, at1, 1), dim, 3)
        wire.go(sent, rest, half(a, at2, at1, 1), half(a, at2, at1, 1), dim, 1)
        wire.go(sent, rest, half(a, at2, at1, 0), half(a, at2, at1, 0), dim, 3)

    first, second = [], []
    for a in range(3):
        sent = wire.group()
        first.append((wire.take(), wire.take(), wire.take(), wire.take(), sent))
        sent, rest_key, far_key = wire.group(), wire.take(), wire.take()
        second.append([(wire.take(), wire.take(), rest_key, far_key, sent) for _ in range(4)])
    rel1 = (0, 3, 1, 2)

    mk1 = [(wire.group(), wire.take()) for _ in range(3)]
    mk2 = [(wire.group(), wire.take()) for _ in range(3)]
    for a in range(3):
        n2, n1 = at[a]
        for by in (1, 2, 3):
            wire.go(*mk1[a], meta.at[a, n2, n1], meta.at[a, n2, n1], ORDERS[a][0], by)
    for a in range(3):
        n2, n1 = at[a]
        spread(a, ORDERS[a][0], n2, n1, first[a])
    for a in range(3):
        n2, n1 = at[a]
        spread(a, ORDERS[a][1], n2, n1, second[a][0])
    for a in range(3):
        n2, n1 = at[a]
        wire.got(mk1[a][1], meta.at[a, n2, pl.ds(0, 3)])
        for by in (1, 2, 3):
            wire.go(*mk2[a], meta.at[a, n2], meta.at[a, n2], ORDERS[a][1], by)

    def pass_on(a, dim, keys, minus, plus):
        from_minus, from_plus, _, far, sent = keys
        wire.got(from_minus, minus(0))
        wire.go(sent, far, minus(0), minus(0), dim, 1)
        wire.got(from_plus, plus(1))
        wire.go(sent, far, plus(1), plus(1), dim, 3)

    def views1(a):
        n2, n1 = at[a]
        return (lambda h: half(a, n2, mod4(n1 + 3), h)), (lambda h: half(a, n2, mod4(n1 + 1), h))

    def views2(a, b):
        n2, n1 = at[a]
        s1 = mod4(n1 + rel1[b])
        return (lambda h: half(a, mod4(n2 + 3), s1, h)), (lambda h: half(a, mod4(n2 + 1), s1, h))

    for a in range(3):
        pass_on(a, ORDERS[a][0], first[a], *views1(a))
    for a in range(3):
        n2, n1 = at[a]
        wire.got(first[a][2], held.at[a, n2, mod4(n1 + 1)])
        for b in (1, 2):
            spread(a, ORDERS[a][1], n2, mod4(n1 + rel1[b]), second[a][b])
    for a in range(3):
        pass_on(a, ORDERS[a][1], second[a][0], *views2(a, 0))
    for a in range(3):
        n2, n1 = at[a]
        wire.got(first[a][3], held.at[a, n2, mod4(n1 + 2)])
        spread(a, ORDERS[a][1], n2, mod4(n1 + 2), second[a][3])

    slots = lax.broadcasted_iota(jnp.int32, (32, 256), 0).astype(F32)
    stored = []

    def weigh(a, r):
        index, weight = column_terms(meta, a, mod4(at[a][0] + r), place)
        for e in range(8):
            spin[pl.ds(32 * e, 32), :] = jnp.where(index[e : e + 1, :] == slots, weight[e : e + 1, :], 0.0)
        w = spin[...].T
        high = w.astype(BF)
        for e in range(8):
            hit = jnp.where(index[e : e + 1, :] == slots, 1.0, 0.0)
            picks[a, r, e % 2, pl.ds(32 * (e // 2), 32), :] = hit.astype(BF)
        n = len(stored)
        if n >= 2:
            stored[n - 2].wait()
        grow[n % 2, 0] = high
        grow[n % 2, 1] = (w - high.astype(F32)).astype(BF)
        stored.append(copy(grow.at[n % 2], grown.at[a, r], 6 + n % 2))

    third = [[(wire.group(), wire.take(), wire.take()) for _ in range(8)] for _ in range(3)]
    fourth = [[(wire.group(), wire.take(), wire.take()) for _ in range(2)] for _ in range(3)]
    passed = [wire.group() for _ in range(3)]
    repassed = [wire.group() for _ in range(3)]
    kept = {}
    rels = (0, 1, 3, 2)

    def where(a, s):
        dim = ORDERS[a][2]
        return s // 4, place.at[dim], mod4(at[a][0] + rels[s % 4]), dim

    def settle(a, s):
        c = kept.pop((a, s), None)
        if c is not None:
            c.wait()

    def pack(s):
        for a in range(3):
            j, n3, s2, dim = where(a, s)
            buf = s % 3
            chosen = picks[a, rels[s % 4], j]
            if s >= 3:
                wire.sent(third[a][s - 3][0], packed.at[a, buf, pl.ds(0, 3)])
                settle(a, s - 3)

            @pl.loop(0, 4)
            def _(n):
                cols = pl.ds(pl.multiple_of(n * 512, 512), 512)
                rows = held[a, s2, :, :, cols].reshape(256, 512)
                got = jnp.dot(chosen, rows, preferred_element_type=F32).astype(BF)
                packed[a, buf, :, :, cols] = got.reshape(4, 32, 512)

            sent, early, _ = third[a][s]
            far = mod4(n3 + 2)
            wire.go(sent, early, packed.at[a, buf, far, pl.ds(0, 16)], relay.at[a, s, 0], dim, 1)
            wire.go(sent, early, packed.at[a, buf, far, pl.ds(16, 16)], relay.at[a, s, 1], dim, 3)

    def direct(s):
        for a in range(3):
            j, n3, s2, dim = where(a, s)
            buf = s % 3
            sent, _, late = third[a][s]
            wire.go(sent, late, packed.at[a, buf, mod4(n3 + 1)], outs[a].at[j, n3, s2], dim, 1)
            wire.go(sent, late, packed.at[a, buf, mod4(n3 + 3)], outs[a].at[j, n3, s2], dim, 3)
            kept[a, s] = copy(packed.at[a, buf, n3], outs[a].at[j, n3, s2], 8 + 3 * a + buf)

    def relays(s):
        for a in range(3):
            j, n3, s2, dim = where(a, s)
            _, early, late = third[a][s]
            sent = passed[a]
            wire.got(early, relay.at[a, s])
            wire.go(sent, late, relay.at[a, s, 0], outs[a].at[j, mod4(n3 + 3), s2, pl.ds(0, 16)], dim, 1)
            wire.go(sent, late, relay.at[a, s, 1], outs[a].at[j, mod4(n3 + 1), s2, pl.ds(16, 16)], dim, 3)

    loads = {}

    def fetch(s):
        for a in range(3):
            j, n3, s2, dim = where(a, s)
            wire.got(third[a][s][2], outs[a].at[j, pl.ds(0, 3), s2])
            settle(a, s)
            loads[a, s] = copy(outs[a].at[j, :, s2], chunk.at[a, s % 4], 17 + 4 * a + s % 4)

    def layer(s, stages):
        j, half2 = s // 4, s % 4
        for a in range(3):
            if 0 in stages:
                loads[a, s].wait()
                loads[a, s + 1].wait()
            spots2 = [where(a, s + i)[2] for i in range(2)]

            @pl.loop(min(stages), max(stages) + 1)
            def _(n):
                cols = pl.ds(pl.multiple_of(n * 256, 256), 256)
                rows = chunk[a, half2 : half2 + 2].reshape(256, D)

                def put(ref, value):
                    value = value.reshape(2, 4, 4, 8, 256)
                    for i in range(2):
                        ref[:, spots2[i], :, :, cols] = value[i]

                if a == 2:
                    put(back, jnp.dot(rows, wd[j, :, cols], preferred_element_type=F32))
                else:
                    x, y = (pre, lin) if a == 0 else (dirg, diru)
                    put(x, jnp.dot(rows, wg[j, :, cols], preferred_element_type=F32))
                    put(y, jnp.dot(rows, wu[j, :, cols], preferred_element_type=F32))

    def mix():
        @pl.loop(0, 24)
        def _(i):
            n, q = i % 3, i // 3
            zp, xp, yp = q // 4, (q // 2) % 2, q % 2
            cols = pl.ds(pl.multiple_of(n * 256, 256), 256)
            part = {}
            for dz in range(2):
                for dx in range(2):
                    for dy in range(2):
                        z, x, y = 2 * zp + dz, 2 * xp + dx, 2 * yp + dy
                        p, l = pre[z, x, y, :, cols], lin[z, x, y, :, cols]
                        pd, ld = dirg[y, z, x, :, cols], diru[y, z, x, :, cols]
                        b = back[x, y, z, :, cols]
                        s = jax.nn.sigmoid(p)
                        one = s * (1.0 + p * (1.0 - s))
                        two = s * (1.0 - s) * (2.0 + p * (1.0 - 2.0 * s))
                        part[dz, dx, dy] = (b * (ld * one + l * two * pd), b * one * pd)

            def put(a, hi, lo, inner, pair):
                at_row = pl.multiple_of(128 * hi + 32 * lo + 16 * inner, 16)
                for which in range(2):
                    value = jnp.concatenate([v[which] for v in pair], axis=0).astype(BF)
                    parts[a, which, pl.ds(at_row, 16), cols] = value

            for u in range(2):
                for w in range(2):
                    put(0, 2 * zp + u, 2 * xp + w, yp, (part[u, w, 0], part[u, w, 1]))
                    put(1, 2 * yp + u, 2 * zp + w, xp, (part[w, 0, u], part[w, 1, u]))
                    put(2, 2 * xp + u, 2 * yp + w, zp, (part[0, u, w], part[1, u, w]))

    replied = []

    def reply(j):
        for a in range(3):
            f0, f = SPANS[a]
            out = replies[a]
            if j == 1:
                wire.sent(fourth[a][0][0], out.at[pl.ds(0, 3)])
                replied[a].wait()
            done = 0
            while done < f:
                n = min(256, f - done)
                rows = pl.ds(f0 + done, n)
                got = lax.dot_general(parts[a, 0], wg[j, rows, :], NT, preferred_element_type=F32)
                got += lax.dot_general(parts[a, 1], wu[j, rows, :], NT, preferred_element_type=F32)
                out[:, :, :, done : done + n] = got.astype(BF).reshape(4, 4, 32, n)
                done += n
            n3, dim = place.at[ORDERS[a][2]], ORDERS[a][2]
            sent, early, late = fourth[a][j]
            far = mod4(n3 + 2)
            wire.go(sent, early, out.at[far, pl.ds(0, 2)], passing[a].at[j, 0], dim, 1)
            wire.go(sent, early, out.at[far, pl.ds(2, 2)], passing[a].at[j, 1], dim, 3)
            wire.go(sent, late, out.at[mod4(n3 + 1)], backs[a].at[:, n3, j], dim, 1)
            wire.go(sent, late, out.at[mod4(n3 + 3)], backs[a].at[:, n3, j], dim, 3)
            replied.append(copy(out.at[n3], backs[a].at[:, n3, j], 29 + 3 * j + a))

    def replays(j):
        for a in range(3):
            n3, dim = place.at[ORDERS[a][2]], ORDERS[a][2]
            hold = passing[a]
            _, early, late = fourth[a][j]
            wire.got(early, hold.at[j])
            wire.go(repassed[a], late, hold.at[j, 0], backs[a].at[pl.ds(0, 2), mod4(n3 + 3), j], dim, 1)
            wire.go(repassed[a], late, hold.at[j, 1], backs[a].at[pl.ds(2, 2), mod4(n3 + 1), j], dim, 3)

    for a in range(3):
        wire.got(mk2[a][1], meta.at[a, pl.ds(0, 3)])
    def turn_over(k):
        if k == 0:
            heavy[2].wait()

        @pl.loop(0, 8)
        def _(m):
            cols = pl.ds(pl.multiple_of(m * 256, 256), 256)
            block = chunk[k // 2, 2 * (k % 2) : 2 * (k % 2) + 2, :, :, cols].reshape(256, 256)
            wd[k // 3, cols, 256 * (k % 3) : 256 * (k % 3) + 256] = block.T

    for b in (1, 2):
        for a in range(3):
            pass_on(a, ORDERS[a][1], second[a][b], *views2(a, b))
            weigh(a, 2 * b - 2)
            weigh(a, 2 * b - 1)
            turn_over(3 * b - 3 + a)
        if b == 1:
            pack(0)
    for a in range(3):
        pass_on(a, ORDERS[a][1], second[a][3], *views2(a, 3))
    for a in range(3):
        wire.got(second[a][0][2], held.at[a, 0])
    pack(1)
    direct(0)
    relays(0)
    pack(2)
    direct(1)
    relays(1)
    for a in range(3):
        wire.got(second[a][0][3], held.at[a, 0])
    pack(3)
    direct(2)
    relays(2)
    heavy[0].wait()
    heavy[1].wait()
    fetch(0)
    pack(4)
    direct(3)
    relays(3)
    fetch(1)
    layer(0, (0, 1, 2))
    pack(5)
    direct(4)
    relays(4)
    fetch(2)
    fetch(3)
    layer(2, (0,))
    pack(6)
    direct(5)
    relays(5)
    layer(2, (1, 2))
    pack(7)
    direct(6)
    relays(6)
    fetch(4)
    direct(7)
    relays(7)
    mix()
    fetch(5)
    layer(4, (0, 1, 2))
    fetch(6)
    reply(0)
    fetch(7)
    layer(6, (0, 1, 2))
    replays(0)
    mix()
    reply(1)
    replays(1)
    for a in range(3):
        for j in range(2):
            wire.got(fourth[a][j][2], backs[a].at[pl.ds(0, 3), :, j])
        wire.sent(first[a][4], held.at[a, 0, pl.ds(0, 3)])
        wire.sent(second[a][0][4], held.at[a, pl.ds(0, 3)])
        wire.sent(mk1[a][0], meta.at[a, 0, pl.ds(0, 3)])
        wire.sent(mk2[a][0], meta.at[a, pl.ds(0, 3)])
        for s in (5, 6, 7):
            wire.sent(third[a][s][0], packed.at[a, 0, pl.ds(0, 3)])
        wire.sent(passed[a], relay.at[a])
        wire.sent(fourth[a][1][0], replies[a].at[pl.ds(0, 3)])
        wire.sent(repassed[a], passing[a])
    for c in replied[3:] + stored[-2:]:
        c.wait()


N_GROUPS, N_TAKEN, N_LOCAL = 6 + 6 + 30 + 6, 42 + 6 + 48 + 12, 35
SPANS = ((0, 768), (768, 640), (1408, 640))


def dispatch(tok, tan, adj, ids, gates, wg, wu, wd):
    vmem = pl.BlockSpec(memory_space=pltpu.VMEM)
    hbm = pl.BlockSpec(memory_space=pl.ANY)
    rows = jax.ShapeDtypeStruct((2, 4, 4, 32, D), BF)
    out = pl.pallas_call(
        dispatch_kernel,
        out_shape=(rows, rows, rows)
        + tuple(jax.ShapeDtypeStruct((4, 4, 2, 32, f), BF) for _, f in SPANS)
        + (jax.ShapeDtypeStruct((3, 4, 2, 256, 256), BF),),
        in_specs=[hbm] * 3 + [vmem] * 2 + [hbm] * 3,
        out_specs=(hbm,) * 7,
        scratch_shapes=[
            pltpu.VMEM((3, 4, 4, TOK, D), BF),
            pltpu.VMEM((3, 3, 4, 32, D), BF),
            pltpu.VMEM((3, 8, 2, 16, D), BF),
            pltpu.VMEM((3, 4, 4, 8, 128), F32),
            pltpu.VMEM((3, 4, 4, 32, D), BF),
            pltpu.VMEM((2, D, FF), BF),
            pltpu.VMEM((2, D, FF), BF),
            pltpu.VMEM((2, D, FF), BF),
        ]
        + [pltpu.VMEM((4, 4, 4, 8, FF), F32)] * 5
        + [pltpu.VMEM((3, 2, 512, FF), BF)]
        + [pltpu.VMEM((4, 4, 32, f), BF) for _, f in SPANS]
        + [pltpu.VMEM((2, 2, 2, 32, f), BF) for _, f in SPANS]
        + [
            pltpu.VMEM((3, 4, 2, 128, 256), BF),
            pltpu.VMEM((256, 256), F32),
            pltpu.VMEM((2, 2, 256, 256), BF),
            pltpu.SemaphoreType.DMA((N_GROUPS,)),
            pltpu.SemaphoreType.DMA((N_TAKEN,)),
            pltpu.SemaphoreType.DMA((N_LOCAL,)),
        ],
        compiler_params=pltpu.CompilerParams(
            collective_id=1, has_side_effects=True, vmem_limit_bytes=67043328
        ),
        name="dispatch",
    )(tok, tan, adj, ids, gates, wg, wu, wd)
    return out[3:]


def collect_kernel(b0, b1, b2, grown_in, tan, hvp, ratio, *scratch):
    place = Place()
    n_part = 8
    parts = [scratch[i * n_part : (i + 1) * n_part] for i in range(9)]
    grown, plane, line, send, recv, local = scratch[9 * n_part :]
    wire = Wire(place, send, recv)
    spots = iter(range(12))
    backs = (b0, b1, b2)

    def copy(src, dst):
        c = pltpu.make_async_copy(src, dst, local.at[next(spots)])
        c.start()
        return c

    loads = {}
    for q in range(3):
        for a, f0, n in PARTS[q]:
            loads[q, a] = copy(backs[a].at[:, :, :, pl.ds(f0 - SPANS[a][0], n)], parts[3 * q + a][0])
            if q == 0:
                loads[a] = copy(grown_in.at[a], grown.at[a])
    y, x, z = place.at
    near = [(place.dp, lax.rem(y + i // 4, 4) * 16 + lax.rem(x + i % 4, 4) * 4 + z) for i in range(1, 16)]
    tall = [(lax.rem(place.dp + i // 4, 2), place.shifted(2, i % 4)) for i in range(1, 8)]
    sem = pltpu.get_barrier_semaphore()
    for other in near + tall:
        pl.semaphore_signal(sem, inc=1, device_id=other, device_id_type=MESH)
    pl.semaphore_wait(sem, 22)
    keys = [[[wire.group(), wire.group()] + [wire.take() for _ in range(4)] for _ in range(3)] for _ in range(3)]
    at = [tuple(place.at[d] for d in ORDERS[a]) for a in range(3)]
    state = {"square": jnp.zeros((8, 128), F32)}

    def total(q, a, r):
        n = PARTS[q][a][2]
        rows = parts[3 * q + a][0][mod4(at[a][1] + r)].reshape(256, n)
        got = jnp.dot(grown[a, r, 0], rows, preferred_element_type=F32)
        got = got + jnp.dot(grown[a, r, 1], rows, preferred_element_type=F32)
        return got.reshape(4, 64, n)

    def far2(q):
        for a, _, n in PARTS[q]:
            own, out2, mid2 = parts[3 * q + a][1:4]
            dim = ORDERS[a][1]
            k = keys[q][a]
            loads[q, a].wait()
            if q == 0:
                loads[a].wait()
            out2[...] = total(q, a, 2).astype(BF)
            wire.go(k[0], k[2], out2.at[pl.ds(0, 2)], mid2.at[0], dim, 1)
            wire.go(k[0], k[3], out2.at[pl.ds(2, 2)], mid2.at[1], dim, 3)
        for a, _, n in PARTS[q]:
            parts[3 * q + a][1][...] = total(q, a, 0)

    def near2(q):
        for a, _, n in PARTS[q]:
            mid2, to2, in2 = parts[3 * q + a][3:6]
            k, dim = keys[q][a], ORDERS[a][1]
            for side, r in ((0, 1), (1, 3)):
                got = total(q, a, r)
                wire.got(k[2 + side], mid2.at[side])
                came = mid2[side].astype(F32)
                lo, hi = got[0:2], got[2:4]
                if side == 0:
                    lo = lo + came
                else:
                    hi = hi + came
                to2[side, 0:2] = lo.astype(BF)
                to2[side, 2:4] = hi.astype(BF)
                wire.go(k[0], k[4], to2.at[side], in2.at[side], dim, r)

    def last(q):
        for a, _, n in PARTS[q]:
            own, in2, out1, mid1 = (parts[3 * q + a][i] for i in (1, 5, 6, 7))
            n1, dim = at[a][0], ORDERS[a][0]
            k = keys[q][a]
            wire.got(k[4], in2)
            own[...] = own[...] + (in2[0].astype(F32) + in2[1].astype(F32))
            for by in (2, 1, 3):
                out1[by - 1] = own[mod4(n1 + by)].astype(BF)
                wire.go(k[1], k[5], out1.at[by - 1], mid1.at[by - 1], dim, by)

    def finish(q):
        for a, f0, n in PARTS[q]:
            own, mid1 = parts[3 * q + a][1], parts[3 * q + a][7]
            k = keys[q][a]
            wire.got(k[5], mid1)
            got = own[at[a][0]] + (mid1[0].astype(F32) + mid1[1].astype(F32) + mid1[2].astype(F32))
            hvp[:, f0 : f0 + n] = got
            state["square"] += jnp.sum((got * got).reshape(8, 8, n // 128, 128), axis=(0, 2))

    far2(0)
    far2(1)
    near2(0)
    far2(2)
    last(0)
    near2(1)
    t = tan[...].astype(F32)
    low = jnp.sum((t * t).reshape(8, 8, 16, 128), axis=(0, 2))
    near2(2)
    finish(0)
    last(1)
    finish(1)
    last(2)
    finish(2)

    def share(table, value, spot, others):
        table[spot, 0] = value[0]
        table[spot, 1] = value[1]
        sent, came = wire.group(), wire.take()
        for other in others:
            wire.push(sent, came, table.at[spot], table.at[spot], other)
        wire.got(came, table.at[pl.ds(0, len(others))])
        wire.sent(sent, table.at[pl.ds(0, len(others))])
        return jnp.sum(table[...], axis=0)

    full = share(plane, (state["square"], low), y * 4 + x, near)
    full = share(line, (full[0], full[1]), place.dp * 4 + z, tall)
    top, low = jnp.sum(full[0]), jnp.sum(full[1])
    ratio[...] = jnp.full((1, 1), top, F32) / jnp.full((1, 1), low, F32)
    for q in range(3):
        for a in range(3):
            back, _, _, _, _, _, out1, _ = parts[3 * q + a]
            wire.sent(keys[q][a][0], back.at[pl.ds(0, 3)])
            wire.sent(keys[q][a][1], out1)


N_SENT, N_CAME = 18 + 2, 36 + 2


def collect(backs, grown, tan):
    vmem = pl.BlockSpec(memory_space=pltpu.VMEM)
    hbm = pl.BlockSpec(memory_space=pl.ANY)
    scratch = []
    for q in range(3):
        for _, _, f in PARTS[q]:
            scratch += [
                pltpu.VMEM((4, 4, 64, f), BF),
                pltpu.VMEM((4, 64, f), F32),
                pltpu.VMEM((4, 64, f), BF),
                pltpu.VMEM((2, 2, 64, f), BF),
                pltpu.VMEM((2, 4, 64, f), BF),
                pltpu.VMEM((2, 4, 64, f), BF),
                pltpu.VMEM((3, 64, f), BF),
                pltpu.VMEM((3, 64, f), BF),
            ]
    scratch += [
        pltpu.VMEM((3, 4, 2, 256, 256), BF),
        pltpu.VMEM((16, 2, 8, 128), F32),
        pltpu.VMEM((8, 2, 8, 128), F32),
        pltpu.SemaphoreType.DMA((N_SENT,)),
        pltpu.SemaphoreType.DMA((N_CAME,)),
        pltpu.SemaphoreType.DMA((12,)),
    ]
    return pl.pallas_call(
        collect_kernel,
        out_shape=(jax.ShapeDtypeStruct((TOK, D), F32), jax.ShapeDtypeStruct((1, 1), F32)),
        in_specs=[hbm] * 4 + [vmem],
        out_specs=(vmem, vmem),
        scratch_shapes=scratch,
        compiler_params=pltpu.CompilerParams(
            collective_id=2, has_side_effects=True, vmem_limit_bytes=67043328
        ),
        name="collect",
    )(*backs, grown, tan)


def local(tokens, tangent, adjoint, gates, expert_ids, w_gate, w_up, w_down):
    w_down = w_down.reshape(3, 4, 4, 32, D)
    *backs, grown = dispatch(tokens, tangent, adjoint, expert_ids.T, gates.T, w_gate, w_up, w_down)
    backs = [b.reshape(4, 4, 64, b.shape[-1]) for b in backs]
    hvp, ratio = collect(backs, grown, tangent)
    return hvp, ratio[0, 0]


def solution(mesh):
    rows = P(("dp", "expert"), None)
    weights = P("expert", None, None)
    return jax.shard_map(
        local,
        mesh=mesh,
        in_specs=(rows,) * 5 + (weights,) * 3,
        out_specs=(rows, P()),
        check_vma=False,
    )
```
